32 devices in a mesh: dp: 16 (over z, y, core), shard: 2 (over x).
Axes of the slice: x: 2, y: 2, z: 4, core: 2. Of those that a mesh axis runs over, the one named last changes fastest.
Arguments:
- tokens: float32 [16384, 1024], P(('dp', 'shard')), may hold values from -6 to 6
- out_grad: float32 [16384, 1024], P(('dp', 'shard')), may hold values from -30 to 30
- segment_ids: int32 [16, 1024], P('dp'), may hold values from 0 to 3, never falling along the last dimension, each value on 1 to 512 neighbouring positions
- qkv_weight: float32 [1024, 3072], P('dp', 'shard'), may hold values from -0.1875 to 0.1875
- proj_weight: float32 [1024, 1024], P('dp', 'shard'), may hold values from -1.5 to 1.5
- up_weight: float32 [1024, 4096], P('dp', 'shard'), may hold values from -0.1875 to 0.1875
- down_weight: float32 [4096, 1024], P('dp', 'shard'), may hold values from -0.09375 to 0.09375
- vectors: float32 [12, 1024], P(None, ('dp', 'shard')), may hold values from -4 to 4
- qkv_moments: float32 [2, 1024, 3072], P(None, 'dp', 'shard'), may hold values from -0.05 to 0.05
- proj_moments: float32 [2, 1024, 1024], P(None, 'dp', 'shard'), may hold values from -0.05 to 0.05
- up_moments: float32 [2, 1024, 4096], P(None, 'dp', 'shard'), may hold values from -0.05 to 0.05
- down_moments: float32 [2, 4096, 1024], P(None, 'dp', 'shard'), may hold values from -0.05 to 0.05
- vector_moments: float32 [2, 12, 1024], P(None, None, ('dp', 'shard')), may hold values from -1 to 1
Outputs:
- block_out: float32 [16384, 1024], P(('dp', 'shard'))
- tokens_grad: float32 [16384, 1024], P(('dp', 'shard'))
- qkv_grad: float32 [1024, 3072], P('dp', 'shard')
- proj_grad: float32 [1024, 1024], P('dp', 'shard')
- up_grad: float32 [1024, 4096], P('dp', 'shard')
- down_grad: float32 [4096, 1024], P('dp', 'shard')
- vectors_grad: float32 [12, 1024], P(None, ('dp', 'shard'))
- qkv_new: float32 [1024, 3072], P('dp', 'shard')
- proj_new: float32 [1024, 1024], P('dp', 'shard')
- up_new: float32 [1024, 4096], P('dp', 'shard')
- down_new: float32 [4096, 1024], P('dp', 'shard')
- vectors_new: float32 [12, 1024], P(None, ('dp', 'shard'))
- qkv_moments_new: float32 [2, 1024, 3072], P(None, 'dp', 'shard')
- proj_moments_new: float32 [2, 1024, 1024], P(None, 'dp', 'shard')
- up_moments_new: float32 [2, 1024, 4096], P(None, 'dp', 'shard')
- down_moments_new: float32 [2, 4096, 1024], P(None, 'dp', 'shard')
- vector_moments_new: float32 [2, 12, 1024], P(None, None, ('dp', 'shard'))
The draws below stay inside these ranges and needn't reach their ends.
All inputs are finite; a program needn't handle non-finite values.
Results may differ from the reference program's by a relative error of at most 0.011.
Values may be sent and summed in bfloat16 or wider, within the bound.
A program may use at most 320 MiB of HBM per device.

```python
import math
import jax
import jax.numpy as jnp
import numpy as np
from jax import lax

D = 1024
FF = 4096
HD = 64
ROT = 16
SEQ_LEN = 1024
DOCS = 4
STEP = 4
VROWS = 12
NPARAM = 12595200
SEQS = 16
TOKENS = 16384


def moment_pair(key, shape):
    first_key = jax.random.fold_in(key, 11)
    second_key = jax.random.fold_in(key, 12)
    first_moment = 0.01 * jax.random.truncated_normal(first_key, -4.0, 4.0, shape, jnp.float32)
    exponent_draw = jax.random.uniform(second_key, shape, jnp.float32, math.log(1e-05), math.log(0.001))
    return jnp.stack([first_moment, jnp.exp(exponent_draw)])


def draw_qkv_moments(key, part):
    return moment_pair(key, (D, 3 * D))


def draw_proj_moments(key, part):
    return moment_pair(key, (D, D))


def draw_up_moments(key, part):
    return moment_pair(key, (D, FF))


def draw_down_moments(key, part):
    return moment_pair(key, (FF, D))


def draw_vector_moments(key, part):
    sign_key = jax.random.fold_in(key, 41)
    size_key = jax.random.fold_in(key, 42)
    second_key = jax.random.fold_in(key, 43)
    shape = (VROWS, D)
    size_log = jax.random.uniform(size_key, shape, jnp.float32, math.log(0.01), math.log(1.0))
    second_log = jax.random.uniform(second_key, shape, jnp.float32, math.log(0.001), math.log(0.5))
    signs = jnp.where(jax.random.uniform(sign_key, shape, jnp.float32) < 0.5, -1.0, 1.0)
    return jnp.stack([signs * jnp.exp(size_log), jnp.exp(second_log)])


def draw_vectors(key, part):
    gain_key = jax.random.fold_in(key, 21)
    bias_key = jax.random.fold_in(key, 22)
    trend_key = jax.random.fold_in(key, 23)
    gains = jax.random.uniform(gain_key, (2, D), jnp.float32, 0.6, 1.4)
    noise_rows = 0.3 * jax.random.truncated_normal(bias_key, -4.0, 4.0, (6, D), jnp.float32)
    trend_noise = 0.5 * jax.random.truncated_normal(trend_key, -3.0, 3.0, (FF,), jnp.float32)
    ramp = -1.0 + 3.0 * jnp.arange(FF, dtype=jnp.float32) / FF
    up_rows = (ramp + trend_noise).reshape(FF // D, D)
    return jnp.concatenate([gains[0:1], noise_rows[0:1], gains[1:2], noise_rows[1:2], noise_rows[2:6], up_rows], axis=0)


def draw_out_grad(key, part):
    base_key = jax.random.fold_in(key, 31)
    row_key = jax.random.fold_in(key, 32)
    column_key = jax.random.fold_in(key, 33)
    column_pos = jnp.arange(D, dtype=jnp.float32) / D
    column_scale = jnp.exp(math.log(10.0) * (column_pos - 0.5)) * jnp.exp(jax.random.uniform(column_key, (D,), jnp.float32, -0.35, 0.35))
    row_scale = jnp.exp(jax.random.uniform(row_key, (TOKENS, 1), jnp.float32, math.log(0.5), math.log(2.0)))
    base_values = jax.random.truncated_normal(base_key, -3.0, 3.0, (TOKENS, D), jnp.float32)
    return base_values * row_scale * column_scale[None, :]


def block_scale(key, extent, cuts, low, top_value):
    factor_of = 1.0
    for dim, shards_of in cuts:
        steps = jax.random.uniform(jax.random.fold_in(jax.random.fold_in(key, 6), dim), (shards_of,), jnp.float32, low / len(cuts), top_value / len(cuts))
        factor_of = factor_of * jnp.repeat(jnp.exp(steps), extent[dim] // shards_of).reshape((-1,) + (1,) * (len(extent) - 1 - dim))
    return factor_of


def split_up(amount, total, limit, lean):
    portions = [(1 << 20) // math.isqrt(standing ** lean) + 1 for standing in range(2, amount + 1)]
    surplus, holding = total - limit - (amount - 1), [1] * (amount - 1)
    while surplus > 0:
        candidates = [i for i in range(amount - 1) if holding[i] < limit]
        whole, budget = sum([portions[i] for i in candidates]), surplus
        for i in candidates:
            more = min(limit - holding[i], max(1, budget * portions[i] // whole), surplus)
            holding[i] = holding[i] + more
            surplus = surplus - more
    return np.array([limit] + holding)


def uneven_parts(key, amount, total, limit, lean):
    if amount == 2:
        one = jax.random.randint(key, (), max(1, total - limit), min(limit, total - 1) + 1)
        return jnp.stack([one, total - one])
    tallies = jnp.asarray(split_up(amount, total, limit, lean), jnp.int32)
    twos = (amount - 1) // 2
    donor, sink = tallies[1:1 + 2 * twos:2], tallies[2:2 + 2 * twos:2]
    margin = jnp.minimum(donor - 1, limit - sink)
    moved = jax.random.randint(jax.random.fold_in(key, 1), (twos,), 0, 1 << 20) % (margin + 1)
    tallies = tallies.at[1:1 + 2 * twos:2].set(donor - moved).at[2:2 + 2 * twos:2].set(sink + moved)
    return tallies[jax.random.permutation(jax.random.fold_in(key, 2), amount)]


def normal_values(own_key, dims, width, limit, pieces=(), kind=jnp.bfloat16):
    entries = width * jax.random.normal(own_key, dims, jnp.float32)
    if pieces:
        entries = entries * block_scale(own_key, dims, pieces, -0.22, 0.18)
    return jnp.clip(entries, -limit, limit).astype(kind)


def setup_inputs(seed: int = 0) -> dict:
    key_of = jax.random.split(jax.random.key(seed), 14)
    return {
        "tokens": normal_values(key_of[0], (TOKENS, D), 1.0, 6.0, ((0, 32),), jnp.float32),
        "out_grad": draw_out_grad(jax.random.fold_in(key_of[13], 71), 0),
        "segment_ids": jax.vmap(lambda own: jnp.searchsorted(jnp.cumsum(uneven_parts(own, DOCS, SEQ_LEN, SEQ_LEN // 2, 0)), jnp.arange(SEQ_LEN), side="right"))(jax.random.split(key_of[2], SEQS)).reshape((SEQS, SEQ_LEN)).astype(jnp.int32),
        "qkv_weight": normal_values(key_of[3], (D, 3 * D), D ** -0.5, 0.1875, ((0, 16), (1, 2)), jnp.float32),
        "proj_weight": normal_values(key_of[4], (D, D), (D // 64) ** -0.5, 1.5, ((0, 16), (1, 2)), jnp.float32),
        "up_weight": normal_values(key_of[5], (D, FF), D ** -0.5, 0.1875, ((0, 16), (1, 2)), jnp.float32),
        "down_weight": normal_values(key_of[6], (FF, D), FF ** -0.5, 0.09375, ((0, 16), (1, 2)), jnp.float32),
        "vectors": draw_vectors(jax.random.fold_in(key_of[13], 71), 0),
        "qkv_moments": draw_qkv_moments(jax.random.fold_in(key_of[13], 71), 0),
        "proj_moments": draw_proj_moments(jax.random.fold_in(key_of[13], 71), 0),
        "up_moments": draw_up_moments(jax.random.fold_in(key_of[13], 71), 0),
        "down_moments": draw_down_moments(jax.random.fold_in(key_of[13], 71), 0),
        "vector_moments": draw_vector_moments(jax.random.fold_in(key_of[13], 71), 0),
    }


ln_eps = 1e-05
beta_one = 0.9
beta_two = 0.95
learn_rate = 0.005
decay_rate = 0.01
adam_eps = 1e-08
rope_base = 10000.0

def rounded(values):
    return lax.optimization_barrier(values.astype(jnp.bfloat16))

def as_float(values):
    return values.astype(jnp.float32)

def norm_rows(inputs, gain_row, bias_row):
    center = inputs - lax.optimization_barrier(jnp.mean(inputs, axis=-1, keepdims=True))
    inverse = lax.rsqrt(lax.optimization_barrier(jnp.mean(center * center, axis=-1, keepdims=True)) + ln_eps)
    unit_rows = center * inverse
    return (unit_rows * gain_row + bias_row, unit_rows, inverse)

def norm_back(upstream, unit_rows, inverse, gain_row):
    gain_grad = lax.optimization_barrier(jnp.sum(upstream * unit_rows, axis=0))
    bias_grad = lax.optimization_barrier(jnp.sum(upstream, axis=0))
    scaled_up = upstream * gain_row
    mean_plain = lax.optimization_barrier(jnp.mean(scaled_up, axis=-1, keepdims=True))
    mean_unit = lax.optimization_barrier(jnp.mean(scaled_up * unit_rows, axis=-1, keepdims=True))
    return (inverse * (scaled_up - mean_plain - unit_rows * mean_unit), gain_grad, bias_grad)

def doc_positions(segment_row):
    length_all = segment_row.shape[0]
    indices = jnp.arange(length_all, dtype=jnp.int32)
    starting = jnp.concatenate([jnp.ones((1,), dtype=jnp.bool_), segment_row[1:] != segment_row[:-1]])
    begins = lax.cummax(jnp.where(starting, indices, 0), axis=0)
    return indices - begins

def rotary_tables(positions, rot_dims):
    half_dims = rot_dims // 2
    exponent = jnp.arange(half_dims, dtype=jnp.float32) * (2.0 / rot_dims)
    inverse_freq = jnp.exp(-math.log(rope_base) * exponent)
    angles = positions.astype(jnp.float32)[:, None] * inverse_freq[None, :]
    return (jnp.cos(angles)[:, None, :], jnp.sin(angles)[:, None, :])

def rotate(head_rows, cosine_table, sine_table):
    half_dims = cosine_table.shape[-1]
    lower_half = head_rows[..., :half_dims]
    upper_half = head_rows[..., half_dims:2 * half_dims]
    return jnp.concatenate([lower_half * cosine_table - upper_half * sine_table, upper_half * cosine_table + lower_half * sine_table, head_rows[..., 2 * half_dims:]], axis=-1)

def gelu_pair(pre_act):
    normal_cdf = 0.5 * (1.0 + lax.erf(pre_act * (1.0 / math.sqrt(2.0))))
    density = jnp.exp(-0.5 * pre_act * pre_act) * (1.0 / math.sqrt(2.0 * math.pi))
    return (pre_act * normal_cdf, normal_cdf + pre_act * density)

def adam_update(weight, moments, gradient, clip_factor):
    clipped = gradient * clip_factor
    first_new = beta_one * moments[0] + (1.0 - beta_one) * clipped
    second_new = beta_two * moments[1] + (1.0 - beta_two) * clipped * clipped
    fix_first = 1.0 - math.pow(beta_one, STEP)
    fix_second = 1.0 - math.pow(beta_two, STEP)
    direction = first_new / fix_first / (jnp.sqrt(second_new / fix_second) + adam_eps)
    return (weight - learn_rate * (direction + decay_rate * weight), jnp.stack([first_new, second_new]))

def sequence_pass(seq_rows, seq_cot, segment_row, qkv_work, proj_work, up_work, down_work, vec_work):
    head_count = D // HD
    score_scale = 1.0 / math.sqrt(HD)
    length_all = seq_rows.shape[0]
    normed_one, unit_one, inverse_one = norm_rows(seq_rows, vec_work[0], vec_work[1])
    hidden_one = rounded(normed_one)
    mixed_rows = jnp.dot(hidden_one, qkv_work, preferred_element_type=jnp.float32)
    query_raw = (mixed_rows[:, :D] + vec_work[4]).reshape(length_all, head_count, HD)
    key_raw = mixed_rows[:, D:2 * D].reshape(length_all, head_count, HD)
    value_bf = rounded(mixed_rows[:, 2 * D:] + vec_work[5]).reshape(length_all, head_count, HD)
    cosine_table, sine_table = rotary_tables(doc_positions(segment_row), ROT)
    query_bf = rounded(rotate(query_raw, cosine_table, sine_table))
    key_bf = rounded(rotate(key_raw, cosine_table, sine_table))
    indices = jnp.arange(length_all, dtype=jnp.int32)
    allowed = (segment_row[:, None] == segment_row[None, :]) & (indices[None, :] <= indices[:, None])
    scores = jnp.einsum('qhd,khd->hqk', as_float(query_bf), as_float(key_bf)) * score_scale
    exp_scores = jnp.where(allowed[None], jnp.exp(scores), 0.0)
    totals = lax.optimization_barrier(jnp.sum(exp_scores, axis=-1))
    numerator = jnp.einsum('hqk,khd->qhd', as_float(rounded(exp_scores)), as_float(value_bf))
    attended = numerator / jnp.transpose(totals)[:, :, None]
    log_totals = jnp.log(totals)
    attended_bf = rounded(attended.reshape(length_all, D))
    proj_out = jnp.dot(attended_bf, proj_work, preferred_element_type=jnp.float32) + vec_work[6]
    normed_two, unit_two, inverse_two = norm_rows(seq_rows, vec_work[2], vec_work[3])
    hidden_two = rounded(normed_two)
    pre_act = jnp.dot(hidden_two, up_work, preferred_element_type=jnp.float32) + vec_work[8:].reshape(FF)
    act_values, act_slope = gelu_pair(pre_act)
    act_bf = rounded(act_values)
    mlp_out = jnp.dot(act_bf, down_work, preferred_element_type=jnp.float32) + vec_work[7]
    out_rows = seq_rows + proj_out + mlp_out
    cot_bf = rounded(seq_cot)
    down_part = jnp.dot(act_bf.T, cot_bf, preferred_element_type=jnp.float32)
    proj_part = jnp.dot(attended_bf.T, cot_bf, preferred_element_type=jnp.float32)
    cot_sum = lax.optimization_barrier(jnp.sum(seq_cot, axis=0))
    grad_pre = jnp.dot(cot_bf, down_work.T, preferred_element_type=jnp.float32) * act_slope
    grad_pre_bf = rounded(grad_pre)
    up_part = jnp.dot(hidden_two.T, grad_pre_bf, preferred_element_type=jnp.float32)
    rows_two, ln2_gain_part, ln2_bias_part = norm_back(jnp.dot(grad_pre_bf, up_work.T, preferred_element_type=jnp.float32), unit_two, inverse_two, vec_work[2])
    grad_att_bf = rounded(jnp.dot(cot_bf, proj_work.T, preferred_element_type=jnp.float32)).reshape(length_all, head_count, HD)
    probability = jnp.where(allowed[None], jnp.exp(scores - log_totals[:, :, None]), 0.0)
    grad_prob = jnp.einsum('qhd,khd->hqk', as_float(grad_att_bf), as_float(value_bf))
    row_delta = jnp.transpose(lax.optimization_barrier(jnp.sum(as_float(grad_att_bf) * attended, axis=-1)))
    grad_score = rounded(probability * (grad_prob - row_delta[:, :, None]) * score_scale)
    grad_query = jnp.einsum('hqk,khd->qhd', as_float(grad_score), as_float(key_bf))
    grad_key = jnp.einsum('hqk,qhd->khd', as_float(grad_score), as_float(query_bf))
    grad_value = jnp.einsum('hqk,qhd->khd', as_float(rounded(probability)), as_float(grad_att_bf))
    grad_query = rotate(grad_query, cosine_table, -sine_table).reshape(length_all, D)
    grad_key = rotate(grad_key, cosine_table, -sine_table).reshape(length_all, D)
    grad_value = grad_value.reshape(length_all, D)
    grad_mixed_bf = rounded(jnp.concatenate([grad_query, grad_key, grad_value], axis=1))
    qkv_part = jnp.dot(hidden_one.T, grad_mixed_bf, preferred_element_type=jnp.float32)
    rows_one, ln1_gain_part, ln1_bias_part = norm_back(jnp.dot(grad_mixed_bf, qkv_work.T, preferred_element_type=jnp.float32), unit_one, inverse_one, vec_work[0])
    in_grad = seq_cot + rows_one + rows_two
    vec_part = jnp.concatenate([jnp.stack([ln1_gain_part, ln1_bias_part, ln2_gain_part, ln2_bias_part, lax.optimization_barrier(jnp.sum(grad_query, axis=0)), lax.optimization_barrier(jnp.sum(grad_value, axis=0)), cot_sum, cot_sum]), lax.optimization_barrier(jnp.sum(grad_pre, axis=0)).reshape(FF // D, D)], axis=0)
    return (out_rows, in_grad, (qkv_part, proj_part, up_part, down_part, vec_part))

def reference(tokens, out_grad, segment_ids, qkv_weight, proj_weight, up_weight, down_weight, vectors, qkv_moments, proj_moments, up_moments, down_moments, vector_moments):
    qkv_work = qkv_weight.astype(jnp.bfloat16)
    proj_work = proj_weight.astype(jnp.bfloat16)
    up_work = up_weight.astype(jnp.bfloat16)
    down_work = down_weight.astype(jnp.bfloat16)
    vec_work = as_float(rounded(vectors))
    seq_tokens = tokens.reshape(SEQS, SEQ_LEN, D)
    seq_cots = out_grad.reshape(SEQS, SEQ_LEN, D)
    zero_grads = (jnp.zeros((D, 3 * D), jnp.float32), jnp.zeros((D, D), jnp.float32), jnp.zeros((D, FF), jnp.float32), jnp.zeros((FF, D), jnp.float32), jnp.zeros((VROWS, D), jnp.float32))

    def one_sequence(running, inputs):
        seq_rows, seq_cot, segment_row = inputs
        out_rows, in_grad, grads = sequence_pass(seq_rows, seq_cot, segment_row, qkv_work, proj_work, up_work, down_work, vec_work)
        return (jax.tree.map(lambda summed, latest: summed + latest, running, grads), (out_rows, in_grad))
    totals_grad, (out_seq, grad_seq) = lax.scan(one_sequence, zero_grads, (seq_tokens, seq_cots, segment_ids))
    qkv_grad, proj_grad, up_grad, down_grad, vectors_grad = totals_grad
    square_total = jnp.sum(qkv_grad * qkv_grad) + jnp.sum(proj_grad * proj_grad) + jnp.sum(up_grad * up_grad) + jnp.sum(down_grad * down_grad) + jnp.sum(vectors_grad * vectors_grad)
    norm_limit = math.sqrt(NPARAM)
    clip_factor = norm_limit / jnp.maximum(jnp.sqrt(square_total), norm_limit)
    qkv_new, qkv_moments_new = adam_update(qkv_weight, qkv_moments, qkv_grad, clip_factor)
    proj_new, proj_moments_new = adam_update(proj_weight, proj_moments, proj_grad, clip_factor)
    up_new, up_moments_new = adam_update(up_weight, up_moments, up_grad, clip_factor)
    down_new, down_moments_new = adam_update(down_weight, down_moments, down_grad, clip_factor)
    vectors_new, vector_moments_new = adam_update(vectors, vector_moments, vectors_grad, clip_factor)
    return (out_seq.reshape(TOKENS, D), grad_seq.reshape(TOKENS, D), qkv_grad, proj_grad, up_grad, down_grad, vectors_grad, qkv_new, proj_new, up_new, down_new, vectors_new, qkv_moments_new, proj_moments_new, up_moments_new, down_moments_new, vector_moments_new)
```

```python
import math

import jax
import jax.numpy as jnp
from jax import lax
from jax.experimental import pallas as pl
from jax.experimental.pallas import tpu as pltpu
from jax.sharding import PartitionSpec as P

D = 1024
FF = 4096
HD = 64
ROT = 16
STEP = 4
VROWS = 12
NPARAM = 12595200


ln_eps = 1e-05
beta_one = 0.9
beta_two = 0.95
learn_rate = 0.005
decay_rate = 0.01
adam_eps = 1e-08
rope_base = 10000.0


def norm_rows(inputs, gain_row, bias_row):
    center = inputs - jnp.mean(inputs, axis=-1, keepdims=True)
    inverse = lax.rsqrt(jnp.mean(center * center, axis=-1, keepdims=True) + ln_eps)
    unit_rows = center * inverse
    return (unit_rows * gain_row + bias_row, unit_rows, inverse)


def norm_back(upstream, unit_rows, inverse, gain_row):
    gain_grad = jnp.sum(upstream * unit_rows, axis=0)
    bias_grad = jnp.sum(upstream, axis=0)
    scaled_up = upstream * gain_row
    mean_plain = jnp.mean(scaled_up, axis=-1, keepdims=True)
    mean_unit = jnp.mean(scaled_up * unit_rows, axis=-1, keepdims=True)
    return (inverse * (scaled_up - mean_plain - unit_rows * mean_unit), gain_grad, bias_grad)


def doc_positions(segment_row):
    length_all = segment_row.shape[0]
    indices = jnp.arange(length_all, dtype=jnp.int32)
    starting = jnp.concatenate(
        [jnp.ones((1,), dtype=jnp.bool_), segment_row[1:] != segment_row[:-1]]
    )
    begins = lax.cummax(jnp.where(starting, indices, 0), axis=0)
    return indices - begins


def rotary_tables(positions, rot_dims):
    half_dims = rot_dims // 2
    exponent = jnp.arange(half_dims, dtype=jnp.float32) * (2.0 / rot_dims)
    inverse_freq = jnp.exp(-math.log(rope_base) * exponent)
    angles = positions.astype(jnp.float32)[:, None] * inverse_freq[None, :]
    return (jnp.cos(angles)[:, None, :], jnp.sin(angles)[:, None, :])


def rotate(head_rows, cosine_table, sine_table):
    half_dims = cosine_table.shape[-1]
    lower_half = head_rows[..., :half_dims]
    upper_half = head_rows[..., half_dims : 2 * half_dims]
    return jnp.concatenate(
        [
            lower_half * cosine_table - upper_half * sine_table,
            upper_half * cosine_table + lower_half * sine_table,
            head_rows[..., 2 * half_dims :],
        ],
        axis=-1,
    )


def gelu_pair(pre_act):
    normal_cdf = 0.5 * (1.0 + lax.erf(pre_act * (1.0 / math.sqrt(2.0))))
    density = jnp.exp(-0.5 * pre_act * pre_act) * (1.0 / math.sqrt(2.0 * math.pi))
    return (pre_act * normal_cdf, normal_cdf + pre_act * density)


def times_transposed(left, right):
    return lax.dot_general(
        left, right, (((1,), (1,)), ((), ())), preferred_element_type=jnp.float32
    )


def transposed_times(left, right):
    return lax.dot_general(
        left, right, (((0,), (0,)), ((), ())), preferred_element_type=jnp.float32
    )


def adam_update(weight, moments, gradient, clip_factor):
    clipped = gradient * clip_factor
    first_new = beta_one * moments[0] + (1.0 - beta_one) * clipped
    second_new = beta_two * moments[1] + (1.0 - beta_two) * clipped * clipped
    fix_first = 1.0 - math.pow(beta_one, STEP)
    fix_second = 1.0 - math.pow(beta_two, STEP)
    direction = first_new / fix_first / (jnp.sqrt(second_new / fix_second) + adam_eps)
    return (
        weight - learn_rate * (direction + decay_rate * weight),
        jnp.stack([first_new, second_new]),
    )


def plain_shards(
    tokens,
    out_grad,
    segment_ids,
    qkv_weight,
    proj_weight,
    up_weight,
    down_weight,
    vectors,
    qkv_moments,
    proj_moments,
    up_moments,
    down_moments,
    vector_moments,
):
    columns_full = (
        lax.all_gather(qkv_weight.astype(jnp.bfloat16), "shard", axis=1, tiled=True),
        lax.all_gather(proj_weight.astype(jnp.bfloat16), "shard", axis=1, tiled=True),
        lax.all_gather(up_weight.astype(jnp.bfloat16), "shard", axis=1, tiled=True),
        lax.all_gather(down_weight.astype(jnp.bfloat16), "shard", axis=1, tiled=True),
        lax.all_gather(vectors.astype(jnp.bfloat16), "shard", axis=1, tiled=True),
    )
    qkv_work, proj_work, up_work, down_work, vec_bf = (
        lax.all_gather(columns_full[0], "dp", axis=0, tiled=True),
        lax.all_gather(columns_full[1], "dp", axis=0, tiled=True),
        lax.all_gather(columns_full[2], "dp", axis=0, tiled=True),
        lax.all_gather(columns_full[3], "dp", axis=0, tiled=True),
        lax.all_gather(columns_full[4], "dp", axis=1, tiled=True),
    )
    vec_work = vec_bf.astype(jnp.float32)
    head_count = D // HD
    score_scale = 1.0 / math.sqrt(HD)
    local_rows = tokens.shape[0]
    segment_row = segment_ids[0]
    length_all = segment_row.shape[0]
    row_start = lax.axis_index("shard") * local_rows
    query_index = row_start + jnp.arange(local_rows, dtype=jnp.int32)
    query_segment = lax.dynamic_slice_in_dim(segment_row, row_start, local_rows)
    positions = lax.dynamic_slice_in_dim(doc_positions(segment_row), row_start, local_rows)
    normed_one, unit_one, inverse_one = norm_rows(tokens, vec_work[0], vec_work[1])
    hidden_one = normed_one.astype(jnp.bfloat16)
    mixed_rows = jnp.dot(hidden_one, qkv_work, preferred_element_type=jnp.float32)
    query_raw = (mixed_rows[:, :D] + vec_work[4]).reshape(local_rows, head_count, HD)
    key_raw = mixed_rows[:, D : 2 * D].reshape(local_rows, head_count, HD)
    value_bf = (mixed_rows[:, 2 * D :] + vec_work[5]).astype(jnp.bfloat16)
    cosine_table, sine_table = rotary_tables(positions, ROT)
    query_bf = rotate(query_raw, cosine_table, sine_table).astype(jnp.bfloat16)
    key_bf = rotate(key_raw, cosine_table, sine_table).astype(jnp.bfloat16).reshape(local_rows, D)
    key_piece = lax.all_gather(key_bf, "shard", axis=0, tiled=True)
    value_piece = lax.all_gather(value_bf, "shard", axis=0, tiled=True)
    piece_rows = key_piece.shape[0]
    key_heads = key_piece.reshape(piece_rows, head_count, HD)
    value_heads = value_piece.reshape(piece_rows, head_count, HD)
    key_index = jnp.arange(piece_rows, dtype=jnp.int32)
    allowed = (segment_row[None, :] == query_segment[:, None]) & (
        key_index[None, :] <= query_index[:, None]
    )
    scores = (
        jnp.einsum("qhd,khd->hqk", query_bf, key_heads, preferred_element_type=jnp.float32)
        * score_scale
    )
    exp_scores = jnp.where(allowed[None], jnp.exp(scores), 0.0)
    numerator = jnp.einsum(
        "hqk,khd->qhd",
        exp_scores.astype(jnp.bfloat16),
        value_heads,
        preferred_element_type=jnp.float32,
    )
    numerator, totals = (numerator, jnp.sum(exp_scores, axis=-1))
    attended = numerator / jnp.transpose(totals)[:, :, None]
    log_totals = jnp.log(totals)
    attended_bf = attended.reshape(local_rows, D).astype(jnp.bfloat16)
    proj_out = jnp.dot(attended_bf, proj_work, preferred_element_type=jnp.float32) + vec_work[6]
    normed_two, unit_two, inverse_two = norm_rows(tokens, vec_work[2], vec_work[3])
    hidden_two = normed_two.astype(jnp.bfloat16)
    pre_act = jnp.dot(hidden_two, up_work, preferred_element_type=jnp.float32) + vec_work[
        8:
    ].reshape(FF)
    act_values, act_slope = gelu_pair(pre_act)
    act_bf = act_values.astype(jnp.bfloat16)
    block_out = (
        tokens
        + proj_out
        + (jnp.dot(act_bf, down_work, preferred_element_type=jnp.float32) + vec_work[7])
    )
    cot_bf = out_grad.astype(jnp.bfloat16)
    down_part = transposed_times(act_bf, cot_bf)
    proj_part = transposed_times(attended_bf, cot_bf)
    cot_sum = jnp.sum(out_grad, axis=0)
    grad_pre = times_transposed(cot_bf, down_work) * act_slope
    grad_pre_bf = grad_pre.astype(jnp.bfloat16)
    up_part = transposed_times(hidden_two, grad_pre_bf)
    rows_two, ln2_gain_part, ln2_bias_part = norm_back(
        times_transposed(grad_pre_bf, up_work), unit_two, inverse_two, vec_work[2]
    )
    grad_att_bf = (
        times_transposed(cot_bf, proj_work).astype(jnp.bfloat16).reshape(local_rows, head_count, HD)
    )
    keys_all, values_all = (
        lax.all_gather(key_bf, "shard", axis=0, tiled=True),
        lax.all_gather(value_bf, "shard", axis=0, tiled=True),
    )
    key_heads = keys_all.reshape(length_all, head_count, HD)
    value_heads = values_all.reshape(length_all, head_count, HD)
    key_index = jnp.arange(length_all, dtype=jnp.int32)
    allowed = (segment_row[None, :] == query_segment[:, None]) & (
        key_index[None, :] <= query_index[:, None]
    )
    scores = (
        jnp.einsum("qhd,khd->hqk", query_bf, key_heads, preferred_element_type=jnp.float32)
        * score_scale
    )
    probability = jnp.where(allowed[None], jnp.exp(scores - log_totals[:, :, None]), 0.0)
    grad_prob = jnp.einsum(
        "qhd,khd->hqk", grad_att_bf, value_heads, preferred_element_type=jnp.float32
    )
    row_delta = jnp.transpose(jnp.sum(grad_att_bf.astype(jnp.float32) * attended, axis=-1))
    grad_score = (probability * (grad_prob - row_delta[:, :, None]) * score_scale).astype(
        jnp.bfloat16
    )
    grad_query = jnp.einsum(
        "hqk,khd->qhd", grad_score, key_heads, preferred_element_type=jnp.float32
    )
    grad_query = rotate(grad_query, cosine_table, -sine_table).reshape(local_rows, D)
    key_terms = jnp.einsum(
        "hqk,qhd->khd", grad_score, query_bf, preferred_element_type=jnp.float32
    ).reshape(length_all, D)
    value_terms = jnp.einsum(
        "hqk,qhd->khd",
        probability.astype(jnp.bfloat16),
        grad_att_bf,
        preferred_element_type=jnp.float32,
    ).reshape(length_all, D)
    key_value_grad = lax.psum_scatter(
        jnp.concatenate([key_terms, value_terms], axis=1), "shard", scatter_dimension=0, tiled=True
    )
    grad_key = rotate(
        key_value_grad[:, :D].reshape(local_rows, head_count, HD), cosine_table, -sine_table
    ).reshape(local_rows, D)
    grad_value = key_value_grad[:, D:]
    grad_mixed_bf = jnp.concatenate([grad_query, grad_key, grad_value], axis=1).astype(jnp.bfloat16)
    qkv_part = transposed_times(hidden_one, grad_mixed_bf)
    rows_one, ln1_gain_part, ln1_bias_part = norm_back(
        times_transposed(grad_mixed_bf, qkv_work), unit_one, inverse_one, vec_work[0]
    )
    tokens_grad = out_grad + rows_one + rows_two
    vec_part = jnp.concatenate(
        [
            jnp.stack(
                [
                    ln1_gain_part,
                    ln1_bias_part,
                    ln2_gain_part,
                    ln2_bias_part,
                    jnp.sum(grad_query, axis=0),
                    jnp.sum(grad_value, axis=0),
                    cot_sum,
                    cot_sum,
                ]
            ),
            jnp.sum(grad_pre, axis=0).reshape(FF // D, D),
        ],
        axis=0,
    )
    groups = lax.axis_size("dp")
    members = lax.axis_size("shard")
    owners = groups * members
    vec_split = vec_part.reshape(VROWS, groups, members, D // owners)
    group_sums = (
        lax.psum_scatter(qkv_part, "shard", scatter_dimension=1, tiled=True),
        lax.psum_scatter(proj_part, "shard", scatter_dimension=1, tiled=True),
        lax.psum_scatter(up_part, "shard", scatter_dimension=1, tiled=True),
        lax.psum_scatter(down_part, "shard", scatter_dimension=1, tiled=True),
        lax.psum_scatter(vec_split, "shard", scatter_dimension=2, tiled=True),
    )
    owner_sums = (
        lax.psum_scatter(group_sums[0], "dp", scatter_dimension=0, tiled=True),
        lax.psum_scatter(group_sums[1], "dp", scatter_dimension=0, tiled=True),
        lax.psum_scatter(group_sums[2], "dp", scatter_dimension=0, tiled=True),
        lax.psum_scatter(group_sums[3], "dp", scatter_dimension=0, tiled=True),
        lax.psum_scatter(group_sums[4], "dp", scatter_dimension=1, tiled=True),
    )
    qkv_grad = owner_sums[0]
    proj_grad = owner_sums[1]
    up_grad = owner_sums[2]
    down_grad = owner_sums[3]
    vectors_grad = owner_sums[4].reshape(VROWS, D // owners)
    local_square = (
        jnp.sum(qkv_grad * qkv_grad)
        + jnp.sum(proj_grad * proj_grad)
        + jnp.sum(up_grad * up_grad)
        + jnp.sum(down_grad * down_grad)
        + jnp.sum(vectors_grad * vectors_grad)
    )
    square_total = lax.psum(local_square, ("dp", "shard"))
    norm_limit = math.sqrt(NPARAM)
    clip_factor = norm_limit / jnp.maximum(jnp.sqrt(square_total), norm_limit)
    qkv_new, qkv_moments_new = adam_update(qkv_weight, qkv_moments, qkv_grad, clip_factor)
    proj_new, proj_moments_new = adam_update(proj_weight, proj_moments, proj_grad, clip_factor)
    up_new, up_moments_new = adam_update(up_weight, up_moments, up_grad, clip_factor)
    down_new, down_moments_new = adam_update(down_weight, down_moments, down_grad, clip_factor)
    vectors_new, vector_moments_new = adam_update(
        vectors, vector_moments, vectors_grad, clip_factor
    )
    return (
        block_out,
        tokens_grad,
        qkv_grad,
        proj_grad,
        up_grad,
        down_grad,
        vectors_grad,
        qkv_new,
        proj_new,
        up_new,
        down_new,
        vectors_new,
        qkv_moments_new,
        proj_moments_new,
        up_moments_new,
        down_moments_new,
        vector_moments_new,
    )

MESH = pl.DeviceIdType.MESH
LANES = 128


def place(groups):
    group = lax.axis_index("dp")
    depth = groups // 4
    return depth, group // 4, lax.rem(group // 2, 2), lax.rem(group, 2), lax.axis_index("shard")


def device(z, y, c, x):
    return (z * 4 + y * 2 + c, x)


def greet(peers):
    barrier = pltpu.get_barrier_semaphore()
    for peer in peers:
        pl.semaphore_signal(barrier, inc=1, device_id=peer, device_id_type=MESH)
    pl.semaphore_wait(barrier, len(peers))


def half_lanes(member, width):
    return pl.ds(pl.multiple_of(member * width, LANES), width)


def gather_kernel(
    groups,
    vec_in, qkv_keep, qkv_send, proj_in, up_keep, up_send, down_keep, down_send, unit_in, cot_in,
    vec_out, qkv_out, proj_out, up_out, down_out, unit_out, cot_out,
    send_sem, recv_sem, row_send, row_recv, local_sem,
):
    depth, z, y, c, x = place(groups)
    names = ("vec", "qkv", "proj", "up", "down")
    outs = dict(vec=vec_out, qkv=qkv_out, proj=proj_out, up=up_out, down=down_out)

    def block(name, zz, yy, cc):
        ref = outs[name]
        if name == "proj":
            return ref.at[zz, cc, :, half_lanes(yy, ref.shape[3] // 2)]
        return ref.at[zz, yy, cc]

    def rows(name, member):
        ref = outs[name]
        if name == "vec":
            return ref.at[z, y, c, member]
        return ref.at[z, y, c, :, half_lanes(member, ref.shape[4] // 2)]

    def remote(src, dst, sems, index, peer):
        return pltpu.make_async_remote_copy(
            src_ref=src, dst_ref=dst, send_sem=sems[0].at[index], recv_sem=sems[1].at[index],
            device_id=peer, device_id_type=MESH,
        )

    weight_sems, row_sems = (send_sem, recv_sem), (row_send, row_recv)
    across = device(z, y, c, 1 - x)
    beside = device(z, 1 - y, c, x)
    twin = device(z, y, 1 - c, x)
    corner = device(z, x, c, y)
    far = [lax.rem(z + k, depth) for k in range(1, depth)]
    back = [lax.rem(z + depth - k, depth) for k in range(depth)]
    greet(
        [across, beside, twin, device(z, 1 - y, c, 1 - x)] + [device(zz, y, c, x) for zz in far]
    )

    swaps, stays = {}, {}
    pieces = dict(
        vec=(vec_in, vec_in), qkv=(qkv_keep, qkv_send), up=(up_keep, up_send),
        down=(down_keep, down_send),
    )
    local = 0
    for a, name in enumerate(names):
        if name == "proj":
            continue
        keep, sent = pieces[name]
        swaps[name] = remote(sent, rows(name, x), weight_sems, (a, 0), across)
        swaps[name].start()
        stays[name] = pltpu.make_async_copy(keep, rows(name, x), local_sem.at[local])
        stays[name].start()
        local += 1
    own = block("proj", z, y, c)
    proj_index = names.index("proj")
    proj_move = remote(
        proj_in, proj_out.at[z, c, :, half_lanes(x, proj_out.shape[3] // 2)],
        weight_sems, (proj_index, 0), corner,
    )
    proj_stay = pltpu.make_async_copy(proj_in, own, local_sem.at[local])
    pl.when(x != y)(lambda: proj_move.start())
    pl.when(x == y)(lambda: proj_stay.start())
    local += 1
    row_copies = []
    for k, (mine, whole) in enumerate(((unit_in, unit_out), (cot_in, cot_out))):
        copy = remote(mine, whole.at[x], row_sems, k, across)
        stay = pltpu.make_async_copy(mine, whole.at[x], local_sem.at[local])
        copy.start()
        stay.start()
        local += 1
        row_copies.append((copy, stay))

    along, over, pair = {}, {}, {}
    for a, name in enumerate(names):
        if name == "proj":
            def moved():
                proj_move.wait()

            def stayed():
                proj_stay.wait()

            pl.when(x != y)(moved)
            pl.when(x == y)(stayed)
        else:
            stays[name].wait()
            swaps[name].wait()
        mine = block(name, z, y, c)
        for k in range(1, depth):
            along[name, k] = remote(
                mine, mine, weight_sems, (a, k), device(far[k - 1], y, c, x)
            )
            along[name, k].start()
        over[name, 0] = remote(mine, mine, weight_sems, (a, depth), beside)
        over[name, 0].start()
        pair[name, 0, 0] = remote(mine, mine, weight_sems, (a, 2 * depth), twin)
        pair[name, 0, 0].start()
    for a, name in enumerate(names):
        for k in range(1, depth):
            along[name, k].wait_recv()
            come = block(name, back[k], y, c)
            over[name, k] = remote(come, come, weight_sems, (a, depth + k), beside)
            over[name, k].start()
            pair[name, 0, k] = remote(come, come, weight_sems, (a, 2 * depth + k), twin)
            pair[name, 0, k].start()
        for k in range(depth):
            over[name, k].wait_recv()
            come = block(name, back[k], 1 - y, c)
            pair[name, 1, k] = remote(come, come, weight_sems, (a, 3 * depth + k), twin)
            pair[name, 1, k].start()
    for copy, stay in row_copies:
        stay.wait()
        copy.wait()
    for name in names:
        for side in range(2):
            for k in range(depth):
                pair[name, side, k].wait()
        for k in range(depth):
            over[name, k].wait_send()
        for k in range(1, depth):
            along[name, k].wait_send()


def gather_all(groups, vec_in, qkv, proj_in, up, down, unit_bf, cot_bf):
    depth = groups // 4
    (qkv_keep, qkv_send), (up_keep, up_send), (down_keep, down_send) = qkv, up, down
    kind = jnp.bfloat16

    def grid_of(piece):
        return jax.ShapeDtypeStruct((depth, 2, 2, piece.shape[0], 2 * piece.shape[1]), kind)

    shapes = [
        jax.ShapeDtypeStruct((depth, 2, 2, 2) + vec_in.shape, kind),
        grid_of(qkv_keep),
        jax.ShapeDtypeStruct((depth, 2, proj_in.shape[0], 2 * proj_in.shape[1]), kind),
        grid_of(up_keep),
        grid_of(down_keep),
        jax.ShapeDtypeStruct((2,) + unit_bf.shape, kind),
        jax.ShapeDtypeStruct((2,) + cot_bf.shape, kind),
    ]
    vmem = pl.BlockSpec(memory_space=pltpu.VMEM)
    hbm = pl.BlockSpec(memory_space=pl.ANY)
    sent = 16 * qkv_keep.size * 13
    return pl.pallas_call(
        lambda *refs: gather_kernel(groups, *refs),
        in_specs=[vmem] * 10,
        out_specs=[hbm] * 7,
        out_shape=shapes,
        scratch_shapes=[
            pltpu.SemaphoreType.DMA((5, 4 * depth)),
            pltpu.SemaphoreType.DMA((5, 4 * depth)),
            pltpu.SemaphoreType.DMA((2,)),
            pltpu.SemaphoreType.DMA((2,)),
            pltpu.SemaphoreType.DMA((7,)),
        ],
        compiler_params=pltpu.CompilerParams(collective_id=0, has_side_effects=True),
        cost_estimate=pl.CostEstimate(flops=0, bytes_accessed=sent, transcendentals=0),
        name="gather_all",
    )(vec_in, qkv_keep, qkv_send, proj_in, up_keep, up_send, down_keep, down_send, unit_bf, cot_bf)


def square_sum(values):
    return jnp.sum(jnp.sum(values * values, axis=1, keepdims=True), axis=0, keepdims=True)


def reduce_kernel(
    groups,
    down_in, up_in, proj_in, qkv_in, vec_in,
    down_out, up_out, proj_out, qkv_out, vec_out, square_out,
    down_own, down_one, down_mid, down_two, down_cross, down_last, down_three, down_end, down_swap,
    up_own, up_one, up_mid, up_two, up_cross, up_last, up_three, up_end, up_swap,
    proj_own, proj_one, proj_mid, proj_two, proj_cross, proj_last, proj_three, proj_end, proj_swap,
    qkv_own, qkv_one, qkv_mid, qkv_two, qkv_cross, qkv_last, qkv_three, qkv_end, qkv_swap,
    vec_held, vec_come, tile_held, tile_come,
    send_sem, recv_sem, vec_send, vec_recv, local_sem,
):
    depth, z, y, c, x = place(groups)
    names = ("down", "up", "proj", "qkv")
    parts = dict(down=down_in, up=up_in, proj=proj_in, qkv=qkv_in)
    own = dict(down=down_own, up=up_own, proj=proj_own, qkv=qkv_own)
    one = dict(down=down_one, up=up_one, proj=proj_one, qkv=qkv_one)
    mid = dict(down=down_mid, up=up_mid, proj=proj_mid, qkv=qkv_mid)
    two = dict(down=down_two, up=up_two, proj=proj_two, qkv=qkv_two)
    cross = dict(down=down_cross, up=up_cross, proj=proj_cross, qkv=qkv_cross)
    last = dict(down=down_last, up=up_last, proj=proj_last, qkv=qkv_last)
    three = dict(down=down_three, up=up_three, proj=proj_three, qkv=qkv_three)
    end = dict(down=down_end, up=up_end, proj=proj_end, qkv=qkv_end)
    swap = dict(down=down_swap, up=up_swap, proj=proj_swap, qkv=qkv_swap)
    across = device(z, y, c, 1 - x)
    beside = device(z, 1 - y, c, x)
    twin = device(z, y, 1 - c, x)
    corner = device(z, x, c, y)
    far = [lax.rem(z + k, depth) for k in range(1, depth)]
    alongs = [device(zz, y, c, x) for zz in far]
    near = [
        device(z, yy, cc, xx)
        for xx in (x, 1 - x) for yy in (y, 1 - y) for cc in (c, 1 - c)
    ][1:]
    greet(near + alongs)

    def remote(src, dst, index, peer, sems=(send_sem, recv_sem)):
        return pltpu.make_async_remote_copy(
            src_ref=src, dst_ref=dst, send_sem=sems[0].at[index], recv_sem=sems[1].at[index],
            device_id=peer, device_id_type=MESH,
        )

    def wide(values):
        return values.astype(jnp.float32)

    vec_sems = (vec_send, vec_recv)
    vec_copies = [remote(vec_in, vec_come.at[0], 0, twin, vec_sems)]
    vec_copies[0].start()
    first, stays = {}, {}
    for a, name in enumerate(names):
        part = parts[name]
        theirs = part.at[:, 1 - c] if name == "proj" else part.at[:, :, 1 - c]
        mine = part.at[:, c] if name == "proj" else part.at[:, :, c]
        first[name] = remote(theirs, one[name], (a, 0), twin)
        first[name].start()
        stays[name] = pltpu.make_async_copy(mine, own[name], local_sem.at[a])
        stays[name].start()

    second, third, fourth = {}, {}, {}

    def step_one(a, name):
        first[name].wait()
        stays[name].wait()

        def body(zz, carry):
            if name == "proj":
                half = own[name].shape[2] // 2
                ours, theirs = half_lanes(y, half), half_lanes(1 - y, half)
                cross[name][zz] = (
                    wide(own[name][zz, :, theirs]) + wide(one[name][zz, :, theirs])
                ).astype(jnp.bfloat16)
                mid[name][zz] = wide(own[name][zz, :, ours]) + wide(one[name][zz, :, ours])
            else:
                cross[name][zz] = (
                    wide(own[name][zz, 1 - y]) + wide(one[name][zz, 1 - y])
                ).astype(jnp.bfloat16)
                mid[name][zz] = wide(own[name][zz, y]) + wide(one[name][zz, y])
            return carry

        lax.fori_loop(0, depth, body, 0)
        second[name] = remote(cross[name], two[name], (a, 1), beside)
        second[name].start()

    def step_two(a, name):
        second[name].wait()
        for k in range(1, depth):
            zz = far[k - 1]
            last[name][k - 1] = (mid[name][zz] + wide(two[name][zz])).astype(jnp.bfloat16)
            third[name, k] = remote(
                last[name].at[k - 1], three[name].at[k - 1], (a, 1 + k), alongs[k - 1]
            )
            third[name, k].start()

    def moved(name):
        return name != "proj"

    def step_three(a, name):
        for k in range(1, depth):
            third[name, k].wait()
        total = mid[name][z] + wide(two[name][z])
        for k in range(1, depth):
            total = total + wide(three[name][k - 1])
        mid[name][0] = total
        if name == "proj":
            end[name][...] = total.astype(jnp.bfloat16)
            fourth[name] = remote(end[name], swap[name], (a, depth + 1), corner)
            pl.when(x != y)(lambda: fourth[name].start())
        else:
            half = total.shape[1] // 2
            end[name][...] = mid[name][0, :, half_lanes(1 - x, half)].astype(jnp.bfloat16)
            fourth[name] = remote(end[name], swap[name], (a, depth + 1), across)
            fourth[name].start()

    def step_four(a, name):
        if name == "proj":
            def swapped():
                fourth[name].wait()
                proj_out[...] = wide(swap[name][...])

            def kept():
                proj_out[...] = mid[name][0]

            pl.when(x != y)(swapped)
            pl.when(x == y)(kept)
            return square_sum(proj_out[...])
        fourth[name].wait()
        half = swap[name].shape[1]
        mine = mid[name][0, :, half_lanes(x, half)]
        theirs = wide(swap[name][...])
        if name == "down":
            size = mine.shape[0]
            down_out[pl.ds(pl.multiple_of(x * size, 8), size), :] = mine
            down_out[pl.ds(pl.multiple_of((1 - x) * size, 8), size), :] = theirs
        else:
            out = dict(up=up_out, qkv=qkv_out)[name]
            for b in range(half // LANES):
                lanes = slice(b * LANES, (b + 1) * LANES)
                out[:, half_lanes(2 * b + x, LANES)] = mine[:, lanes]
                out[:, half_lanes(2 * b + 1 - x, LANES)] = theirs[:, lanes]
        return square_sum(mine) + square_sum(theirs)

    def vec_step(index, peers):
        for copy in vec_copies:
            copy.wait()
        vec_copies.clear()
        held = vec_in[...] if index == 0 else vec_held[index - 1]
        come = (0,) if index == 0 else (index,)
        vec_held[index] = held + vec_come[come[0]]
        for k, peer in enumerate(peers):
            copy = remote(
                vec_held.at[index], vec_come.at[index + 1 + k], index + 1 + k, peer, vec_sems
            )
            copy.start()
            vec_copies.append(copy)

    step_one(0, "down")
    vec_step(0, [across])
    step_one(1, "up")
    step_two(0, "down")
    vec_step(1, [beside])
    step_one(2, "proj")
    step_one(3, "qkv")
    step_two(1, "up")
    vec_step(2, alongs)
    step_three(0, "down")
    step_two(2, "proj")
    step_two(3, "qkv")
    step_three(1, "up")
    squares = step_four(0, "down")
    for copy in vec_copies:
        copy.wait()
    vec_total = vec_held[2]
    for k in range(depth - 1):
        vec_total = vec_total + vec_come[3 + k]
    vec_out[...] = vec_total
    step_three(2, "proj")
    squares = squares + step_four(1, "up")
    step_three(3, "qkv")
    squares = squares + step_four(2, "proj")
    squares = squares + step_four(3, "qkv")

    base = 3 + depth
    tile_held[0] = jnp.broadcast_to(squares, tile_held.shape[1:])
    copies = [
        remote(tile_held.at[0], tile_come.at[k], base + k, peer, vec_sems)
        for k, peer in enumerate(alongs)
    ]
    for copy in copies:
        copy.start()
    for copy in copies:
        copy.wait()
    tile = tile_held[0]
    for k in range(depth - 1):
        tile = tile + tile_come[k]
    tile_held[1] = tile
    copies = [
        remote(tile_held.at[1], tile_come.at[depth - 1 + k], base + depth - 1 + k, peer, vec_sems)
        for k, peer in enumerate(near)
    ]
    for copy in copies:
        copy.start()
    for copy in copies:
        copy.wait()
    for k in range(len(near)):
        tile = tile + tile_come[depth - 1 + k]
    square_out[...] = tile + square_sum(vec_total)


def reduce_all(groups, down_part, up_part, proj_part, qkv_part, vec_part):
    depth = groups // 4
    wide, kind = jnp.float32, jnp.bfloat16

    def grid_of(part):
        return part.reshape(depth, 2, 2, part.shape[0] // groups, part.shape[1])

    parts = [
        grid_of(down_part),
        grid_of(up_part),
        proj_part.reshape(depth, 2, proj_part.shape[0] // depth // 2, proj_part.shape[1]),
        grid_of(qkv_part),
    ]
    scratch = []
    for index, part in enumerate(parts):
        rows, columns = part.shape[-2:]
        block = (rows, columns // 2 if index == 2 else columns)
        held = (depth, rows, columns) if index == 2 else (depth, 2, rows, columns)
        final = block if index == 2 else (rows, columns // 2)
        scratch += [
            pltpu.VMEM(held, kind), pltpu.VMEM(held, kind),
            pltpu.VMEM((depth,) + block, wide), pltpu.VMEM((depth,) + block, kind),
            pltpu.VMEM((depth,) + block, kind), pltpu.VMEM((depth - 1,) + block, kind),
            pltpu.VMEM((depth - 1,) + block, kind), pltpu.VMEM(final, kind),
            pltpu.VMEM(final, kind),
        ]
    near = 7
    scratch += [
        pltpu.VMEM((3,) + vec_part.shape, wide),
        pltpu.VMEM((2 + depth,) + vec_part.shape, wide),
        pltpu.VMEM((2, 8, LANES), wide),
        pltpu.VMEM((depth - 1 + near, 8, LANES), wide),
        pltpu.SemaphoreType.DMA((4, depth + 2)),
        pltpu.SemaphoreType.DMA((4, depth + 2)),
        pltpu.SemaphoreType.DMA((2 + 2 * depth + near,)),
        pltpu.SemaphoreType.DMA((2 + 2 * depth + near,)),
        pltpu.SemaphoreType.DMA((4,)),
    ]
    down, up, proj, qkv = parts
    shapes = [
        jax.ShapeDtypeStruct((2 * down.shape[-2], down.shape[-1] // 2), wide),
        jax.ShapeDtypeStruct(up.shape[-2:], wide),
        jax.ShapeDtypeStruct((proj.shape[-2], proj.shape[-1] // 2), wide),
        jax.ShapeDtypeStruct(qkv.shape[-2:], wide),
        jax.ShapeDtypeStruct(vec_part.shape, wide),
        jax.ShapeDtypeStruct((8, LANES), wide),
    ]
    vmem = pl.BlockSpec(memory_space=pltpu.VMEM)
    hbm = pl.BlockSpec(memory_space=pl.ANY)
    return pl.pallas_call(
        lambda *refs: reduce_kernel(groups, *refs),
        in_specs=[hbm] * 4 + [vmem],
        out_specs=[vmem] * 6,
        out_shape=shapes,
        scratch_shapes=scratch,
        compiler_params=pltpu.CompilerParams(
            collective_id=1, has_side_effects=True, vmem_limit_bytes=56 * 1024 * 1024
        ),
        cost_estimate=pl.CostEstimate(
            flops=0, bytes_accessed=4 * sum(part.size for part in parts), transcendentals=0
        ),
        name="reduce_all",
    )(*parts, vec_part)


def adam_kernel(square_ref, *refs):
    count = len(refs) // 6
    norm_limit = math.sqrt(NPARAM)
    clip = norm_limit / jnp.maximum(jnp.sqrt(square_ref[0:1, 0:1]), norm_limit)
    fix_first = 1.0 - math.pow(beta_one, STEP)
    fix_second = 1.0 - math.pow(beta_two, STEP)
    ins, outs = refs[: 3 * count], refs[3 * count :]
    for index in range(count):
        weight_ref, moment_ref, grad_ref = ins[3 * index : 3 * index + 3]
        grad_out, weight_out, moment_out = outs[3 * index : 3 * index + 3]
        grad, weight = grad_ref[...], weight_ref[...]
        clipped = grad * clip
        first_new = beta_one * moment_ref[0] + (1.0 - beta_one) * clipped
        second_new = beta_two * moment_ref[1] + (1.0 - beta_two) * clipped * clipped
        direction = first_new / fix_first / (jnp.sqrt(second_new / fix_second) + adam_eps)
        grad_out[...] = grad
        weight_out[...] = weight - learn_rate * (direction + decay_rate * weight)
        moment_out[0] = first_new
        moment_out[1] = second_new


def adam_all(square, weights, moments, grads):
    steps = 4
    in_specs = [pl.BlockSpec(square.shape, lambda i: (0, 0))]
    out_specs, shapes, ins = [], [], [square]
    for weight, moment, grad in zip(weights, moments, grads):
        rows, columns = weight.shape
        if rows % (8 * steps) == 0:
            flat = pl.BlockSpec((rows // steps, columns), lambda i: (i, 0))
            both = pl.BlockSpec((2, rows // steps, columns), lambda i: (0, i, 0))
        else:
            flat = pl.BlockSpec((rows, columns), lambda i: (0, 0))
            both = pl.BlockSpec((2, rows, columns), lambda i: (0, 0, 0))
        in_specs += [flat, both, flat]
        out_specs += [flat, flat, both]
        shapes += [
            jax.ShapeDtypeStruct(grad.shape, grad.dtype),
            jax.ShapeDtypeStruct(weight.shape, weight.dtype),
            jax.ShapeDtypeStruct(moment.shape, moment.dtype),
        ]
        ins += [weight, moment, grad]
    size = sum(weight.size for weight in weights)
    results = pl.pallas_call(
        adam_kernel,
        grid=(steps,),
        in_specs=in_specs,
        out_specs=out_specs,
        out_shape=shapes,
        cost_estimate=pl.CostEstimate(
            flops=20 * size, bytes_accessed=32 * size, transcendentals=2 * size
        ),
        name="adam_all",
    )(*ins)
    return results[0::3], results[1::3], results[2::3]


def swap_shard(piece):
    return lax.ppermute(piece, "shard", [(0, 1), (1, 0)])


def pick(array, index, axis):
    return lax.dynamic_index_in_dim(array, index, axis=axis, keepdims=False)


def split_columns(piece, member):
    rows = piece.shape[0]
    blocks = piece.reshape(rows, -1, 2, LANES)
    return (
        pick(blocks, member, 2).reshape(rows, -1),
        pick(blocks, 1 - member, 2).reshape(rows, -1),
    )


def sum_halves(partial, member, local_rows):
    halves = partial.reshape(2, local_rows, partial.shape[-1])
    received = swap_shard(pick(halves, 1 - member, 0).astype(jnp.bfloat16))
    return pick(halves, member, 0) + received.astype(jnp.float32)


def spread(values, width, member):
    blocks = values.reshape(-1, 1, width)
    chosen = jnp.arange(2, dtype=jnp.int32)[None, :, None] == member
    return jnp.where(chosen, blocks, 0.0).reshape(-1)


def rolled(rows, cosine, down_sine, up_sine):
    width = rows.shape[1]
    lower = pltpu.roll(rows, width - ROT // 2, 1)
    upper = pltpu.roll(rows, ROT // 2, 1)
    return rows * cosine + lower * down_sine + upper * up_sine


def split_pair(rows):
    lanes = lax.broadcasted_iota(jnp.int32, rows.shape, 1)
    return (
        jnp.where(lanes < HD, rows, jnp.zeros_like(rows)),
        jnp.where(lanes < HD, jnp.zeros_like(rows), rows),
    )


def block_mask(seg_column, seg_row, start, size, extent):
    rows = start + lax.broadcasted_iota(jnp.int32, (size, extent), 0)
    keys = lax.broadcasted_iota(jnp.int32, (size, extent), 1)
    same = seg_column[start : start + size, :] == seg_row[:, :extent]
    return same & (keys <= rows)


def attend_kernel(
    query_ref, key_ref, value_ref, q_bias_ref, v_bias_ref, cos_ref, down_ref, up_ref,
    column_ref, row_ref, query_out, key_out, value_out, att_out, att_bf_out, log_out,
):
    scale = 1.0 / math.sqrt(HD)
    length = query_ref.shape[0]
    size = length // 4
    cosine, down_sine, up_sine = cos_ref[...], down_ref[...], up_ref[...]
    query_out[...] = rolled(
        query_ref[...] + q_bias_ref[...], cosine, down_sine, up_sine
    ).astype(jnp.bfloat16)
    key_out[...] = rolled(key_ref[...], cosine, down_sine, up_sine).astype(jnp.bfloat16)
    value_out[...] = (value_ref[...] + v_bias_ref[...]).astype(jnp.bfloat16)
    for start in range(0, length, size):
        extent = start + size
        mask = block_mask(column_ref, row_ref, start, size, extent)
        keys, values = key_out[:extent, :], value_out[:extent, :]
        results = []
        for query in split_pair(query_out[start:extent, :].astype(jnp.float32)):
            scores = times_transposed(query.astype(jnp.bfloat16), keys) * scale
            exp_scores = jnp.where(mask, jnp.exp(scores), 0.0)
            totals = jnp.sum(exp_scores, axis=1, keepdims=True)
            numerator = jnp.dot(
                exp_scores.astype(jnp.bfloat16), values, preferred_element_type=jnp.float32
            )
            results.append((numerator / totals, jnp.log(totals)))
        lanes = lax.broadcasted_iota(jnp.int32, (size, 2 * HD), 1) < HD
        attended = jnp.where(lanes, results[0][0], results[1][0])
        att_out[start:extent, :] = attended
        att_bf_out[start:extent, :] = attended.astype(jnp.bfloat16)
        log_out[start:extent, :] = jnp.where(lanes, results[0][1], results[1][1])


def attend_back_kernel(
    query_ref, key_ref, value_ref, grad_ref, att_ref, log_ref, cos_ref, down_ref, up_ref,
    column_ref, row_ref, query_out, key_out, value_out, q_bias_out, v_bias_out,
    query_sum, key_sum, value_sum,
):
    scale = 1.0 / math.sqrt(HD)
    length = query_ref.shape[0]
    size = length // 4
    key_sum[...] = jnp.zeros_like(key_sum)
    value_sum[...] = jnp.zeros_like(value_sum)
    for start in range(0, length, size):
        extent = start + size
        mask = block_mask(column_ref, row_ref, start, size, extent)
        keys, values = key_ref[:extent, :], value_ref[:extent, :]
        queries = split_pair(query_ref[start:extent, :].astype(jnp.float32))
        grads = split_pair(grad_ref[start:extent, :].astype(jnp.float32))
        attended = att_ref[start:extent, :]
        pieces = []
        for head in range(2):
            query = queries[head].astype(jnp.bfloat16)
            grad = grads[head].astype(jnp.bfloat16)
            log_total = log_ref[start:extent, head * HD : head * HD + 1]
            scores = times_transposed(query, keys) * scale
            probability = jnp.where(mask, jnp.exp(scores - log_total), 0.0)
            grad_prob = times_transposed(grad, values)
            delta = jnp.sum(grads[head] * attended, axis=1, keepdims=True)
            grad_score = (probability * (grad_prob - delta) * scale).astype(jnp.bfloat16)
            pieces.append(jnp.dot(grad_score, keys, preferred_element_type=jnp.float32))
            key_sum[:extent, :] += transposed_times(grad_score, query)
            value_sum[:extent, :] += transposed_times(probability.astype(jnp.bfloat16), grad)
        lanes = lax.broadcasted_iota(jnp.int32, (size, 2 * HD), 1) < HD
        query_sum[start:extent, :] = jnp.where(lanes, pieces[0], pieces[1])
    cosine, down_sine, up_sine = cos_ref[...], down_ref[...], up_ref[...]
    grad_query = rolled(query_sum[...], cosine, -down_sine, -up_sine)
    query_out[...] = grad_query.astype(jnp.bfloat16)
    q_bias_out[...] = jnp.sum(grad_query, axis=0, keepdims=True)
    key_out[...] = rolled(key_sum[...], cosine, -down_sine, -up_sine).astype(jnp.bfloat16)
    grad_value = value_sum[...]
    value_out[...] = grad_value.astype(jnp.bfloat16)
    v_bias_out[...] = jnp.sum(grad_value, axis=0, keepdims=True)


def lane_tables(positions):
    dims = jnp.arange(2 * HD, dtype=jnp.int32) % HD
    half_dims = ROT // 2
    exponent = (dims % half_dims).astype(jnp.float32) * (2.0 / ROT)
    inverse_freq = jnp.exp(-math.log(rope_base) * exponent)
    angles = positions.astype(jnp.float32)[:, None] * inverse_freq[None, :]
    sine = jnp.sin(angles)
    return (
        jnp.where(dims[None] < ROT, jnp.cos(angles), 1.0),
        jnp.where(dims[None] < half_dims, -sine, 0.0),
        jnp.where((dims[None] >= half_dims) & (dims[None] < ROT), sine, 0.0),
    )


def pair_specs(length):
    def columns(offset):
        return pl.BlockSpec((length, 2 * HD), lambda j: (0, offset + j))

    table = pl.BlockSpec((length, 2 * HD), lambda j: (0, 0))
    bias = pl.BlockSpec((1, 2 * HD), lambda j: (0, j))
    seg_column = pl.BlockSpec((length, 1), lambda j: (0, 0))
    seg_row = pl.BlockSpec((1, length), lambda j: (0, 0))
    return columns, table, bias, seg_column, seg_row


def attend(mixed_rows, q_bias, v_bias, tables, segment_row):
    length = mixed_rows.shape[0]
    width = mixed_rows.shape[1] // 3
    pairs = width // (2 * HD)
    columns, table, bias, seg_column, seg_row = pair_specs(length)
    shapes = [jnp.bfloat16, jnp.bfloat16, jnp.bfloat16, jnp.float32, jnp.bfloat16, jnp.float32]
    flops = 4 * length * length * width
    return pl.pallas_call(
        attend_kernel,
        grid=(pairs,),
        in_specs=[columns(0), columns(pairs), columns(2 * pairs), bias, bias, table, table, table,
                  seg_column, seg_row],
        out_specs=[columns(0)] * 6,
        out_shape=[jax.ShapeDtypeStruct((length, width), kind) for kind in shapes],
        cost_estimate=pl.CostEstimate(
            flops=flops, bytes_accessed=24 * length * width, transcendentals=flops // (4 * HD)
        ),
        name="attend",
    )(mixed_rows, mixed_rows, mixed_rows, q_bias[None], v_bias[None], *tables,
      segment_row[:, None], segment_row[None, :])


def attend_back(query, key, value, grad, attended, log_totals, tables, segment_row):
    length, width = query.shape
    pairs = width // (2 * HD)
    columns, table, bias, seg_column, seg_row = pair_specs(length)
    flops = 10 * length * length * width
    return pl.pallas_call(
        attend_back_kernel,
        grid=(pairs,),
        in_specs=[columns(0)] * 6 + [table, table, table, seg_column, seg_row],
        out_specs=[columns(0)] * 3 + [bias, bias],
        out_shape=[jax.ShapeDtypeStruct((length, width), jnp.bfloat16)] * 3
        + [jax.ShapeDtypeStruct((1, width), jnp.float32)] * 2,
        scratch_shapes=[pltpu.VMEM((length, 2 * HD), jnp.float32)] * 3,
        cost_estimate=pl.CostEstimate(
            flops=flops, bytes_accessed=24 * length * width, transcendentals=flops // (10 * HD)
        ),
        name="attend_back",
    )(query, key, value, grad, attended, log_totals, *tables,
      segment_row[:, None], segment_row[None, :])


def shards(
    tokens,
    out_grad,
    segment_ids,
    qkv_weight,
    proj_weight,
    up_weight,
    down_weight,
    vectors,
    qkv_moments,
    proj_moments,
    up_moments,
    down_moments,
    vector_moments,
):
    groups = lax.axis_size("dp")
    members = lax.axis_size("shard")
    head_count = D // HD
    if members != 2 or groups != head_count:
        return plain_shards(
            tokens,
            out_grad,
            segment_ids,
            qkv_weight,
            proj_weight,
            up_weight,
            down_weight,
            vectors,
            qkv_moments,
            proj_moments,
            up_moments,
            down_moments,
            vector_moments,
        )
    member = lax.axis_index("shard")
    group = lax.axis_index("dp")
    half = D // 2
    local_rows = tokens.shape[0]
    vec_width = vectors.shape[1]
    pairs = half // LANES

    center = tokens - jnp.mean(tokens, axis=-1, keepdims=True)
    inverse = lax.rsqrt(jnp.mean(center * center, axis=-1, keepdims=True) + ln_eps)
    unit = center * inverse

    vec_piece = jnp.pad(
        vectors.astype(jnp.bfloat16), ((0, 16 - VROWS), (0, LANES - vec_width))
    )
    down_blocks = down_weight.astype(jnp.bfloat16).reshape(2, LANES, half)
    vec_all, qkv_all, proj_all, up_all, down_all, unit_all, cot_all = gather_all(
        groups,
        vec_piece,
        split_columns(qkv_weight.astype(jnp.bfloat16), member),
        proj_weight.astype(jnp.bfloat16),
        split_columns(up_weight.astype(jnp.bfloat16), member),
        (pick(down_blocks, member, 0), pick(down_blocks, 1 - member, 0)),
        unit.astype(jnp.bfloat16),
        out_grad.astype(jnp.bfloat16),
    )
    vec_work = (
        vec_all.reshape(2 * groups, 16, LANES)[:, :VROWS, :vec_width]
        .transpose(1, 0, 2)
        .reshape(VROWS, D)
        .astype(jnp.float32)
    )
    qkv_work = qkv_all.reshape(D, 3 * half)
    proj_work = proj_all.reshape(half, D)
    up_work = up_all.reshape(D, FF // 2)
    down_work = down_all.reshape(FF // 2, D)
    unit_rows = unit_all.reshape(2 * local_rows, D).astype(jnp.float32)
    cot_bf = cot_all.reshape(2 * local_rows, D)
    hidden_one = (unit_rows * vec_work[0] + vec_work[1]).astype(jnp.bfloat16)
    hidden_two = (unit_rows * vec_work[2] + vec_work[3]).astype(jnp.bfloat16)

    segment_row = segment_ids[0]
    positions = doc_positions(segment_row)
    tables = lane_tables(positions)

    q_bias = pick(vec_work[4].reshape(pairs, 2, LANES), member, 1).reshape(-1)
    v_bias = pick(vec_work[5].reshape(pairs, 2, LANES), member, 1).reshape(-1)
    up_bias = pick(vec_work[8:].reshape(groups, 2, LANES), member, 1).reshape(-1)

    mixed_rows = jnp.dot(hidden_one, qkv_work, preferred_element_type=jnp.float32)
    query_bf, key_bf, value_bf, attended, attended_bf, log_totals = attend(
        mixed_rows, q_bias, v_bias, tables, segment_row
    )
    grad_att_bf = times_transposed(cot_bf, proj_work).astype(jnp.bfloat16)
    proj_part = transposed_times(attended_bf, cot_bf).astype(jnp.bfloat16)

    pre_act = jnp.dot(hidden_two, up_work, preferred_element_type=jnp.float32) + up_bias
    act_values, act_slope = gelu_pair(pre_act)
    act_bf = act_values.astype(jnp.bfloat16)
    grad_pre = times_transposed(cot_bf, down_work) * act_slope
    grad_pre_bf = grad_pre.astype(jnp.bfloat16)
    down_part = transposed_times(act_bf, cot_bf).astype(jnp.bfloat16)
    up_part = transposed_times(hidden_two, grad_pre_bf).astype(jnp.bfloat16)

    out_partial = jnp.dot(
        attended_bf, proj_work, preferred_element_type=jnp.float32
    ) + jnp.dot(act_bf, down_work, preferred_element_type=jnp.float32)
    block_out = (
        tokens + sum_halves(out_partial, member, local_rows) + vec_work[6] + vec_work[7]
    )
    rows_two, ln2_gain_part, ln2_bias_part = norm_back(
        sum_halves(times_transposed(grad_pre_bf, up_work), member, local_rows),
        unit,
        inverse,
        vec_work[2],
    )
    cot_sum = jnp.sum(out_grad, axis=0)
    grad_att_late, down_part, up_part = lax.optimization_barrier(
        (grad_att_bf, down_part, up_part)
    )
    grad_query, grad_key, grad_value, q_bias_part, v_bias_part = attend_back(
        query_bf, key_bf, value_bf, grad_att_late, attended, log_totals, tables, segment_row
    )
    q_bias_part, v_bias_part = q_bias_part[0], v_bias_part[0]
    grad_mixed_bf = jnp.concatenate([grad_query, grad_key, grad_value], axis=1)
    qkv_part = transposed_times(hidden_one, grad_mixed_bf).astype(jnp.bfloat16)
    rows_one, ln1_gain_part, ln1_bias_part = norm_back(
        sum_halves(times_transposed(grad_mixed_bf, qkv_work), member, local_rows),
        unit,
        inverse,
        vec_work[0],
    )
    tokens_grad = out_grad + rows_one + rows_two
    vec_part = jnp.concatenate(
        [
            jnp.stack(
                [
                    ln1_gain_part,
                    ln1_bias_part,
                    ln2_gain_part,
                    ln2_bias_part,
                    spread(q_bias_part, LANES, member),
                    spread(v_bias_part, LANES, member),
                    cot_sum,
                    cot_sum,
                ]
            ),
            spread(jnp.sum(grad_pre, axis=0), LANES, member).reshape(FF // D, D),
            jnp.zeros((16 - VROWS, D), jnp.float32),
        ],
        axis=0,
    )
    down_grad, up_grad, proj_grad, qkv_grad, vec_sum, square = reduce_all(
        groups, down_part, up_part, proj_part, qkv_part, vec_part
    )
    vectors_grad = lax.dynamic_slice_in_dim(
        vec_sum[:VROWS], (group * 2 + member) * vec_width, vec_width, axis=1
    )
    grads, weights_new, moments_new = adam_all(
        square,
        (qkv_weight, proj_weight, up_weight, down_weight, vectors),
        (qkv_moments, proj_moments, up_moments, down_moments, vector_moments),
        (qkv_grad, proj_grad, up_grad, down_grad, vectors_grad),
    )
    return (block_out, tokens_grad, *grads, *weights_new, *moments_new)


def solution(mesh):
    placed = (
        P(("dp", "shard"), None),
        P(("dp", "shard"), None),
        P("dp", None),
        P("dp", "shard"),
        P("dp", "shard"),
        P("dp", "shard"),
        P("dp", "shard"),
        P(None, ("dp", "shard")),
        P(None, "dp", "shard"),
        P(None, "dp", "shard"),
        P(None, "dp", "shard"),
        P(None, "dp", "shard"),
        P(None, None, ("dp", "shard")),
    )
    return jax.shard_map(
        shards,
        mesh=mesh,
        in_specs=placed,
        out_specs=(
            P(("dp", "shard"), None),
            P(("dp", "shard"), None),
            P("dp", "shard"),
            P("dp", "shard"),
            P("dp", "shard"),
            P("dp", "shard"),
            P(None, ("dp", "shard")),
            P("dp", "shard"),
            P("dp", "shard"),
            P("dp", "shard"),
            P("dp", "shard"),
            P(None, ("dp", "shard")),
            P(None, "dp", "shard"),
            P(None, "dp", "shard"),
            P(None, "dp", "shard"),
            P(None, "dp", "shard"),
            P(None, None, ("dp", "shard")),
        ),
        check_vma=False,
    )
```

```python
import math

import jax
import jax.numpy as jnp
from jax import lax
from jax.experimental import pallas as pl
from jax.experimental.pallas import tpu as pltpu
from jax.sharding import PartitionSpec as P

D = 1024
FF = 4096
HD = 64
ROT = 16
STEP = 4
VROWS = 12
NPARAM = 12595200


ln_eps = 1e-05
beta_one = 0.9
beta_two = 0.95
learn_rate = 0.005
decay_rate = 0.01
adam_eps = 1e-08
rope_base = 10000.0


def norm_rows(inputs, gain_row, bias_row):
    center = inputs - jnp.mean(inputs, axis=-1, keepdims=True)
    inverse = lax.rsqrt(jnp.mean(center * center, axis=-1, keepdims=True) + ln_eps)
    unit_rows = center * inverse
    return (unit_rows * gain_row + bias_row, unit_rows, inverse)


def norm_back(upstream, unit_rows, inverse, gain_row):
    gain_grad = jnp.sum(upstream * unit_rows, axis=0)
    bias_grad = jnp.sum(upstream, axis=0)
    scaled_up = upstream * gain_row
    mean_plain = jnp.mean(scaled_up, axis=-1, keepdims=True)
    mean_unit = jnp.mean(scaled_up * unit_rows, axis=-1, keepdims=True)
    return (inverse * (scaled_up - mean_plain - unit_rows * mean_unit), gain_grad, bias_grad)


def doc_positions(segment_row):
    length_all = segment_row.shape[0]
    indices = jnp.arange(length_all, dtype=jnp.int32)
    starting = jnp.concatenate(
        [jnp.ones((1,), dtype=jnp.bool_), segment_row[1:] != segment_row[:-1]]
    )
    begins = lax.cummax(jnp.where(starting, indices, 0), axis=0)
    return indices - begins


def rotary_tables(positions, rot_dims):
    half_dims = rot_dims // 2
    exponent = jnp.arange(half_dims, dtype=jnp.float32) * (2.0 / rot_dims)
    inverse_freq = jnp.exp(-math.log(rope_base) * exponent)
    angles = positions.astype(jnp.float32)[:, None] * inverse_freq[None, :]
    return (jnp.cos(angles)[:, None, :], jnp.sin(angles)[:, None, :])


def rotate(head_rows, cosine_table, sine_table):
    half_dims = cosine_table.shape[-1]
    lower_half = head_rows[..., :half_dims]
    upper_half = head_rows[..., half_dims : 2 * half_dims]
    return jnp.concatenate(
        [
            lower_half * cosine_table - upper_half * sine_table,
            upper_half * cosine_table + lower_half * sine_table,
            head_rows[..., 2 * half_dims :],
        ],
        axis=-1,
    )


def gelu_pair(pre_act):
    normal_cdf = 0.5 * (1.0 + lax.erf(pre_act * (1.0 / math.sqrt(2.0))))
    density = jnp.exp(-0.5 * pre_act * pre_act) * (1.0 / math.sqrt(2.0 * math.pi))
    return (pre_act * normal_cdf, normal_cdf + pre_act * density)


def times_transposed(left, right):
    return lax.dot_general(
        left, right, (((1,), (1,)), ((), ())), preferred_element_type=jnp.float32
    )


def transposed_times(left, right):
    return lax.dot_general(
        left, right, (((0,), (0,)), ((), ())), preferred_element_type=jnp.float32
    )


def adam_update(weight, moments, gradient, clip_factor):
    clipped = gradient * clip_factor
    first_new = beta_one * moments[0] + (1.0 - beta_one) * clipped
    second_new = beta_two * moments[1] + (1.0 - beta_two) * clipped * clipped
    fix_first = 1.0 - math.pow(beta_one, STEP)
    fix_second = 1.0 - math.pow(beta_two, STEP)
    direction = first_new / fix_first / (jnp.sqrt(second_new / fix_second) + adam_eps)
    return (
        weight - learn_rate * (direction + decay_rate * weight),
        jnp.stack([first_new, second_new]),
    )


def plain_shards(
    tokens,
    out_grad,
    segment_ids,
    qkv_weight,
    proj_weight,
    up_weight,
    down_weight,
    vectors,
    qkv_moments,
    proj_moments,
    up_moments,
    down_moments,
    vector_moments,
):
    columns_full = (
        lax.all_gather(qkv_weight.astype(jnp.bfloat16), "shard", axis=1, tiled=True),
        lax.all_gather(proj_weight.astype(jnp.bfloat16), "shard", axis=1, tiled=True),
        lax.all_gather(up_weight.astype(jnp.bfloat16), "shard", axis=1, tiled=True),
        lax.all_gather(down_weight.astype(jnp.bfloat16), "shard", axis=1, tiled=True),
        lax.all_gather(vectors.astype(jnp.bfloat16), "shard", axis=1, tiled=True),
    )
    qkv_work, proj_work, up_work, down_work, vec_bf = (
        lax.all_gather(columns_full[0], "dp", axis=0, tiled=True),
        lax.all_gather(columns_full[1], "dp", axis=0, tiled=True),
        lax.all_gather(columns_full[2], "dp", axis=0, tiled=True),
        lax.all_gather(columns_full[3], "dp", axis=0, tiled=True),
        lax.all_gather(columns_full[4], "dp", axis=1, tiled=True),
    )
    vec_work = vec_bf.astype(jnp.float32)
    head_count = D // HD
    score_scale = 1.0 / math.sqrt(HD)
    local_rows = tokens.shape[0]
    segment_row = segment_ids[0]
    length_all = segment_row.shape[0]
    row_start = lax.axis_index("shard") * local_rows
    query_index = row_start + jnp.arange(local_rows, dtype=jnp.int32)
    query_segment = lax.dynamic_slice_in_dim(segment_row, row_start, local_rows)
    positions = lax.dynamic_slice_in_dim(doc_positions(segment_row), row_start, local_rows)
    normed_one, unit_one, inverse_one = norm_rows(tokens, vec_work[0], vec_work[1])
    hidden_one = normed_one.astype(jnp.bfloat16)
    mixed_rows = jnp.dot(hidden_one, qkv_work, preferred_element_type=jnp.float32)
    query_raw = (mixed_rows[:, :D] + vec_work[4]).reshape(local_rows, head_count, HD)
    key_raw = mixed_rows[:, D : 2 * D].reshape(local_rows, head_count, HD)
    value_bf = (mixed_rows[:, 2 * D :] + vec_work[5]).astype(jnp.bfloat16)
    cosine_table, sine_table = rotary_tables(positions, ROT)
    query_bf = rotate(query_raw, cosine_table, sine_table).astype(jnp.bfloat16)
    key_bf = rotate(key_raw, cosine_table, sine_table).astype(jnp.bfloat16).reshape(local_rows, D)
    key_piece = lax.all_gather(key_bf, "shard", axis=0, tiled=True)
    value_piece = lax.all_gather(value_bf, "shard", axis=0, tiled=True)
    piece_rows = key_piece.shape[0]
    key_heads = key_piece.reshape(piece_rows, head_count, HD)
    value_heads = value_piece.reshape(piece_rows, head_count, HD)
    key_index = jnp.arange(piece_rows, dtype=jnp.int32)
    allowed = (segment_row[None, :] == query_segment[:, None]) & (
        key_index[None, :] <= query_index[:, None]
    )
    scores = (
        jnp.einsum("qhd,khd->hqk", query_bf, key_heads, preferred_element_type=jnp.float32)
        * score_scale
    )
    exp_scores = jnp.where(allowed[None], jnp.exp(scores), 0.0)
    numerator = jnp.einsum(
        "hqk,khd->qhd",
        exp_scores.astype(jnp.bfloat16),
        value_heads,
        preferred_element_type=jnp.float32,
    )
    numerator, totals = (numerator, jnp.sum(exp_scores, axis=-1))
    attended = numerator / jnp.transpose(totals)[:, :, None]
    log_totals = jnp.log(totals)
    attended_bf = attended.reshape(local_rows, D).astype(jnp.bfloat16)
    proj_out = jnp.dot(attended_bf, proj_work, preferred_element_type=jnp.float32) + vec_work[6]
    normed_two, unit_two, inverse_two = norm_rows(tokens, vec_work[2], vec_work[3])
    hidden_two = normed_two.astype(jnp.bfloat16)
    pre_act = jnp.dot(hidden_two, up_work, preferred_element_type=jnp.float32) + vec_work[
        8:
    ].reshape(FF)
    act_values, act_slope = gelu_pair(pre_act)
    act_bf = act_values.astype(jnp.bfloat16)
    block_out = (
        tokens
        + proj_out
        + (jnp.dot(act_bf, down_work, preferred_element_type=jnp.float32) + vec_work[7])
    )
    cot_bf = out_grad.astype(jnp.bfloat16)
    down_part = transposed_times(act_bf, cot_bf)
    proj_part = transposed_times(attended_bf, cot_bf)
    cot_sum = jnp.sum(out_grad, axis=0)
    grad_pre = times_transposed(cot_bf, down_work) * act_slope
    grad_pre_bf = grad_pre.astype(jnp.bfloat16)
    up_part = transposed_times(hidden_two, grad_pre_bf)
    rows_two, ln2_gain_part, ln2_bias_part = norm_back(
        times_transposed(grad_pre_bf, up_work), unit_two, inverse_two, vec_work[2]
    )
    grad_att_bf = (
        times_transposed(cot_bf, proj_work).astype(jnp.bfloat16).reshape(local_rows, head_count, HD)
    )
    keys_all, values_all = (
        lax.all_gather(key_bf, "shard", axis=0, tiled=True),
        lax.all_gather(value_bf, "shard", axis=0, tiled=True),
    )
    key_heads = keys_all.reshape(length_all, head_count, HD)
    value_heads = values_all.reshape(length_all, head_count, HD)
    key_index = jnp.arange(length_all, dtype=jnp.int32)
    allowed = (segment_row[None, :] == query_segment[:, None]) & (
        key_index[None, :] <= query_index[:, None]
    )
    scores = (
        jnp.einsum("qhd,khd->hqk", query_bf, key_heads, preferred_element_type=jnp.float32)
        * score_scale
    )
    probability = jnp.where(allowed[None], jnp.exp(scores - log_totals[:, :, None]), 0.0)
    grad_prob = jnp.einsum(
        "qhd,khd->hqk", grad_att_bf, value_heads, preferred_element_type=jnp.float32
    )
    row_delta = jnp.transpose(jnp.sum(grad_att_bf.astype(jnp.float32) * attended, axis=-1))
    grad_score = (probability * (grad_prob - row_delta[:, :, None]) * score_scale).astype(
        jnp.bfloat16
    )
    grad_query = jnp.einsum(
        "hqk,khd->qhd", grad_score, key_heads, preferred_element_type=jnp.float32
    )
    grad_query = rotate(grad_query, cosine_table, -sine_table).reshape(local_rows, D)
    key_terms = jnp.einsum(
        "hqk,qhd->khd", grad_score, query_bf, preferred_element_type=jnp.float32
    ).reshape(length_all, D)
    value_terms = jnp.einsum(
        "hqk,qhd->khd",
        probability.astype(jnp.bfloat16),
        grad_att_bf,
        preferred_element_type=jnp.float32,
    ).reshape(length_all, D)
    key_value_grad = lax.psum_scatter(
        jnp.concatenate([key_terms, value_terms], axis=1), "shard", scatter_dimension=0, tiled=True
    )
    grad_key = rotate(
        key_value_grad[:, :D].reshape(local_rows, head_count, HD), cosine_table, -sine_table
    ).reshape(local_rows, D)
    grad_value = key_value_grad[:, D:]
    grad_mixed_bf = jnp.concatenate([grad_query, grad_key, grad_value], axis=1).astype(jnp.bfloat16)
    qkv_part = transposed_times(hidden_one, grad_mixed_bf)
    rows_one, ln1_gain_part, ln1_bias_part = norm_back(
        times_transposed(grad_mixed_bf, qkv_work), unit_one, inverse_one, vec_work[0]
    )
    tokens_grad = out_grad + rows_one + rows_two
    vec_part = jnp.concatenate(
        [
            jnp.stack(
                [
                    ln1_gain_part,
                    ln1_bias_part,
                    ln2_gain_part,
                    ln2_bias_part,
                    jnp.sum(grad_query, axis=0),
                    jnp.sum(grad_value, axis=0),
                    cot_sum,
                    cot_sum,
                ]
            ),
            jnp.sum(grad_pre, axis=0).reshape(FF // D, D),
        ],
        axis=0,
    )
    groups = lax.axis_size("dp")
    members = lax.axis_size("shard")
    owners = groups * members
    vec_split = vec_part.reshape(VROWS, groups, members, D // owners)
    group_sums = (
        lax.psum_scatter(qkv_part, "shard", scatter_dimension=1, tiled=True),
        lax.psum_scatter(proj_part, "shard", scatter_dimension=1, tiled=True),
        lax.psum_scatter(up_part, "shard", scatter_dimension=1, tiled=True),
        lax.psum_scatter(down_part, "shard", scatter_dimension=1, tiled=True),
        lax.psum_scatter(vec_split, "shard", scatter_dimension=2, tiled=True),
    )
    owner_sums = (
        lax.psum_scatter(group_sums[0], "dp", scatter_dimension=0, tiled=True),
        lax.psum_scatter(group_sums[1], "dp", scatter_dimension=0, tiled=True),
        lax.psum_scatter(group_sums[2], "dp", scatter_dimension=0, tiled=True),
        lax.psum_scatter(group_sums[3], "dp", scatter_dimension=0, tiled=True),
        lax.psum_scatter(group_sums[4], "dp", scatter_dimension=1, tiled=True),
    )
    qkv_grad = owner_sums[0]
    proj_grad = owner_sums[1]
    up_grad = owner_sums[2]
    down_grad = owner_sums[3]
    vectors_grad = owner_sums[4].reshape(VROWS, D // owners)
    local_square = (
        jnp.sum(qkv_grad * qkv_grad)
        + jnp.sum(proj_grad * proj_grad)
        + jnp.sum(up_grad * up_grad)
        + jnp.sum(down_grad * down_grad)
        + jnp.sum(vectors_grad * vectors_grad)
    )
    square_total = lax.psum(local_square, ("dp", "shard"))
    norm_limit = math.sqrt(NPARAM)
    clip_factor = norm_limit / jnp.maximum(jnp.sqrt(square_total), norm_limit)
    qkv_new, qkv_moments_new = adam_update(qkv_weight, qkv_moments, qkv_grad, clip_factor)
    proj_new, proj_moments_new = adam_update(proj_weight, proj_moments, proj_grad, clip_factor)
    up_new, up_moments_new = adam_update(up_weight, up_moments, up_grad, clip_factor)
    down_new, down_moments_new = adam_update(down_weight, down_moments, down_grad, clip_factor)
    vectors_new, vector_moments_new = adam_update(
        vectors, vector_moments, vectors_grad, clip_factor
    )
    return (
        block_out,
        tokens_grad,
        qkv_grad,
        proj_grad,
        up_grad,
        down_grad,
        vectors_grad,
        qkv_new,
        proj_new,
        up_new,
        down_new,
        vectors_new,
        qkv_moments_new,
        proj_moments_new,
        up_moments_new,
        down_moments_new,
        vector_moments_new,
    )

MESH = pl.DeviceIdType.MESH
LANES = 128


def place(groups):
    group = lax.axis_index("dp")
    depth = groups // 4
    return depth, group // 4, lax.rem(group // 2, 2), lax.rem(group, 2), lax.axis_index("shard")


def device(z, y, c, x):
    return (z * 4 + y * 2 + c, x)


def greet(peers):
    barrier = pltpu.get_barrier_semaphore()
    for peer in peers:
        pl.semaphore_signal(barrier, inc=1, device_id=peer, device_id_type=MESH)
    pl.semaphore_wait(barrier, len(peers))


def half_lanes(member, width):
    return pl.ds(pl.multiple_of(member * width, LANES), width)


def gather_kernel(
    groups,
    tokens_in, vec_in, qkv_in, proj_in, up_in, down_in,
    vec_out, qkv_out, proj_out, up_out, down_out, rows_out, unit_out, inverse_out,
    vec_piece, qkv_keep, qkv_send, proj_piece, up_keep, up_send, down_keep, down_send, unit_piece,
    send_sem, recv_sem, swap_send, swap_recv, local_sem,
):
    depth, z, y, c, x = place(groups)
    kind = jnp.bfloat16
    across = device(z, y, c, 1 - x)
    beside = device(z, 1 - y, c, x)
    twin = device(z, y, 1 - c, x)
    corner = device(z, x, c, y)
    far = [lax.rem(z + k, depth) for k in range(1, depth)]
    back = [lax.rem(z + depth - k, depth) for k in range(depth)]
    greet(
        [across, beside, twin, device(z, 1 - y, c, 1 - x)] + [device(zz, y, c, x) for zz in far]
    )

    def remote(src, dst, index, peer, sems=(send_sem, recv_sem)):
        return pltpu.make_async_remote_copy(
            src_ref=src, dst_ref=dst, send_sem=sems[0].at[index], recv_sem=sems[1].at[index],
            device_id=peer, device_id_type=MESH,
        )

    def block(item, zz, yy, cc):
        if item == "vec":
            return vec_out.at[zz, yy, cc]
        if item == "proj":
            return proj_out.at[zz, cc, :, half_lanes(yy, proj_out.shape[3] // 2)]
        size = qkv_out.shape[3] // 2
        return qkv_out.at[zz, yy, cc, pl.ds(item * size, size)]

    def split(source, keep, sent):
        for b in range(keep.shape[1] // LANES):
            lanes = slice(b * LANES, (b + 1) * LANES)
            keep[:, lanes] = source[:, half_lanes(2 * b + x, LANES)].astype(kind)
            sent[:, lanes] = source[:, half_lanes(2 * b + 1 - x, LANES)].astype(kind)

    swap_sems = (swap_send, swap_recv)
    swaps, stays = [], []

    def swap(keep, sent, target):
        index = len(swaps)
        swaps.append(remote(sent, target, index, across, swap_sems))
        stays.append(pltpu.make_async_copy(keep, target, local_sem.at[index]))
        swaps[-1].start()
        stays[-1].start()

    split(qkv_in, qkv_keep, qkv_send)
    swap(qkv_keep, qkv_send, qkv_out.at[z, y, c, :, half_lanes(x, qkv_keep.shape[1])])
    vec_piece[...] = jnp.zeros_like(vec_piece)
    vec_piece[: vec_in.shape[0], : vec_in.shape[1]] = vec_in[...].astype(kind)
    swap(vec_piece, vec_piece, vec_out.at[z, y, c, x])
    proj_piece[...] = proj_in[...].astype(kind)
    proj_move = remote(
        proj_piece, proj_out.at[z, c, :, half_lanes(x, proj_out.shape[3] // 2)], 5, corner,
        swap_sems,
    )
    proj_stay = pltpu.make_async_copy(proj_piece, block("proj", z, y, c), local_sem.at[5])
    pl.when(x != y)(lambda: proj_move.start())
    pl.when(x == y)(lambda: proj_stay.start())

    @pl.loop(0, tokens_in.shape[0] // 64)
    def _(step):
        part = pl.ds(pl.multiple_of(step * 64, 64), 64)
        rows = tokens_in[part, :]
        center = rows - jnp.mean(rows, axis=-1, keepdims=True)
        inverse = lax.rsqrt(jnp.mean(center * center, axis=-1, keepdims=True) + ln_eps)
        unit = center * inverse
        unit_out[part, :] = unit
        inverse_out[part, :] = inverse
        unit_piece[part, :] = unit.astype(kind)

    items = ("vec", 0, 1, "proj")
    along, over, pair = {}, {}, {}

    def launch(a, item):
        mine = block(item, z, y, c)
        for k in range(1, depth):
            along[item, k] = remote(mine, mine, (a, k), device(far[k - 1], y, c, x))
            along[item, k].start()
        over[item, 0] = remote(mine, mine, (a, depth), beside)
        over[item, 0].start()
        pair[item, 0, 0] = remote(mine, mine, (a, 2 * depth), twin)
        pair[item, 0, 0].start()

    for index in range(2):
        stays[index].wait()
        swaps[index].wait()
    for a in range(3):
        launch(a, items[a])
    swap(unit_piece, unit_piece, rows_out.at[x])
    split(up_in, up_keep, up_send)
    swap(up_keep, up_send, up_out.at[:, half_lanes(x, up_keep.shape[1])])
    size = down_in.shape[0] // 2
    down_keep[...] = down_in[pl.ds(pl.multiple_of(x * size, 16), size), :].astype(kind)
    down_send[...] = down_in[pl.ds(pl.multiple_of((1 - x) * size, 16), size), :].astype(kind)
    swap(down_keep, down_send, down_out.at[:, half_lanes(x, down_keep.shape[1])])
    pl.when(x != y)(lambda: proj_move.wait())
    pl.when(x == y)(lambda: proj_stay.wait())
    launch(3, "proj")
    for a, item in enumerate(items):
        for k in range(1, depth):
            along[item, k].wait_recv()
            come = block(item, back[k], y, c)
            over[item, k] = remote(come, come, (a, depth + k), beside)
            over[item, k].start()
            pair[item, 0, k] = remote(come, come, (a, 2 * depth + k), twin)
            pair[item, 0, k].start()
    for a, item in enumerate(items):
        for k in range(depth):
            over[item, k].wait_recv()
            come = block(item, back[k], 1 - y, c)
            pair[item, 1, k] = remote(come, come, (a, 3 * depth + k), twin)
            pair[item, 1, k].start()
    for index in range(2, 5):
        stays[index].wait()
        swaps[index].wait()
    for item in items:
        for side in range(2):
            for k in range(depth):
                pair[item, side, k].wait()
        for k in range(depth):
            over[item, k].wait_send()
        for k in range(1, depth):
            along[item, k].wait_send()


def gather_first(groups, tokens, vectors, qkv, proj, up, down):
    depth = groups // 4
    kind, wide = jnp.bfloat16, jnp.float32
    local_rows, width = tokens.shape

    def halves(rows, columns):
        return [pltpu.VMEM((rows, columns), kind)] * 2

    shapes = [
        jax.ShapeDtypeStruct((depth, 2, 2, 2, 16, LANES), kind),
        jax.ShapeDtypeStruct((depth, 2, 2) + qkv.shape, kind),
        jax.ShapeDtypeStruct((depth, 2, proj.shape[0], 2 * proj.shape[1]), kind),
        jax.ShapeDtypeStruct(up.shape, kind),
        jax.ShapeDtypeStruct((down.shape[0] // 2, 2 * down.shape[1]), kind),
        jax.ShapeDtypeStruct((2, local_rows, width), kind),
        jax.ShapeDtypeStruct((local_rows, width), wide),
        jax.ShapeDtypeStruct((local_rows, 1), wide),
    ]
    vmem = pl.BlockSpec(memory_space=pltpu.VMEM)
    hbm = pl.BlockSpec(memory_space=pl.ANY)
    return pl.pallas_call(
        lambda *refs: gather_kernel(groups, *refs),
        in_specs=[vmem] * 6,
        out_specs=[hbm] * 6 + [vmem] * 2,
        out_shape=shapes,
        scratch_shapes=[
            pltpu.VMEM((16, LANES), kind),
            *halves(qkv.shape[0], qkv.shape[1] // 2),
            pltpu.VMEM(proj.shape, kind),
            *halves(up.shape[0], up.shape[1] // 2),
            *halves(down.shape[0] // 2, down.shape[1]),
            pltpu.VMEM((local_rows, width), kind),
            pltpu.SemaphoreType.DMA((4, 4 * depth)),
            pltpu.SemaphoreType.DMA((4, 4 * depth)),
            pltpu.SemaphoreType.DMA((6,)),
            pltpu.SemaphoreType.DMA((6,)),
            pltpu.SemaphoreType.DMA((6,)),
        ],
        compiler_params=pltpu.CompilerParams(collective_id=0, has_side_effects=True),
        cost_estimate=pl.CostEstimate(
            flops=0, bytes_accessed=64 * qkv.size, transcendentals=0
        ),
        name="gather_first",
    )(tokens, vectors, qkv, proj, up, down)


def forward_pair(
    index, mixed_ref, q_bias_ref, v_bias_ref, cos_ref, down_ref, up_ref, column_ref, row_ref,
    query_held, key_held, value_held, att_held, log_held, att_out,
):
    scale = 1.0 / math.sqrt(HD)
    length = mixed_ref.shape[0]
    width = mixed_ref.shape[1] // 3
    size = length // 4
    pairs = width // LANES
    lanes_of = half_lanes(index, LANES)
    cosine, down_sine, up_sine = cos_ref[...], down_ref[...], up_ref[...]
    query_held[index] = rolled(
        mixed_ref[:, lanes_of] + q_bias_ref[:, lanes_of], cosine, down_sine, up_sine
    ).astype(jnp.bfloat16)
    key_held[index] = rolled(
        mixed_ref[:, half_lanes(pairs + index, LANES)], cosine, down_sine, up_sine
    ).astype(jnp.bfloat16)
    value_held[index] = (
        mixed_ref[:, half_lanes(2 * pairs + index, LANES)] + v_bias_ref[:, lanes_of]
    ).astype(jnp.bfloat16)
    for start in range(0, length, size):
        extent = start + size
        mask = block_mask(column_ref, row_ref, start, size, extent)
        keys, values = key_held[index, :extent, :], value_held[index, :extent, :]
        results = []
        for query in split_pair(query_held[index, start:extent, :].astype(jnp.float32)):
            scores = times_transposed(query.astype(jnp.bfloat16), keys) * scale
            exp_scores = jnp.where(mask, jnp.exp(scores), 0.0)
            totals = jnp.sum(exp_scores, axis=1, keepdims=True)
            numerator = jnp.dot(
                exp_scores.astype(jnp.bfloat16), values, preferred_element_type=jnp.float32
            )
            results.append((numerator / totals, jnp.log(totals)))
        lanes = lax.broadcasted_iota(jnp.int32, (size, 2 * HD), 1) < HD
        attended = jnp.where(lanes, results[0][0], results[1][0])
        att_held[index, start:extent, :] = attended
        att_out[start:extent, lanes_of] = attended.astype(jnp.bfloat16)
        log_held[index, start:extent, :] = jnp.where(lanes, results[0][1], results[1][1])


def backward_pair(
    index, cot_ref, proj_ref, cos_ref, down_ref, up_ref, column_ref, row_ref,
    query_held, key_held, value_held, att_held, log_held, grad_held,
    query_sum, key_sum, value_sum, mixed_out, q_bias_out, v_bias_out,
):
    scale = 1.0 / math.sqrt(HD)
    length = query_held.shape[1]
    size = length // 4
    pairs = query_held.shape[0]
    proj_rows = proj_ref[pl.ds(pl.multiple_of(index * LANES, LANES), LANES), :]
    local_rows = cot_ref.shape[1]
    for side in range(2):
        grad_held[side * local_rows : (side + 1) * local_rows, :] = times_transposed(
            cot_ref[side], proj_rows
        ).astype(jnp.bfloat16)
    key_sum[...] = jnp.zeros_like(key_sum)
    value_sum[...] = jnp.zeros_like(value_sum)
    for start in range(0, length, size):
        extent = start + size
        mask = block_mask(column_ref, row_ref, start, size, extent)
        keys, values = key_held[index, :extent, :], value_held[index, :extent, :]
        queries = split_pair(query_held[index, start:extent, :].astype(jnp.float32))
        grads = split_pair(grad_held[start:extent, :].astype(jnp.float32))
        attended = att_held[index, start:extent, :]
        pieces = []
        for head in range(2):
            query = queries[head].astype(jnp.bfloat16)
            grad = grads[head].astype(jnp.bfloat16)
            log_total = log_held[index, start:extent, head * HD : head * HD + 1]
            scores = times_transposed(query, keys) * scale
            probability = jnp.where(mask, jnp.exp(scores - log_total), 0.0)
            grad_prob = times_transposed(grad, values)
            delta = jnp.sum(grads[head] * attended, axis=1, keepdims=True)
            grad_score = (probability * (grad_prob - delta) * scale).astype(jnp.bfloat16)
            pieces.append(jnp.dot(grad_score, keys, preferred_element_type=jnp.float32))
            key_sum[:extent, :] += transposed_times(grad_score, query)
            value_sum[:extent, :] += transposed_times(probability.astype(jnp.bfloat16), grad)
        lanes = lax.broadcasted_iota(jnp.int32, (size, 2 * HD), 1) < HD
        query_sum[start:extent, :] = jnp.where(lanes, pieces[0], pieces[1])
    cosine, down_sine, up_sine = cos_ref[...], down_ref[...], up_ref[...]
    grad_query = rolled(query_sum[...], cosine, -down_sine, -up_sine)
    mixed_out[:, half_lanes(index, LANES)] = grad_query.astype(jnp.bfloat16)
    q_bias_out[:, half_lanes(index, LANES)] = jnp.sum(grad_query, axis=0, keepdims=True)
    mixed_out[:, half_lanes(pairs + index, LANES)] = rolled(
        key_sum[...], cosine, -down_sine, -up_sine
    ).astype(jnp.bfloat16)
    grad_value = value_sum[...]
    mixed_out[:, half_lanes(2 * pairs + index, LANES)] = grad_value.astype(jnp.bfloat16)
    v_bias_out[:, half_lanes(index, LANES)] = jnp.sum(grad_value, axis=0, keepdims=True)


def attention_kernel(
    groups,
    up_in, down_in, cot_in, proj_in, mixed_in, q_bias_in, v_bias_in, cos_in, low_in, high_in,
    column_in, row_in,
    up_out, down_out, cot_out, att_out, mixed_out, q_bias_out, v_bias_out,
    query_held, key_held, value_held, att_held, log_held, grad_held,
    query_sum, key_sum, value_sum,
    send_sem, recv_sem, row_send, row_recv, local_sem,
):
    depth, z, y, c, x = place(groups)
    pairs = query_held.shape[0]
    across = device(z, y, c, 1 - x)
    beside = device(z, 1 - y, c, x)
    twin = device(z, y, 1 - c, x)
    far = [lax.rem(z + k, depth) for k in range(1, depth)]
    back = [lax.rem(z + depth - k, depth) for k in range(depth)]
    greet([across, beside, twin] + [device(zz, y, c, x) for zz in far])

    def remote(src, dst, index, peer, sems=(send_sem, recv_sem)):
        return pltpu.make_async_remote_copy(
            src_ref=src, dst_ref=dst, send_sem=sems[0].at[index], recv_sem=sems[1].at[index],
            device_id=peer, device_id_type=MESH,
        )

    arrays = ((up_in, up_out), (down_in, down_out))

    def rows_of(ref, i):
        size = ref.shape[-2] // pairs
        return pl.ds(pl.multiple_of(i * size, 16), size)

    def block(a, i, zz, yy, cc):
        out = arrays[a][1]
        return out.at[zz, yy, cc, rows_of(out, i)]

    def source(a, i):
        return arrays[a][0].at[rows_of(arrays[a][0], i)]

    def along(a, i, k):
        return remote(
            source(a, i), block(a, i, z, y, c), (a, i, k), device(far[k - 1], y, c, x)
        )

    def over(a, i, k):
        src = source(a, i) if k == 0 else block(a, i, back[k], y, c)
        return remote(src, block(a, i, back[k], y, c), (a, i, depth + k), beside)

    def pair(a, i, side, k):
        come = block(a, i, back[k], 1 - y if side else y, c)
        src = source(a, i) if (side, k) == (0, 0) else come
        return remote(src, come, (a, i, (2 + side) * depth + k), twin)

    cot_swap = remote(cot_in, cot_out.at[x], 0, across, (row_send, row_recv))
    cot_swap.start()
    stays = [
        pltpu.make_async_copy(arrays[a][0], arrays[a][1].at[z, y, c], local_sem.at[a])
        for a in range(2)
    ] + [pltpu.make_async_copy(cot_in, cot_out.at[x], local_sem.at[2])]
    for stay in stays:
        stay.start()

    @pl.loop(0, pairs)
    def _(i):
        for a in range(2):
            for k in range(1, depth):
                along(a, i, k).start()
            over(a, i, 0).start()
            pair(a, i, 0, 0).start()

    def relay_along(i):
        for a in range(2):
            for k in range(1, depth):
                along(a, i, k).wait_recv()
                over(a, i, k).start()
                pair(a, i, 0, k).start()

    def relay_over(i):
        for a in range(2):
            for k in range(depth):
                over(a, i, k).wait_recv()
                pair(a, i, 1, k).start()

    @pl.loop(0, pairs)
    def _(i):
        forward_pair(
            i, mixed_in, q_bias_in, v_bias_in, cos_in, low_in, high_in, column_in, row_in,
            query_held, key_held, value_held, att_held, log_held, att_out,
        )

    relay_along(0)
    relay_along(1)
    stays[2].wait()
    cot_swap.wait()

    @pl.loop(0, pairs)
    def _(i):
        backward_pair(
            i, cot_out, proj_in, cos_in, low_in, high_in, column_in, row_in,
            query_held, key_held, value_held, att_held, log_held, grad_held,
            query_sum, key_sum, value_sum, mixed_out, q_bias_out, v_bias_out,
        )
        pl.when(i == 0)(lambda: relay_along(2))
        pl.when(i == 2)(lambda: relay_along(3))
        relay_over(i)

    for stay in stays[:2]:
        stay.wait()

    @pl.loop(0, pairs)
    def _(i):
        for a in range(2):
            for k in range(depth):
                for side in range(2):
                    pair(a, i, side, k).wait()
                over(a, i, k).wait_send()
            for k in range(1, depth):
                along(a, i, k).wait_send()


def attention_all(
    groups, up, down, cot_bf, proj_work, mixed_rows, q_bias, v_bias, tables, segment_row
):
    depth = groups // 4
    length = mixed_rows.shape[0]
    width = mixed_rows.shape[1] // 3
    pairs = width // LANES
    kind, wide = jnp.bfloat16, jnp.float32
    shapes = [
        jax.ShapeDtypeStruct((depth, 2, 2) + up.shape, kind),
        jax.ShapeDtypeStruct((depth, 2, 2) + down.shape, kind),
        jax.ShapeDtypeStruct((2,) + cot_bf.shape, kind),
        jax.ShapeDtypeStruct((length, width), kind),
        jax.ShapeDtypeStruct((length, 3 * width), kind),
        jax.ShapeDtypeStruct((1, width), wide),
        jax.ShapeDtypeStruct((1, width), wide),
    ]
    held = (pairs, length, LANES)
    vmem = pl.BlockSpec(memory_space=pltpu.VMEM)
    hbm = pl.BlockSpec(memory_space=pl.ANY)
    flops = 14 * length * length * width
    return pl.pallas_call(
        lambda *refs: attention_kernel(groups, *refs),
        in_specs=[vmem] * 12,
        out_specs=[hbm] * 2 + [vmem] * 5,
        out_shape=shapes,
        scratch_shapes=[pltpu.VMEM(held, kind)] * 3
        + [pltpu.VMEM(held, wide)] * 2
        + [pltpu.VMEM((length, LANES), kind)]
        + [pltpu.VMEM((length, LANES), wide)] * 3
        + [
            pltpu.SemaphoreType.DMA((2, pairs, 4 * depth)),
            pltpu.SemaphoreType.DMA((2, pairs, 4 * depth)),
            pltpu.SemaphoreType.DMA((1,)),
            pltpu.SemaphoreType.DMA((1,)),
            pltpu.SemaphoreType.DMA((3,)),
        ],
        compiler_params=pltpu.CompilerParams(
            collective_id=2, has_side_effects=True, vmem_limit_bytes=56 * 1024 * 1024
        ),
        cost_estimate=pl.CostEstimate(
            flops=flops, bytes_accessed=48 * length * width, transcendentals=length * length * 8
        ),
        name="attention_all",
    )(up, down, cot_bf, proj_work, mixed_rows, q_bias[None], v_bias[None], *tables,
      segment_row[:, None], segment_row[None, :])


def square_sum(values):
    return jnp.sum(jnp.sum(values * values, axis=1, keepdims=True), axis=0, keepdims=True)


def reduce_kernel(
    groups,
    down_in, up_in, proj_in, qkv_in, vec_in, rows_in, rows_sent, unit_in, inverse_in, gain_in,
    down_out, up_out, proj_out, qkv_out, vec_out, square_out, rows_out,
    down_own, down_one, down_mid, down_two, down_cross, down_last, down_three, down_end, down_swap,
    up_own, up_one, up_mid, up_two, up_cross, up_last, up_three, up_end, up_swap,
    proj_own, proj_one, proj_mid, proj_two, proj_cross, proj_last, proj_three, proj_end, proj_swap,
    qkv_own, qkv_one, qkv_mid, qkv_two, qkv_cross, qkv_last, qkv_three, qkv_end, qkv_swap,
    vec_held, vec_come, tile_held, tile_come,
    rows_come, vec_sum,
    send_sem, recv_sem, vec_send, vec_recv, row_send, row_recv, local_sem,
):
    depth, z, y, c, x = place(groups)
    names = ("down", "up", "qkv", "proj")
    parts = dict(down=down_in, up=up_in, proj=proj_in, qkv=qkv_in)
    own = dict(down=down_own, up=up_own, proj=proj_own, qkv=qkv_own)
    one = dict(down=down_one, up=up_one, proj=proj_one, qkv=qkv_one)
    mid = dict(down=down_mid, up=up_mid, proj=proj_mid, qkv=qkv_mid)
    two = dict(down=down_two, up=up_two, proj=proj_two, qkv=qkv_two)
    cross = dict(down=down_cross, up=up_cross, proj=proj_cross, qkv=qkv_cross)
    last = dict(down=down_last, up=up_last, proj=proj_last, qkv=qkv_last)
    three = dict(down=down_three, up=up_three, proj=proj_three, qkv=qkv_three)
    end = dict(down=down_end, up=up_end, proj=proj_end, qkv=qkv_end)
    swap = dict(down=down_swap, up=up_swap, proj=proj_swap, qkv=qkv_swap)
    across = device(z, y, c, 1 - x)
    beside = device(z, 1 - y, c, x)
    twin = device(z, y, 1 - c, x)
    corner = device(z, x, c, y)
    far = [lax.rem(z + k, depth) for k in range(1, depth)]
    alongs = [device(zz, y, c, x) for zz in far]
    near = [
        device(z, yy, cc, xx)
        for xx in (x, 1 - x) for yy in (y, 1 - y) for cc in (c, 1 - c)
    ][1:]
    greet(near + alongs)

    def remote(src, dst, index, peer, sems=(send_sem, recv_sem)):
        return pltpu.make_async_remote_copy(
            src_ref=src, dst_ref=dst, send_sem=sems[0].at[index], recv_sem=sems[1].at[index],
            device_id=peer, device_id_type=MESH,
        )

    def wide(values):
        return values.astype(jnp.float32)

    vec_sems = (vec_send, vec_recv)
    vec_copies = []
    first, stays = {}, {}
    for a, name in enumerate(names):
        part = parts[name]
        theirs = part.at[:, 1 - c] if name == "proj" else part.at[:, :, 1 - c]
        mine = part.at[:, c] if name == "proj" else part.at[:, :, c]
        first[name] = remote(theirs, one[name], (a, 0), twin)
        first[name].start()
        stays[name] = pltpu.make_async_copy(mine, own[name], local_sem.at[a])
        stays[name].start()

    rows_swap = remote(rows_sent, rows_come, 0, across, (row_send, row_recv))
    rows_swap.start()
    second, third, fourth = {}, {}, {}

    def rows_back():
        rows_swap.wait()
        vec_sum[...] = vec_in[...]
        gain = gain_in[...]

        @pl.loop(0, rows_in.shape[0] // 64)
        def _(step):
            part = pl.ds(pl.multiple_of(step * 64, 64), 64)
            upstream = rows_in[part, :] + wide(rows_come[part, :])
            unit = unit_in[part, :]
            scaled = upstream * gain
            mean_plain = jnp.mean(scaled, axis=-1, keepdims=True)
            mean_unit = jnp.mean(scaled * unit, axis=-1, keepdims=True)
            rows_out[part, :] = inverse_in[part, :] * (scaled - mean_plain - unit * mean_unit)
            vec_sum[0:1, :] += jnp.sum(upstream * unit, axis=0, keepdims=True)
            vec_sum[1:2, :] += jnp.sum(upstream, axis=0, keepdims=True)

        vec_copies.append(remote(vec_sum, vec_come.at[0], 0, twin, vec_sems))
        vec_copies[0].start()

    def step_one(a, name):
        first[name].wait()
        stays[name].wait()

        def body(zz, carry):
            if name == "proj":
                half = own[name].shape[2] // 2
                ours, theirs = half_lanes(y, half), half_lanes(1 - y, half)
                cross[name][zz] = (
                    wide(own[name][zz, :, theirs]) + wide(one[name][zz, :, theirs])
                ).astype(jnp.bfloat16)
                mid[name][zz] = wide(own[name][zz, :, ours]) + wide(one[name][zz, :, ours])
            else:
                cross[name][zz] = (
                    wide(own[name][zz, 1 - y]) + wide(one[name][zz, 1 - y])
                ).astype(jnp.bfloat16)
                mid[name][zz] = wide(own[name][zz, y]) + wide(one[name][zz, y])
            return carry

        lax.fori_loop(0, depth, body, 0)
        second[name] = remote(cross[name], two[name], (a, 1), beside)
        second[name].start()

    def step_two(a, name):
        second[name].wait()
        for k in range(1, depth):
            zz = far[k - 1]
            last[name][k - 1] = (mid[name][zz] + wide(two[name][zz])).astype(jnp.bfloat16)
            third[name, k] = remote(
                last[name].at[k - 1], three[name].at[k - 1], (a, 1 + k), alongs[k - 1]
            )
            third[name, k].start()

    def moved(name):
        return name != "proj"

    def step_three(a, name):
        for k in range(1, depth):
            third[name, k].wait()
        total = mid[name][z] + wide(two[name][z])
        for k in range(1, depth):
            total = total + wide(three[name][k - 1])
        mid[name][0] = total
        if name == "proj":
            end[name][...] = total.astype(jnp.bfloat16)
            fourth[name] = remote(end[name], swap[name], (a, depth + 1), corner)
            pl.when(x != y)(lambda: fourth[name].start())
        else:
            half = total.shape[1] // 2
            end[name][...] = mid[name][0, :, half_lanes(1 - x, half)].astype(jnp.bfloat16)
            fourth[name] = remote(end[name], swap[name], (a, depth + 1), across)
            fourth[name].start()

    def step_four(a, name):
        if name == "proj":
            def swapped():
                fourth[name].wait()
                proj_out[...] = wide(swap[name][...])

            def kept():
                proj_out[...] = mid[name][0]

            pl.when(x != y)(swapped)
            pl.when(x == y)(kept)
            return square_sum(proj_out[...])
        fourth[name].wait()
        half = swap[name].shape[1]
        mine = mid[name][0, :, half_lanes(x, half)]
        theirs = wide(swap[name][...])
        if name == "down":
            size = mine.shape[0]
            down_out[pl.ds(pl.multiple_of(x * size, 8), size), :] = mine
            down_out[pl.ds(pl.multiple_of((1 - x) * size, 8), size), :] = theirs
        else:
            out = dict(up=up_out, qkv=qkv_out)[name]
            for b in range(half // LANES):
                lanes = slice(b * LANES, (b + 1) * LANES)
                out[:, half_lanes(2 * b + x, LANES)] = mine[:, lanes]
                out[:, half_lanes(2 * b + 1 - x, LANES)] = theirs[:, lanes]
        return square_sum(mine) + square_sum(theirs)

    def vec_step(index, peers):
        for copy in vec_copies:
            copy.wait()
        vec_copies.clear()
        held = vec_sum[...] if index == 0 else vec_held[index - 1]
        come = (0,) if index == 0 else (index,)
        vec_held[index] = held + vec_come[come[0]]
        for k, peer in enumerate(peers):
            copy = remote(
                vec_held.at[index], vec_come.at[index + 1 + k], index + 1 + k, peer, vec_sems
            )
            copy.start()
            vec_copies.append(copy)

    step_one(0, "down")
    step_one(1, "up")
    step_one(2, "qkv")
    step_one(3, "proj")
    step_two(0, "down")
    rows_back()
    step_two(1, "up")
    vec_step(0, [across])
    step_three(0, "down")
    vec_step(1, [beside])
    squares = step_four(0, "down")
    vec_step(2, alongs)
    step_two(2, "qkv")
    step_three(1, "up")
    step_two(3, "proj")
    squares = squares + step_four(1, "up")
    for copy in vec_copies:
        copy.wait()
    vec_total = vec_held[2]
    for k in range(depth - 1):
        vec_total = vec_total + vec_come[3 + k]
    vec_out[...] = vec_total
    step_three(2, "qkv")
    step_three(3, "proj")
    squares = squares + step_four(2, "qkv")
    squares = squares + step_four(3, "proj")

    base = 3 + depth
    tile_held[0] = jnp.broadcast_to(squares, tile_held.shape[1:])
    copies = [
        remote(tile_held.at[0], tile_come.at[k], base + k, peer, vec_sems)
        for k, peer in enumerate(alongs)
    ]
    for copy in copies:
        copy.start()
    for copy in copies:
        copy.wait()
    tile = tile_held[0]
    for k in range(depth - 1):
        tile = tile + tile_come[k]
    tile_held[1] = tile
    copies = [
        remote(tile_held.at[1], tile_come.at[depth - 1 + k], base + depth - 1 + k, peer, vec_sems)
        for k, peer in enumerate(near)
    ]
    for copy in copies:
        copy.start()
    for copy in copies:
        copy.wait()
    for k in range(len(near)):
        tile = tile + tile_come[depth - 1 + k]
    square_out[...] = tile + square_sum(vec_total)


def reduce_all(groups, down_part, up_part, proj_part, qkv_part, vec_part, row_args):
    depth = groups // 4
    wide, kind = jnp.float32, jnp.bfloat16

    def grid_of(part):
        return part.reshape(depth, 2, 2, part.shape[0] // groups, part.shape[1])

    parts = [
        grid_of(down_part),
        grid_of(up_part),
        proj_part.reshape(depth, 2, proj_part.shape[0] // depth // 2, proj_part.shape[1]),
        grid_of(qkv_part),
    ]
    scratch = []
    for index, part in enumerate(parts):
        rows, columns = part.shape[-2:]
        block = (rows, columns // 2 if index == 2 else columns)
        held = (depth, rows, columns) if index == 2 else (depth, 2, rows, columns)
        final = block if index == 2 else (rows, columns // 2)
        scratch += [
            pltpu.VMEM(held, kind), pltpu.VMEM(held, kind),
            pltpu.VMEM((depth,) + block, wide), pltpu.VMEM((depth,) + block, kind),
            pltpu.VMEM((depth,) + block, kind), pltpu.VMEM((depth - 1,) + block, kind),
            pltpu.VMEM((depth - 1,) + block, kind), pltpu.VMEM(final, kind),
            pltpu.VMEM(final, kind),
        ]
    near = 7
    scratch += [
        pltpu.VMEM((3,) + vec_part.shape, wide),
        pltpu.VMEM((2 + depth,) + vec_part.shape, wide),
        pltpu.VMEM((2, 8, LANES), wide),
        pltpu.VMEM((depth - 1 + near, 8, LANES), wide),
        pltpu.VMEM(row_args[1].shape, kind),
        pltpu.VMEM(vec_part.shape, wide),
        pltpu.SemaphoreType.DMA((4, depth + 2)),
        pltpu.SemaphoreType.DMA((4, depth + 2)),
        pltpu.SemaphoreType.DMA((2 + 2 * depth + near,)),
        pltpu.SemaphoreType.DMA((2 + 2 * depth + near,)),
        pltpu.SemaphoreType.DMA((1,)),
        pltpu.SemaphoreType.DMA((1,)),
        pltpu.SemaphoreType.DMA((4,)),
    ]
    down, up, proj, qkv = parts
    shapes = [
        jax.ShapeDtypeStruct((2 * down.shape[-2], down.shape[-1] // 2), wide),
        jax.ShapeDtypeStruct(up.shape[-2:], wide),
        jax.ShapeDtypeStruct((proj.shape[-2], proj.shape[-1] // 2), wide),
        jax.ShapeDtypeStruct(qkv.shape[-2:], wide),
        jax.ShapeDtypeStruct(vec_part.shape, wide),
        jax.ShapeDtypeStruct((8, LANES), wide),
        jax.ShapeDtypeStruct(row_args[0].shape, wide),
    ]
    vmem = pl.BlockSpec(memory_space=pltpu.VMEM)
    hbm = pl.BlockSpec(memory_space=pl.ANY)
    return pl.pallas_call(
        lambda *refs: reduce_kernel(groups, *refs),
        in_specs=[hbm] * 4 + [vmem] * 6,
        out_specs=[vmem] * 7,
        out_shape=shapes,
        scratch_shapes=scratch,
        compiler_params=pltpu.CompilerParams(
            collective_id=1, has_side_effects=True, vmem_limit_bytes=56 * 1024 * 1024
        ),
        cost_estimate=pl.CostEstimate(
            flops=0, bytes_accessed=4 * sum(part.size for part in parts), transcendentals=0
        ),
        name="reduce_all",
    )(*parts, vec_part, *row_args)


def adam_kernel(square_ref, *refs):
    count = len(refs) // 6
    norm_limit = math.sqrt(NPARAM)
    clip = norm_limit / jnp.maximum(jnp.sqrt(square_ref[0:1, 0:1]), norm_limit)
    fix_first = 1.0 - math.pow(beta_one, STEP)
    fix_second = 1.0 - math.pow(beta_two, STEP)
    ins, outs = refs[: 3 * count], refs[3 * count :]
    for index in range(count):
        weight_ref, moment_ref, grad_ref = ins[3 * index : 3 * index + 3]
        grad_out, weight_out, moment_out = outs[3 * index : 3 * index + 3]
        grad, weight = grad_ref[...], weight_ref[...]
        clipped = grad * clip
        first_new = beta_one * moment_ref[0] + (1.0 - beta_one) * clipped
        second_new = beta_two * moment_ref[1] + (1.0 - beta_two) * clipped * clipped
        direction = first_new / fix_first / (jnp.sqrt(second_new / fix_second) + adam_eps)
        grad_out[...] = grad
        weight_out[...] = weight - learn_rate * (direction + decay_rate * weight)
        moment_out[0] = first_new
        moment_out[1] = second_new


def adam_all(square, weights, moments, grads):
    steps = 4
    in_specs = [pl.BlockSpec(square.shape, lambda i: (0, 0))]
    out_specs, shapes, ins = [], [], [square]
    for weight, moment, grad in zip(weights, moments, grads):
        rows, columns = weight.shape
        if rows % (8 * steps) == 0:
            flat = pl.BlockSpec((rows // steps, columns), lambda i: (i, 0))
            both = pl.BlockSpec((2, rows // steps, columns), lambda i: (0, i, 0))
        else:
            flat = pl.BlockSpec((rows, columns), lambda i: (0, 0))
            both = pl.BlockSpec((2, rows, columns), lambda i: (0, 0, 0))
        in_specs += [flat, both, flat]
        out_specs += [flat, flat, both]
        shapes += [
            jax.ShapeDtypeStruct(grad.shape, grad.dtype),
            jax.ShapeDtypeStruct(weight.shape, weight.dtype),
            jax.ShapeDtypeStruct(moment.shape, moment.dtype),
        ]
        ins += [weight, moment, grad]
    size = sum(weight.size for weight in weights)
    results = pl.pallas_call(
        adam_kernel,
        grid=(steps,),
        in_specs=in_specs,
        out_specs=out_specs,
        out_shape=shapes,
        cost_estimate=pl.CostEstimate(
            flops=20 * size, bytes_accessed=32 * size, transcendentals=2 * size
        ),
        name="adam_all",
    )(*ins)
    return results[0::3], results[1::3], results[2::3]


def swap_shard(piece):
    return lax.ppermute(piece, "shard", [(0, 1), (1, 0)])


def pick(array, index, axis):
    return lax.dynamic_index_in_dim(array, index, axis=axis, keepdims=False)


def sum_halves(partial, member, local_rows):
    halves = partial.reshape(2, local_rows, partial.shape[-1])
    received = swap_shard(pick(halves, 1 - member, 0).astype(jnp.bfloat16))
    return pick(halves, member, 0) + received.astype(jnp.float32)


def spread(values, width, member):
    blocks = values.reshape(-1, 1, width)
    chosen = jnp.arange(2, dtype=jnp.int32)[None, :, None] == member
    return jnp.where(chosen, blocks, 0.0).reshape(-1)


def rolled(rows, cosine, down_sine, up_sine):
    width = rows.shape[1]
    lower = pltpu.roll(rows, width - ROT // 2, 1)
    upper = pltpu.roll(rows, ROT // 2, 1)
    return rows * cosine + lower * down_sine + upper * up_sine


def split_pair(rows):
    lanes = lax.broadcasted_iota(jnp.int32, rows.shape, 1)
    return (
        jnp.where(lanes < HD, rows, jnp.zeros_like(rows)),
        jnp.where(lanes < HD, jnp.zeros_like(rows), rows),
    )


def block_mask(seg_column, seg_row, start, size, extent):
    rows = start + lax.broadcasted_iota(jnp.int32, (size, extent), 0)
    keys = lax.broadcasted_iota(jnp.int32, (size, extent), 1)
    same = seg_column[start : start + size, :] == seg_row[:, :extent]
    return same & (keys <= rows)


def lane_tables(positions):
    dims = jnp.arange(2 * HD, dtype=jnp.int32) % HD
    half_dims = ROT // 2
    exponent = (dims % half_dims).astype(jnp.float32) * (2.0 / ROT)
    inverse_freq = jnp.exp(-math.log(rope_base) * exponent)
    angles = positions.astype(jnp.float32)[:, None] * inverse_freq[None, :]
    sine = jnp.sin(angles)
    return (
        jnp.where(dims[None] < ROT, jnp.cos(angles), 1.0),
        jnp.where(dims[None] < half_dims, -sine, 0.0),
        jnp.where((dims[None] >= half_dims) & (dims[None] < ROT), sine, 0.0),
    )


def shards(
    tokens,
    out_grad,
    segment_ids,
    qkv_weight,
    proj_weight,
    up_weight,
    down_weight,
    vectors,
    qkv_moments,
    proj_moments,
    up_moments,
    down_moments,
    vector_moments,
):
    groups = lax.axis_size("dp")
    members = lax.axis_size("shard")
    head_count = D // HD
    if members != 2 or groups != head_count:
        return plain_shards(
            tokens,
            out_grad,
            segment_ids,
            qkv_weight,
            proj_weight,
            up_weight,
            down_weight,
            vectors,
            qkv_moments,
            proj_moments,
            up_moments,
            down_moments,
            vector_moments,
        )
    member = lax.axis_index("shard")
    group = lax.axis_index("dp")
    half = D // 2
    local_rows = tokens.shape[0]
    vec_width = vectors.shape[1]
    pairs = half // LANES

    vec_all, qkv_all, proj_all, up_piece, down_piece, unit_all, unit, inverse = gather_first(
        groups, tokens, vectors, qkv_weight, proj_weight, up_weight, down_weight
    )
    vec_work = (
        vec_all.reshape(2 * groups, 16, LANES)[:, :VROWS, :vec_width]
        .transpose(1, 0, 2)
        .reshape(VROWS, D)
        .astype(jnp.float32)
    )
    qkv_work = qkv_all.reshape(D, 3 * half)
    proj_work = proj_all.reshape(half, D)
    unit_rows = unit_all.reshape(2 * local_rows, D).astype(jnp.float32)
    hidden_one = (unit_rows * vec_work[0] + vec_work[1]).astype(jnp.bfloat16)
    hidden_two = (unit_rows * vec_work[2] + vec_work[3]).astype(jnp.bfloat16)

    segment_row = segment_ids[0]
    positions = doc_positions(segment_row)
    tables = lane_tables(positions)

    q_bias = pick(vec_work[4].reshape(pairs, 2, LANES), member, 1).reshape(-1)
    v_bias = pick(vec_work[5].reshape(pairs, 2, LANES), member, 1).reshape(-1)
    up_bias = pick(vec_work[8:].reshape(groups, 2, LANES), member, 1).reshape(-1)

    mixed_rows = jnp.dot(hidden_one, qkv_work, preferred_element_type=jnp.float32)
    up_all, down_all, cot_all, attended_bf, grad_mixed_bf, q_bias_part, v_bias_part = (
        attention_all(
            groups, up_piece, down_piece, out_grad.astype(jnp.bfloat16), proj_work, mixed_rows,
            q_bias, v_bias, tables, segment_row,
        )
    )
    up_work = up_all.reshape(D, FF // 2)
    down_work = down_all.reshape(FF // 2, D)
    cot_bf = cot_all.reshape(2 * local_rows, D)
    proj_part = transposed_times(attended_bf, cot_bf).astype(jnp.bfloat16)
    q_bias_part, v_bias_part = q_bias_part[0], v_bias_part[0]
    qkv_part = transposed_times(hidden_one, grad_mixed_bf).astype(jnp.bfloat16)
    rows_partial = times_transposed(grad_mixed_bf, qkv_work)

    pre_act = jnp.dot(hidden_two, up_work, preferred_element_type=jnp.float32) + up_bias
    act_values, act_slope = gelu_pair(pre_act)
    act_bf = act_values.astype(jnp.bfloat16)
    grad_pre = times_transposed(cot_bf, down_work) * act_slope
    grad_pre_bf = grad_pre.astype(jnp.bfloat16)
    down_part = transposed_times(act_bf, cot_bf).astype(jnp.bfloat16)
    up_part = transposed_times(hidden_two, grad_pre_bf).astype(jnp.bfloat16)

    out_partial = jnp.dot(
        attended_bf, proj_work, preferred_element_type=jnp.float32
    ) + jnp.dot(act_bf, down_work, preferred_element_type=jnp.float32)
    block_out = (
        tokens + sum_halves(out_partial, member, local_rows) + vec_work[6] + vec_work[7]
    )
    rows_two, ln2_gain_part, ln2_bias_part = norm_back(
        sum_halves(times_transposed(grad_pre_bf, up_work), member, local_rows),
        unit,
        inverse,
        vec_work[2],
    )
    cot_sum = jnp.sum(out_grad, axis=0)
    zero_row = jnp.zeros_like(cot_sum)
    base_grad = out_grad + rows_two
    vec_part = jnp.concatenate(
        [
            jnp.stack(
                [
                    zero_row,
                    zero_row,
                    ln2_gain_part,
                    ln2_bias_part,
                    spread(q_bias_part, LANES, member),
                    spread(v_bias_part, LANES, member),
                    cot_sum,
                    cot_sum,
                ]
            ),
            spread(jnp.sum(grad_pre, axis=0), LANES, member).reshape(FF // D, D),
            jnp.zeros((16 - VROWS, D), jnp.float32),
        ],
        axis=0,
    )
    halves = rows_partial.reshape(2, local_rows, D)
    down_grad, up_grad, proj_grad, qkv_grad, vec_sum, square, rows_one = reduce_all(
        groups, down_part, up_part, proj_part, qkv_part, vec_part,
        (
            pick(halves, member, 0), pick(halves, 1 - member, 0).astype(jnp.bfloat16),
            unit, inverse, vec_work[0:1],
        ),
    )
    tokens_grad = base_grad + rows_one
    vectors_grad = lax.dynamic_slice_in_dim(
        vec_sum[:VROWS], (group * 2 + member) * vec_width, vec_width, axis=1
    )
    grads, weights_new, moments_new = adam_all(
        square,
        (qkv_weight, proj_weight, up_weight, down_weight, vectors),
        (qkv_moments, proj_moments, up_moments, down_moments, vector_moments),
        (qkv_grad, proj_grad, up_grad, down_grad, vectors_grad),
    )
    return (block_out, tokens_grad, *grads, *weights_new, *moments_new)


def solution(mesh):
    placed = (
        P(("dp", "shard"), None),
        P(("dp", "shard"), None),
        P("dp", None),
        P("dp", "shard"),
        P("dp", "shard"),
        P("dp", "shard"),
        P("dp", "shard"),
        P(None, ("dp", "shard")),
        P(None, "dp", "shard"),
        P(None, "dp", "shard"),
        P(None, "dp", "shard"),
        P(None, "dp", "shard"),
        P(None, None, ("dp", "shard")),
    )
    return jax.shard_map(
        shards,
        mesh=mesh,
        in_specs=placed,
        out_specs=(
            P(("dp", "shard"), None),
            P(("dp", "shard"), None),
            P("dp", "shard"),
            P("dp", "shard"),
            P("dp", "shard"),
            P("dp", "shard"),
            P(None, ("dp", "shard")),
            P("dp", "shard"),
            P("dp", "shard"),
            P("dp", "shard"),
            P("dp", "shard"),
            P(None, ("dp", "shard")),
            P(None, "dp", "shard"),
            P(None, "dp", "shard"),
            P(None, "dp", "shard"),
            P(None, "dp", "shard"),
            P(None, None, ("dp", "shard")),
        ),
        check_vma=False,
    )
```

```python
import math

import jax
import jax.numpy as jnp
from jax import lax
from jax.experimental import pallas as pl
from jax.experimental.pallas import tpu as pltpu
from jax.sharding import PartitionSpec as P

D = 1024
FF = 4096
HD = 64
ROT = 16
STEP = 4
VROWS = 12
NPARAM = 12595200


ln_eps = 1e-05
beta_one = 0.9
beta_two = 0.95
learn_rate = 0.005
decay_rate = 0.01
adam_eps = 1e-08
rope_base = 10000.0


def norm_rows(inputs, gain_row, bias_row):
    center = inputs - jnp.mean(inputs, axis=-1, keepdims=True)
    inverse = lax.rsqrt(jnp.mean(center * center, axis=-1, keepdims=True) + ln_eps)
    unit_rows = center * inverse
    return (unit_rows * gain_row + bias_row, unit_rows, inverse)


def norm_back(upstream, unit_rows, inverse, gain_row):
    gain_grad = jnp.sum(upstream * unit_rows, axis=0)
    bias_grad = jnp.sum(upstream, axis=0)
    scaled_up = upstream * gain_row
    mean_plain = jnp.mean(scaled_up, axis=-1, keepdims=True)
    mean_unit = jnp.mean(scaled_up * unit_rows, axis=-1, keepdims=True)
    return (inverse * (scaled_up - mean_plain - unit_rows * mean_unit), gain_grad, bias_grad)


def doc_positions(segment_row):
    length_all = segment_row.shape[0]
    indices = jnp.arange(length_all, dtype=jnp.int32)
    starting = jnp.concatenate(
        [jnp.ones((1,), dtype=jnp.bool_), segment_row[1:] != segment_row[:-1]]
    )
    begins = lax.cummax(jnp.where(starting, indices, 0), axis=0)
    return indices - begins


def rotary_tables(positions, rot_dims):
    half_dims = rot_dims // 2
    exponent = jnp.arange(half_dims, dtype=jnp.float32) * (2.0 / rot_dims)
    inverse_freq = jnp.exp(-math.log(rope_base) * exponent)
    angles = positions.astype(jnp.float32)[:, None] * inverse_freq[None, :]
    return (jnp.cos(angles)[:, None, :], jnp.sin(angles)[:, None, :])


def rotate(head_rows, cosine_table, sine_table):
    half_dims = cosine_table.shape[-1]
    lower_half = head_rows[..., :half_dims]
    upper_half = head_rows[..., half_dims : 2 * half_dims]
    return jnp.concatenate(
        [
            lower_half * cosine_table - upper_half * sine_table,
            upper_half * cosine_table + lower_half * sine_table,
            head_rows[..., 2 * half_dims :],
        ],
        axis=-1,
    )


def gelu_pair(pre_act):
    normal_cdf = 0.5 * (1.0 + lax.erf(pre_act * (1.0 / math.sqrt(2.0))))
    density = jnp.exp(-0.5 * pre_act * pre_act) * (1.0 / math.sqrt(2.0 * math.pi))
    return (pre_act * normal_cdf, normal_cdf + pre_act * density)


def times_transposed(left, right):
    return lax.dot_general(
        left, right, (((1,), (1,)), ((), ())), preferred_element_type=jnp.float32
    )


def transposed_times(left, right):
    return lax.dot_general(
        left, right, (((0,), (0,)), ((), ())), preferred_element_type=jnp.float32
    )


def adam_update(weight, moments, gradient, clip_factor):
    clipped = gradient * clip_factor
    first_new = beta_one * moments[0] + (1.0 - beta_one) * clipped
    second_new = beta_two * moments[1] + (1.0 - beta_two) * clipped * clipped
    fix_first = 1.0 - math.pow(beta_one, STEP)
    fix_second = 1.0 - math.pow(beta_two, STEP)
    direction = first_new / fix_first / (jnp.sqrt(second_new / fix_second) + adam_eps)
    return (
        weight - learn_rate * (direction + decay_rate * weight),
        jnp.stack([first_new, second_new]),
    )


def plain_shards(
    tokens,
    out_grad,
    segment_ids,
    qkv_weight,
    proj_weight,
    up_weight,
    down_weight,
    vectors,
    qkv_moments,
    proj_moments,
    up_moments,
    down_moments,
    vector_moments,
):
    columns_full = (
        lax.all_gather(qkv_weight.astype(jnp.bfloat16), "shard", axis=1, tiled=True),
        lax.all_gather(proj_weight.astype(jnp.bfloat16), "shard", axis=1, tiled=True),
        lax.all_gather(up_weight.astype(jnp.bfloat16), "shard", axis=1, tiled=True),
        lax.all_gather(down_weight.astype(jnp.bfloat16), "shard", axis=1, tiled=True),
        lax.all_gather(vectors.astype(jnp.bfloat16), "shard", axis=1, tiled=True),
    )
    qkv_work, proj_work, up_work, down_work, vec_bf = (
        lax.all_gather(columns_full[0], "dp", axis=0, tiled=True),
        lax.all_gather(columns_full[1], "dp", axis=0, tiled=True),
        lax.all_gather(columns_full[2], "dp", axis=0, tiled=True),
        lax.all_gather(columns_full[3], "dp", axis=0, tiled=True),
        lax.all_gather(columns_full[4], "dp", axis=1, tiled=True),
    )
    vec_work = vec_bf.astype(jnp.float32)
    head_count = D // HD
    score_scale = 1.0 / math.sqrt(HD)
    local_rows = tokens.shape[0]
    segment_row = segment_ids[0]
    length_all = segment_row.shape[0]
    row_start = lax.axis_index("shard") * local_rows
    query_index = row_start + jnp.arange(local_rows, dtype=jnp.int32)
    query_segment = lax.dynamic_slice_in_dim(segment_row, row_start, local_rows)
    positions = lax.dynamic_slice_in_dim(doc_positions(segment_row), row_start, local_rows)
    normed_one, unit_one, inverse_one = norm_rows(tokens, vec_work[0], vec_work[1])
    hidden_one = normed_one.astype(jnp.bfloat16)
    mixed_rows = jnp.dot(hidden_one, qkv_work, preferred_element_type=jnp.float32)
    query_raw = (mixed_rows[:, :D] + vec_work[4]).reshape(local_rows, head_count, HD)
    key_raw = mixed_rows[:, D : 2 * D].reshape(local_rows, head_count, HD)
    value_bf = (mixed_rows[:, 2 * D :] + vec_work[5]).astype(jnp.bfloat16)
    cosine_table, sine_table = rotary_tables(positions, ROT)
    query_bf = rotate(query_raw, cosine_table, sine_table).astype(jnp.bfloat16)
    key_bf = rotate(key_raw, cosine_table, sine_table).astype(jnp.bfloat16).reshape(local_rows, D)
    key_piece = lax.all_gather(key_bf, "shard", axis=0, tiled=True)
    value_piece = lax.all_gather(value_bf, "shard", axis=0, tiled=True)
    piece_rows = key_piece.shape[0]
    key_heads = key_piece.reshape(piece_rows, head_count, HD)
    value_heads = value_piece.reshape(piece_rows, head_count, HD)
    key_index = jnp.arange(piece_rows, dtype=jnp.int32)
    allowed = (segment_row[None, :] == query_segment[:, None]) & (
        key_index[None, :] <= query_index[:, None]
    )
    scores = (
        jnp.einsum("qhd,khd->hqk", query_bf, key_heads, preferred_element_type=jnp.float32)
        * score_scale
    )
    exp_scores = jnp.where(allowed[None], jnp.exp(scores), 0.0)
    numerator = jnp.einsum(
        "hqk,khd->qhd",
        exp_scores.astype(jnp.bfloat16),
        value_heads,
        preferred_element_type=jnp.float32,
    )
    numerator, totals = (numerator, jnp.sum(exp_scores, axis=-1))
    attended = numerator / jnp.transpose(totals)[:, :, None]
    log_totals = jnp.log(totals)
    attended_bf = attended.reshape(local_rows, D).astype(jnp.bfloat16)
    proj_out = jnp.dot(attended_bf, proj_work, preferred_element_type=jnp.float32) + vec_work[6]
    normed_two, unit_two, inverse_two = norm_rows(tokens, vec_work[2], vec_work[3])
    hidden_two = normed_two.astype(jnp.bfloat16)
    pre_act = jnp.dot(hidden_two, up_work, preferred_element_type=jnp.float32) + vec_work[
        8:
    ].reshape(FF)
    act_values, act_slope = gelu_pair(pre_act)
    act_bf = act_values.astype(jnp.bfloat16)
    block_out = (
        tokens
        + proj_out
        + (jnp.dot(act_bf, down_work, preferred_element_type=jnp.float32) + vec_work[7])
    )
    cot_bf = out_grad.astype(jnp.bfloat16)
    down_part = transposed_times(act_bf, cot_bf)
    proj_part = transposed_times(attended_bf, cot_bf)
    cot_sum = jnp.sum(out_grad, axis=0)
    grad_pre = times_transposed(cot_bf, down_work) * act_slope
    grad_pre_bf = grad_pre.astype(jnp.bfloat16)
    up_part = transposed_times(hidden_two, grad_pre_bf)
    rows_two, ln2_gain_part, ln2_bias_part = norm_back(
        times_transposed(grad_pre_bf, up_work), unit_two, inverse_two, vec_work[2]
    )
    grad_att_bf = (
        times_transposed(cot_bf, proj_work).astype(jnp.bfloat16).reshape(local_rows, head_count, HD)
    )
    keys_all, values_all = (
        lax.all_gather(key_bf, "shard", axis=0, tiled=True),
        lax.all_gather(value_bf, "shard", axis=0, tiled=True),
    )
    key_heads = keys_all.reshape(length_all, head_count, HD)
    value_heads = values_all.reshape(length_all, head_count, HD)
    key_index = jnp.arange(length_all, dtype=jnp.int32)
    allowed = (segment_row[None, :] == query_segment[:, None]) & (
        key_index[None, :] <= query_index[:, None]
    )
    scores = (
        jnp.einsum("qhd,khd->hqk", query_bf, key_heads, preferred_element_type=jnp.float32)
        * score_scale
    )
    probability = jnp.where(allowed[None], jnp.exp(scores - log_totals[:, :, None]), 0.0)
    grad_prob = jnp.einsum(
        "qhd,khd->hqk", grad_att_bf, value_heads, preferred_element_type=jnp.float32
    )
    row_delta = jnp.transpose(jnp.sum(grad_att_bf.astype(jnp.float32) * attended, axis=-1))
    grad_score = (probability * (grad_prob - row_delta[:, :, None]) * score_scale).astype(
        jnp.bfloat16
    )
    grad_query = jnp.einsum(
        "hqk,khd->qhd", grad_score, key_heads, preferred_element_type=jnp.float32
    )
    grad_query = rotate(grad_query, cosine_table, -sine_table).reshape(local_rows, D)
    key_terms = jnp.einsum(
        "hqk,qhd->khd", grad_score, query_bf, preferred_element_type=jnp.float32
    ).reshape(length_all, D)
    value_terms = jnp.einsum(
        "hqk,qhd->khd",
        probability.astype(jnp.bfloat16),
        grad_att_bf,
        preferred_element_type=jnp.float32,
    ).reshape(length_all, D)
    key_value_grad = lax.psum_scatter(
        jnp.concatenate([key_terms, value_terms], axis=1), "shard", scatter_dimension=0, tiled=True
    )
    grad_key = rotate(
        key_value_grad[:, :D].reshape(local_rows, head_count, HD), cosine_table, -sine_table
    ).reshape(local_rows, D)
    grad_value = key_value_grad[:, D:]
    grad_mixed_bf = jnp.concatenate([grad_query, grad_key, grad_value], axis=1).astype(jnp.bfloat16)
    qkv_part = transposed_times(hidden_one, grad_mixed_bf)
    rows_one, ln1_gain_part, ln1_bias_part = norm_back(
        times_transposed(grad_mixed_bf, qkv_work), unit_one, inverse_one, vec_work[0]
    )
    tokens_grad = out_grad + rows_one + rows_two
    vec_part = jnp.concatenate(
        [
            jnp.stack(
                [
                    ln1_gain_part,
                    ln1_bias_part,
                    ln2_gain_part,
                    ln2_bias_part,
                    jnp.sum(grad_query, axis=0),
                    jnp.sum(grad_value, axis=0),
                    cot_sum,
                    cot_sum,
                ]
            ),
            jnp.sum(grad_pre, axis=0).reshape(FF // D, D),
        ],
        axis=0,
    )
    groups = lax.axis_size("dp")
    members = lax.axis_size("shard")
    owners = groups * members
    vec_split = vec_part.reshape(VROWS, groups, members, D // owners)
    group_sums = (
        lax.psum_scatter(qkv_part, "shard", scatter_dimension=1, tiled=True),
        lax.psum_scatter(proj_part, "shard", scatter_dimension=1, tiled=True),
        lax.psum_scatter(up_part, "shard", scatter_dimension=1, tiled=True),
        lax.psum_scatter(down_part, "shard", scatter_dimension=1, tiled=True),
        lax.psum_scatter(vec_split, "shard", scatter_dimension=2, tiled=True),
    )
    owner_sums = (
        lax.psum_scatter(group_sums[0], "dp", scatter_dimension=0, tiled=True),
        lax.psum_scatter(group_sums[1], "dp", scatter_dimension=0, tiled=True),
        lax.psum_scatter(group_sums[2], "dp", scatter_dimension=0, tiled=True),
        lax.psum_scatter(group_sums[3], "dp", scatter_dimension=0, tiled=True),
        lax.psum_scatter(group_sums[4], "dp", scatter_dimension=1, tiled=True),
    )
    qkv_grad = owner_sums[0]
    proj_grad = owner_sums[1]
    up_grad = owner_sums[2]
    down_grad = owner_sums[3]
    vectors_grad = owner_sums[4].reshape(VROWS, D // owners)
    local_square = (
        jnp.sum(qkv_grad * qkv_grad)
        + jnp.sum(proj_grad * proj_grad)
        + jnp.sum(up_grad * up_grad)
        + jnp.sum(down_grad * down_grad)
        + jnp.sum(vectors_grad * vectors_grad)
    )
    square_total = lax.psum(local_square, ("dp", "shard"))
    norm_limit = math.sqrt(NPARAM)
    clip_factor = norm_limit / jnp.maximum(jnp.sqrt(square_total), norm_limit)
    qkv_new, qkv_moments_new = adam_update(qkv_weight, qkv_moments, qkv_grad, clip_factor)
    proj_new, proj_moments_new = adam_update(proj_weight, proj_moments, proj_grad, clip_factor)
    up_new, up_moments_new = adam_update(up_weight, up_moments, up_grad, clip_factor)
    down_new, down_moments_new = adam_update(down_weight, down_moments, down_grad, clip_factor)
    vectors_new, vector_moments_new = adam_update(
        vectors, vector_moments, vectors_grad, clip_factor
    )
    return (
        block_out,
        tokens_grad,
        qkv_grad,
        proj_grad,
        up_grad,
        down_grad,
        vectors_grad,
        qkv_new,
        proj_new,
        up_new,
        down_new,
        vectors_new,
        qkv_moments_new,
        proj_moments_new,
        up_moments_new,
        down_moments_new,
        vector_moments_new,
    )

MESH = pl.DeviceIdType.MESH
LANES = 128


def place(groups):
    group = lax.axis_index("dp")
    depth = groups // 4
    return depth, group // 4, lax.rem(group // 2, 2), lax.rem(group, 2), lax.axis_index("shard")


def device(z, y, c, x):
    return (z * 4 + y * 2 + c, x)


def greet(peers):
    barrier = pltpu.get_barrier_semaphore()
    for peer in peers:
        pl.semaphore_signal(barrier, inc=1, device_id=peer, device_id_type=MESH)
    pl.semaphore_wait(barrier, len(peers))


def half_lanes(member, width):
    return pl.ds(pl.multiple_of(member * width, LANES), width)


def gather_kernel(
    groups,
    tokens_in, vec_in, qkv_in, proj_in, up_in, down_in,
    vec_out, qkv_out, proj_out, up_out, down_out, rows_out, unit_out, inverse_out,
    vec_piece, qkv_keep, qkv_send, proj_piece, up_keep, up_send, down_keep, down_send, unit_piece,
    send_sem, recv_sem, swap_send, swap_recv, local_sem,
):
    depth, z, y, c, x = place(groups)
    kind = jnp.bfloat16
    across = device(z, y, c, 1 - x)
    beside = device(z, 1 - y, c, x)
    twin = device(z, y, 1 - c, x)
    corner = device(z, x, c, y)
    far = [lax.rem(z + k, depth) for k in range(1, depth)]
    back = [lax.rem(z + depth - k, depth) for k in range(depth)]
    greet(
        [across, beside, twin, device(z, 1 - y, c, 1 - x)] + [device(zz, y, c, x) for zz in far]
    )

    def remote(src, dst, index, peer, sems=(send_sem, recv_sem)):
        return pltpu.make_async_remote_copy(
            src_ref=src, dst_ref=dst, send_sem=sems[0].at[index], recv_sem=sems[1].at[index],
            device_id=peer, device_id_type=MESH,
        )

    def block(item, zz, yy, cc):
        if item == "vec":
            return vec_out.at[zz, yy, cc]
        if item == "proj":
            return proj_out.at[zz, cc, :, half_lanes(yy, proj_out.shape[3] // 2)]
        size = qkv_out.shape[3] // 2
        return qkv_out.at[zz, yy, cc, pl.ds(item * size, size)]

    def split(source, keep, sent):
        for b in range(keep.shape[1] // LANES):
            lanes = slice(b * LANES, (b + 1) * LANES)
            keep[:, lanes] = source[:, half_lanes(2 * b + x, LANES)].astype(kind)
            sent[:, lanes] = source[:, half_lanes(2 * b + 1 - x, LANES)].astype(kind)

    swap_sems = (swap_send, swap_recv)
    swaps, stays = [], []

    def swap(keep, sent, target):
        index = len(swaps)
        swaps.append(remote(sent, target, index, across, swap_sems))
        stays.append(pltpu.make_async_copy(keep, target, local_sem.at[index]))
        swaps[-1].start()
        stays[-1].start()

    split(qkv_in, qkv_keep, qkv_send)
    swap(qkv_keep, qkv_send, qkv_out.at[z, y, c, :, half_lanes(x, qkv_keep.shape[1])])
    vec_piece[...] = jnp.zeros_like(vec_piece)
    vec_piece[: vec_in.shape[0], : vec_in.shape[1]] = vec_in[...].astype(kind)
    swap(vec_piece, vec_piece, vec_out.at[z, y, c, x])
    proj_piece[...] = proj_in[...].astype(kind)
    proj_move = remote(
        proj_piece, proj_out.at[z, c, :, half_lanes(x, proj_out.shape[3] // 2)], 5, corner,
        swap_sems,
    )
    proj_stay = pltpu.make_async_copy(proj_piece, block("proj", z, y, c), local_sem.at[5])
    pl.when(x != y)(lambda: proj_move.start())
    pl.when(x == y)(lambda: proj_stay.start())

    @pl.loop(0, tokens_in.shape[0] // 64)
    def _(step):
        part = pl.ds(pl.multiple_of(step * 64, 64), 64)
        rows = tokens_in[part, :]
        center = rows - jnp.mean(rows, axis=-1, keepdims=True)
        inverse = lax.rsqrt(jnp.mean(center * center, axis=-1, keepdims=True) + ln_eps)
        unit = center * inverse
        unit_out[part, :] = unit
        inverse_out[part, :] = inverse
        unit_piece[part, :] = unit.astype(kind)

    items = ("vec", 0, 1, "proj")
    along, over, pair = {}, {}, {}

    def launch(a, item):
        mine = block(item, z, y, c)
        for k in range(1, depth):
            along[item, k] = remote(mine, mine, (a, k), device(far[k - 1], y, c, x))
            along[item, k].start()
        over[item, 0] = remote(mine, mine, (a, depth), beside)
        over[item, 0].start()
        pair[item, 0, 0] = remote(mine, mine, (a, 2 * depth), twin)
        pair[item, 0, 0].start()

    for index in range(2):
        stays[index].wait()
        swaps[index].wait()
    for a in range(3):
        launch(a, items[a])
    swap(unit_piece, unit_piece, rows_out.at[x])
    split(up_in, up_keep, up_send)
    swap(up_keep, up_send, up_out.at[:, half_lanes(x, up_keep.shape[1])])
    size = down_in.shape[0] // 2
    down_keep[...] = down_in[pl.ds(pl.multiple_of(x * size, 16), size), :].astype(kind)
    down_send[...] = down_in[pl.ds(pl.multiple_of((1 - x) * size, 16), size), :].astype(kind)
    swap(down_keep, down_send, down_out.at[:, half_lanes(x, down_keep.shape[1])])
    pl.when(x != y)(lambda: proj_move.wait())
    pl.when(x == y)(lambda: proj_stay.wait())
    launch(3, "proj")
    for a, item in enumerate(items):
        for k in range(1, depth):
            along[item, k].wait_recv()
            come = block(item, back[k], y, c)
            over[item, k] = remote(come, come, (a, depth + k), beside)
            over[item, k].start()
            pair[item, 0, k] = remote(come, come, (a, 2 * depth + k), twin)
            pair[item, 0, k].start()
    for a, item in enumerate(items):
        for k in range(depth):
            over[item, k].wait_recv()
            come = block(item, back[k], 1 - y, c)
            pair[item, 1, k] = remote(come, come, (a, 3 * depth + k), twin)
            pair[item, 1, k].start()
    for index in range(2, 5):
        stays[index].wait()
        swaps[index].wait()
    for item in items:
        for side in range(2):
            for k in range(depth):
                pair[item, side, k].wait()
        for k in range(depth):
            over[item, k].wait_send()
        for k in range(1, depth):
            along[item, k].wait_send()


def gather_first(groups, tokens, vectors, qkv, proj, up, down):
    depth = groups // 4
    kind, wide = jnp.bfloat16, jnp.float32
    local_rows, width = tokens.shape

    def halves(rows, columns):
        return [pltpu.VMEM((rows, columns), kind)] * 2

    shapes = [
        jax.ShapeDtypeStruct((depth, 2, 2, 2, 16, LANES), kind),
        jax.ShapeDtypeStruct((depth, 2, 2) + qkv.shape, kind),
        jax.ShapeDtypeStruct((depth, 2, proj.shape[0], 2 * proj.shape[1]), kind),
        jax.ShapeDtypeStruct(up.shape, kind),
        jax.ShapeDtypeStruct((down.shape[0] // 2, 2 * down.shape[1]), kind),
        jax.ShapeDtypeStruct((2, local_rows, width), kind),
        jax.ShapeDtypeStruct((local_rows, width), wide),
        jax.ShapeDtypeStruct((local_rows, 1), wide),
    ]
    vmem = pl.BlockSpec(memory_space=pltpu.VMEM)
    hbm = pl.BlockSpec(memory_space=pl.ANY)
    return pl.pallas_call(
        lambda *refs: gather_kernel(groups, *refs),
        in_specs=[vmem] * 6,
        out_specs=[hbm] * 6 + [vmem] * 2,
        out_shape=shapes,
        scratch_shapes=[
            pltpu.VMEM((16, LANES), kind),
            *halves(qkv.shape[0], qkv.shape[1] // 2),
            pltpu.VMEM(proj.shape, kind),
            *halves(up.shape[0], up.shape[1] // 2),
            *halves(down.shape[0] // 2, down.shape[1]),
            pltpu.VMEM((local_rows, width), kind),
            pltpu.SemaphoreType.DMA((4, 4 * depth)),
            pltpu.SemaphoreType.DMA((4, 4 * depth)),
            pltpu.SemaphoreType.DMA((6,)),
            pltpu.SemaphoreType.DMA((6,)),
            pltpu.SemaphoreType.DMA((6,)),
        ],
        compiler_params=pltpu.CompilerParams(collective_id=0, has_side_effects=True),
        cost_estimate=pl.CostEstimate(
            flops=0, bytes_accessed=64 * qkv.size, transcendentals=0
        ),
        name="gather_first",
    )(tokens, vectors, qkv, proj, up, down)


def forward_pair(
    index, mixed_ref, q_bias_ref, v_bias_ref, cos_ref, down_ref, up_ref, column_ref, row_ref,
    query_held, key_held, value_held, att_held, log_held, att_out,
):
    scale = 1.0 / math.sqrt(HD)
    length = mixed_ref.shape[0]
    width = mixed_ref.shape[1] // 3
    size = length // 4
    pairs = width // LANES
    lanes_of = half_lanes(index, LANES)
    cosine, down_sine, up_sine = cos_ref[...], down_ref[...], up_ref[...]
    query_held[index] = rolled(
        mixed_ref[:, lanes_of] + q_bias_ref[:, lanes_of], cosine, down_sine, up_sine
    ).astype(jnp.bfloat16)
    key_held[index] = rolled(
        mixed_ref[:, half_lanes(pairs + index, LANES)], cosine, down_sine, up_sine
    ).astype(jnp.bfloat16)
    value_held[index] = (
        mixed_ref[:, half_lanes(2 * pairs + index, LANES)] + v_bias_ref[:, lanes_of]
    ).astype(jnp.bfloat16)
    for start in range(0, length, size):
        extent = start + size
        mask = block_mask(column_ref, row_ref, start, size, extent)
        keys, values = key_held[index, :extent, :], value_held[index, :extent, :]
        results = []
        for query in split_pair(query_held[index, start:extent, :].astype(jnp.float32)):
            scores = times_transposed(query.astype(jnp.bfloat16), keys) * scale
            exp_scores = jnp.where(mask, jnp.exp(scores), 0.0)
            totals = jnp.sum(exp_scores, axis=1, keepdims=True)
            numerator = jnp.dot(
                exp_scores.astype(jnp.bfloat16), values, preferred_element_type=jnp.float32
            )
            results.append((numerator / totals, jnp.log(totals)))
        lanes = lax.broadcasted_iota(jnp.int32, (size, 2 * HD), 1) < HD
        attended = jnp.where(lanes, results[0][0], results[1][0])
        att_held[index, start:extent, :] = attended
        att_out[start:extent, lanes_of] = attended.astype(jnp.bfloat16)
        log_held[index, start:extent, :] = jnp.where(lanes, results[0][1], results[1][1])


def backward_pair(
    index, cot_ref, proj_ref, cos_ref, down_ref, up_ref, column_ref, row_ref,
    query_held, key_held, value_held, att_held, log_held, grad_held,
    query_sum, key_sum, value_sum, mixed_out, q_bias_out, v_bias_out,
):
    scale = 1.0 / math.sqrt(HD)
    length = query_held.shape[1]
    size = length // 4
    pairs = query_held.shape[0]
    proj_rows = proj_ref[pl.ds(pl.multiple_of(index * LANES, LANES), LANES), :]
    local_rows = cot_ref.shape[1]
    for side in range(2):
        grad_held[side * local_rows : (side + 1) * local_rows, :] = times_transposed(
            cot_ref[side], proj_rows
        ).astype(jnp.bfloat16)
    key_sum[...] = jnp.zeros_like(key_sum)
    value_sum[...] = jnp.zeros_like(value_sum)
    for start in range(0, length, size):
        extent = start + size
        mask = block_mask(column_ref, row_ref, start, size, extent)
        keys, values = key_held[index, :extent, :], value_held[index, :extent, :]
        queries = split_pair(query_held[index, start:extent, :].astype(jnp.float32))
        grads = split_pair(grad_held[start:extent, :].astype(jnp.float32))
        attended = att_held[index, start:extent, :]
        pieces = []
        for head in range(2):
            query = queries[head].astype(jnp.bfloat16)
            grad = grads[head].astype(jnp.bfloat16)
            log_total = log_held[index, start:extent, head * HD : head * HD + 1]
            scores = times_transposed(query, keys) * scale
            probability = jnp.where(mask, jnp.exp(scores - log_total), 0.0)
            grad_prob = times_transposed(grad, values)
            delta = jnp.sum(grads[head] * attended, axis=1, keepdims=True)
            grad_score = (probability * (grad_prob - delta) * scale).astype(jnp.bfloat16)
            pieces.append(jnp.dot(grad_score, keys, preferred_element_type=jnp.float32))
            key_sum[:extent, :] += transposed_times(grad_score, query)
            value_sum[:extent, :] += transposed_times(probability.astype(jnp.bfloat16), grad)
        lanes = lax.broadcasted_iota(jnp.int32, (size, 2 * HD), 1) < HD
        query_sum[start:extent, :] = jnp.where(lanes, pieces[0], pieces[1])
    cosine, down_sine, up_sine = cos_ref[...], down_ref[...], up_ref[...]
    grad_query = rolled(query_sum[...], cosine, -down_sine, -up_sine)
    mixed_out[:, half_lanes(index, LANES)] = grad_query.astype(jnp.bfloat16)
    q_bias_out[:, half_lanes(index, LANES)] = jnp.sum(grad_query, axis=0, keepdims=True)
    mixed_out[:, half_lanes(pairs + index, LANES)] = rolled(
        key_sum[...], cosine, -down_sine, -up_sine
    ).astype(jnp.bfloat16)
    grad_value = value_sum[...]
    mixed_out[:, half_lanes(2 * pairs + index, LANES)] = grad_value.astype(jnp.bfloat16)
    v_bias_out[:, half_lanes(index, LANES)] = jnp.sum(grad_value, axis=0, keepdims=True)


def attention_kernel(
    groups,
    up_in, down_in, cot_in, proj_in, mixed_in, q_bias_in, v_bias_in, cos_in, low_in, high_in,
    column_in, row_in,
    up_out, down_out, cot_out, att_out, mixed_out, q_bias_out, v_bias_out,
    query_held, key_held, value_held, att_held, log_held, grad_held,
    query_sum, key_sum, value_sum,
    send_sem, recv_sem, row_send, row_recv, local_sem,
):
    depth, z, y, c, x = place(groups)
    pairs = query_held.shape[0]
    across = device(z, y, c, 1 - x)
    beside = device(z, 1 - y, c, x)
    twin = device(z, y, 1 - c, x)
    far = [lax.rem(z + k, depth) for k in range(1, depth)]
    back = [lax.rem(z + depth - k, depth) for k in range(depth)]
    greet([across, beside, twin] + [device(zz, y, c, x) for zz in far])

    def remote(src, dst, index, peer, sems=(send_sem, recv_sem)):
        return pltpu.make_async_remote_copy(
            src_ref=src, dst_ref=dst, send_sem=sems[0].at[index], recv_sem=sems[1].at[index],
            device_id=peer, device_id_type=MESH,
        )

    arrays = ((up_in, up_out), (down_in, down_out))

    def rows_of(ref, i):
        size = ref.shape[-2] // pairs
        return pl.ds(pl.multiple_of(i * size, 16), size)

    def block(a, i, zz, yy, cc):
        out = arrays[a][1]
        return out.at[zz, yy, cc, rows_of(out, i)]

    def source(a, i):
        return arrays[a][0].at[rows_of(arrays[a][0], i)]

    def along(a, i, k):
        return remote(
            source(a, i), block(a, i, z, y, c), (a, i, k), device(far[k - 1], y, c, x)
        )

    def over(a, i, k):
        src = source(a, i) if k == 0 else block(a, i, back[k], y, c)
        return remote(src, block(a, i, back[k], y, c), (a, i, depth + k), beside)

    def pair(a, i, side, k):
        come = block(a, i, back[k], 1 - y if side else y, c)
        src = source(a, i) if (side, k) == (0, 0) else come
        return remote(src, come, (a, i, (2 + side) * depth + k), twin)

    cot_swap = remote(cot_in, cot_out.at[x], 0, across, (row_send, row_recv))
    cot_swap.start()
    stays = [
        pltpu.make_async_copy(arrays[a][0], arrays[a][1].at[z, y, c], local_sem.at[a])
        for a in range(2)
    ] + [pltpu.make_async_copy(cot_in, cot_out.at[x], local_sem.at[2])]
    for stay in stays:
        stay.start()

    @pl.loop(0, pairs)
    def _(i):
        for a in range(2):
            for k in range(1, depth):
                along(a, i, k).start()
            over(a, i, 0).start()
            pair(a, i, 0, 0).start()

    def relay_along(i):
        for a in range(2):
            for k in range(1, depth):
                along(a, i, k).wait_recv()
                over(a, i, k).start()
                pair(a, i, 0, k).start()

    def relay_over(i):
        for a in range(2):
            for k in range(depth):
                over(a, i, k).wait_recv()
                pair(a, i, 1, k).start()

    @pl.loop(0, pairs)
    def _(i):
        forward_pair(
            i, mixed_in, q_bias_in, v_bias_in, cos_in, low_in, high_in, column_in, row_in,
            query_held, key_held, value_held, att_held, log_held, att_out,
        )

    relay_along(0)
    relay_along(1)
    stays[2].wait()
    cot_swap.wait()

    @pl.loop(0, pairs)
    def _(i):
        backward_pair(
            i, cot_out, proj_in, cos_in, low_in, high_in, column_in, row_in,
            query_held, key_held, value_held, att_held, log_held, grad_held,
            query_sum, key_sum, value_sum, mixed_out, q_bias_out, v_bias_out,
        )
        pl.when(i == 0)(lambda: relay_along(2))
        pl.when(i == 2)(lambda: relay_along(3))
        relay_over(i)

    for stay in stays[:2]:
        stay.wait()

    @pl.loop(0, pairs)
    def _(i):
        for a in range(2):
            for k in range(depth):
                for side in range(2):
                    pair(a, i, side, k).wait()
                over(a, i, k).wait_send()
            for k in range(1, depth):
                along(a, i, k).wait_send()


def attention_all(
    groups, up, down, cot_bf, proj_work, mixed_rows, q_bias, v_bias, tables, segment_row
):
    depth = groups // 4
    length = mixed_rows.shape[0]
    width = mixed_rows.shape[1] // 3
    pairs = width // LANES
    kind, wide = jnp.bfloat16, jnp.float32
    shapes = [
        jax.ShapeDtypeStruct((depth, 2, 2) + up.shape, kind),
        jax.ShapeDtypeStruct((depth, 2, 2) + down.shape, kind),
        jax.ShapeDtypeStruct((2,) + cot_bf.shape, kind),
        jax.ShapeDtypeStruct((length, width), kind),
        jax.ShapeDtypeStruct((length, 3 * width), kind),
        jax.ShapeDtypeStruct((1, width), wide),
        jax.ShapeDtypeStruct((1, width), wide),
    ]
    held = (pairs, length, LANES)
    vmem = pl.BlockSpec(memory_space=pltpu.VMEM)
    hbm = pl.BlockSpec(memory_space=pl.ANY)
    flops = 14 * length * length * width
    return pl.pallas_call(
        lambda *refs: attention_kernel(groups, *refs),
        in_specs=[vmem] * 12,
        out_specs=[hbm] * 2 + [vmem] * 5,
        out_shape=shapes,
        scratch_shapes=[pltpu.VMEM(held, kind)] * 3
        + [pltpu.VMEM(held, wide)] * 2
        + [pltpu.VMEM((length, LANES), kind)]
        + [pltpu.VMEM((length, LANES), wide)] * 3
        + [
            pltpu.SemaphoreType.DMA((2, pairs, 4 * depth)),
            pltpu.SemaphoreType.DMA((2, pairs, 4 * depth)),
            pltpu.SemaphoreType.DMA((1,)),
            pltpu.SemaphoreType.DMA((1,)),
            pltpu.SemaphoreType.DMA((3,)),
        ],
        compiler_params=pltpu.CompilerParams(
            collective_id=2, has_side_effects=True, vmem_limit_bytes=56 * 1024 * 1024
        ),
        cost_estimate=pl.CostEstimate(
            flops=flops, bytes_accessed=48 * length * width, transcendentals=length * length * 8
        ),
        name="attention_all",
    )(up, down, cot_bf, proj_work, mixed_rows, q_bias[None], v_bias[None], *tables,
      segment_row[:, None], segment_row[None, :])


def square_sum(values):
    return jnp.sum(jnp.sum(values * values, axis=1, keepdims=True), axis=0, keepdims=True)


REDUCE_ITEMS = (
    ("proj", 0), ("up", 0), ("up", 1), ("down", 0), ("down", 1), ("qkv", 0), ("qkv", 1)
)


def reduce_kernel(groups, *refs):
    (
        down_in, up_in, proj_in, qkv_in, vec_in, rows_in, rows_sent, unit_in, inverse_in, gain_in,
        down_out, up_out, proj_out, qkv_out, vec_out, square_out, rows_out,
    ) = refs[:17]
    count = len(REDUCE_ITEMS)
    sets = [refs[17 + 9 * i : 26 + 9 * i] for i in range(count)]
    own, one, mid, two, cross, last, three, end, swap = zip(*sets)
    (
        vec_held, vec_come, tile_held, tile_come, rows_come, vec_sum,
        send_sem, recv_sem, vec_send, vec_recv, row_send, row_recv, local_sem,
    ) = refs[17 + 9 * count :]
    depth, z, y, c, x = place(groups)
    parts = dict(down=down_in, up=up_in, proj=proj_in, qkv=qkv_in)
    across = device(z, y, c, 1 - x)
    beside = device(z, 1 - y, c, x)
    twin = device(z, y, 1 - c, x)
    corner = device(z, x, c, y)
    far = [lax.rem(z + k, depth) for k in range(1, depth)]
    alongs = [device(zz, y, c, x) for zz in far]
    near = [
        device(z, yy, cc, xx)
        for xx in (x, 1 - x) for yy in (y, 1 - y) for cc in (c, 1 - c)
    ][1:]
    greet(near + alongs)

    def remote(src, dst, index, peer, sems=(send_sem, recv_sem)):
        return pltpu.make_async_remote_copy(
            src_ref=src, dst_ref=dst, send_sem=sems[0].at[index], recv_sem=sems[1].at[index],
            device_id=peer, device_id_type=MESH,
        )

    def wide(values):
        return values.astype(jnp.float32)

    vec_sems = (vec_send, vec_recv)
    vec_copies = []
    first, stays, second, third, fourth = {}, {}, {}, {}, {}
    for i, (name, piece) in enumerate(REDUCE_ITEMS):
        part = parts[name]
        first[i], stays[i] = [], []
        if name == "proj":
            moves = [(part.at[:, 1 - c], one[i], part.at[:, c], own[i])]
        else:
            size = own[i].shape[-1] // 2
            moves = []
            for side in range(2):
                start = side * part.shape[-1] // 2 + piece * size
                from_lanes, to_lanes = pl.ds(start, size), pl.ds(side * size, size)
                moves.append((
                    part.at[:, :, 1 - c, :, from_lanes], one[i].at[:, :, :, to_lanes],
                    part.at[:, :, c, :, from_lanes], own[i].at[:, :, :, to_lanes],
                ))
        for side, (theirs, there, mine, here) in enumerate(moves):
            first[i].append(remote(theirs, there, (i, side), twin))
            first[i][-1].start()
            stays[i].append(pltpu.make_async_copy(mine, here, local_sem.at[i, side]))
            stays[i][-1].start()
    rows_swap = remote(rows_sent, rows_come, 0, across, (row_send, row_recv))
    rows_swap.start()

    def rows_back():
        rows_swap.wait()
        vec_sum[...] = vec_in[...]
        gain = gain_in[...]

        @pl.loop(0, rows_in.shape[0] // 64)
        def _(step):
            part = pl.ds(pl.multiple_of(step * 64, 64), 64)
            upstream = rows_in[part, :] + wide(rows_come[part, :])
            unit = unit_in[part, :]
            scaled = upstream * gain
            mean_plain = jnp.mean(scaled, axis=-1, keepdims=True)
            mean_unit = jnp.mean(scaled * unit, axis=-1, keepdims=True)
            rows_out[part, :] = inverse_in[part, :] * (scaled - mean_plain - unit * mean_unit)
            vec_sum[0:1, :] += jnp.sum(upstream * unit, axis=0, keepdims=True)
            vec_sum[1:2, :] += jnp.sum(upstream, axis=0, keepdims=True)

        vec_copies.append(remote(vec_sum, vec_come.at[0], 0, twin, vec_sems))
        vec_copies[0].start()

    def step_one(i):
        name = REDUCE_ITEMS[i][0]
        for copy in first[i] + stays[i]:
            copy.wait()

        def body(zz, carry):
            if name == "proj":
                half = own[i].shape[2] // 2
                ours, theirs = half_lanes(y, half), half_lanes(1 - y, half)
                cross[i][zz] = (
                    wide(own[i][zz, :, theirs]) + wide(one[i][zz, :, theirs])
                ).astype(jnp.bfloat16)
                mid[i][zz] = wide(own[i][zz, :, ours]) + wide(one[i][zz, :, ours])
            else:
                cross[i][zz] = (
                    wide(own[i][zz, 1 - y]) + wide(one[i][zz, 1 - y])
                ).astype(jnp.bfloat16)
                mid[i][zz] = wide(own[i][zz, y]) + wide(one[i][zz, y])
            return carry

        lax.fori_loop(0, depth, body, 0)
        second[i] = remote(cross[i], two[i], (i, 2), beside)
        second[i].start()

    def step_two(i):
        second[i].wait()
        for k in range(1, depth):
            zz = far[k - 1]
            last[i][k - 1] = (mid[i][zz] + wide(two[i][zz])).astype(jnp.bfloat16)
            third[i, k] = remote(
                last[i].at[k - 1], three[i].at[k - 1], (i, 2 + k), alongs[k - 1]
            )
            third[i, k].start()

    def step_three(i):
        for k in range(1, depth):
            third[i, k].wait()
        total = mid[i][z] + wide(two[i][z])
        for k in range(1, depth):
            total = total + wide(three[i][k - 1])
        mid[i][0] = total
        if REDUCE_ITEMS[i][0] == "proj":
            end[i][...] = total.astype(jnp.bfloat16)
            fourth[i] = remote(end[i], swap[i], (i, depth + 2), corner)
            pl.when(x != y)(lambda: fourth[i].start())
        else:
            half = total.shape[1] // 2
            end[i][...] = mid[i][0, :, half_lanes(1 - x, half)].astype(jnp.bfloat16)
            fourth[i] = remote(end[i], swap[i], (i, depth + 2), across)
            fourth[i].start()

    def step_four(i):
        name, piece = REDUCE_ITEMS[i]
        if name == "proj":
            def swapped():
                fourth[i].wait()
                proj_out[...] = wide(swap[i][...])

            def kept():
                proj_out[...] = mid[i][0]

            pl.when(x != y)(swapped)
            pl.when(x == y)(kept)
            return square_sum(proj_out[...])
        fourth[i].wait()
        half = swap[i].shape[1]
        mine = mid[i][0, :, half_lanes(x, half)]
        theirs = wide(swap[i][...])
        if name == "down":
            size = mine.shape[0]
            lanes = slice(piece * half, (piece + 1) * half)
            down_out[pl.ds(pl.multiple_of(x * size, 8), size), lanes] = mine
            down_out[pl.ds(pl.multiple_of((1 - x) * size, 8), size), lanes] = theirs
        else:
            out = dict(up=up_out, qkv=qkv_out)[name]
            blocks = half // LANES
            for b in range(blocks):
                lanes = slice(b * LANES, (b + 1) * LANES)
                to = 2 * (piece * blocks + b)
                out[:, half_lanes(to + x, LANES)] = mine[:, lanes]
                out[:, half_lanes(to + 1 - x, LANES)] = theirs[:, lanes]
        return square_sum(mine) + square_sum(theirs)

    def vec_step(index, peers):
        for copy in vec_copies:
            copy.wait()
        vec_copies.clear()
        held = vec_sum[...] if index == 0 else vec_held[index - 1]
        vec_held[index] = held + vec_come[index]
        for k, peer in enumerate(peers):
            copy = remote(
                vec_held.at[index], vec_come.at[index + 1 + k], index + 1 + k, peer, vec_sems
            )
            copy.start()
            vec_copies.append(copy)

    step_one(0)
    step_one(1)
    squares = jnp.zeros((1, 1), jnp.float32)
    for t in range(count + 2):
        if t + 2 < count:
            step_one(t + 2)
        if t < count:
            step_two(t)
        if t == 2:
            rows_back()
        if t == 3:
            vec_step(0, [across])
        if t == 4:
            vec_step(1, [beside])
        if t == 5:
            vec_step(2, alongs)
        if 0 <= t - 1 < count:
            step_three(t - 1)
        if t == count:
            for copy in vec_copies:
                copy.wait()
            vec_total = vec_held[2]
            for k in range(depth - 1):
                vec_total = vec_total + vec_come[3 + k]
            vec_out[...] = vec_total
            vec_square = square_sum(vec_total)
        if 0 <= t - 2:
            squares = squares + step_four(t - 2)

    base = 3 + depth
    tile_held[0] = jnp.broadcast_to(squares, tile_held.shape[1:])
    copies = [
        remote(tile_held.at[0], tile_come.at[k], base + k, peer, vec_sems)
        for k, peer in enumerate(alongs)
    ]
    for copy in copies:
        copy.start()
    for copy in copies:
        copy.wait()
    tile = tile_held[0]
    for k in range(depth - 1):
        tile = tile + tile_come[k]
    tile_held[1] = tile
    copies = [
        remote(tile_held.at[1], tile_come.at[depth - 1 + k], base + depth - 1 + k, peer, vec_sems)
        for k, peer in enumerate(near)
    ]
    for copy in copies:
        copy.start()
    for copy in copies:
        copy.wait()
    for k in range(len(near)):
        tile = tile + tile_come[depth - 1 + k]
    square_out[...] = tile + vec_square


def reduce_all(groups, down_part, up_part, proj_part, qkv_part, vec_part, row_args):
    depth = groups // 4
    wide, kind = jnp.float32, jnp.bfloat16

    def grid_of(part):
        return part.reshape(depth, 2, 2, part.shape[0] // groups, part.shape[1])

    down, up, qkv = grid_of(down_part), grid_of(up_part), grid_of(qkv_part)
    proj = proj_part.reshape(depth, 2, proj_part.shape[0] // depth // 2, proj_part.shape[1])
    parts = dict(down=down, up=up, proj=proj, qkv=qkv)
    scratch = []
    for name, _ in REDUCE_ITEMS:
        rows, columns = parts[name].shape[-2:]
        block = (rows, columns // 2)
        whole = name == "proj"
        held = (depth, rows, columns) if whole else (depth, 2) + block
        final = block if whole else (rows, columns // 4)
        scratch += [
            pltpu.VMEM(held, kind), pltpu.VMEM(held, kind),
            pltpu.VMEM((depth,) + block, wide), pltpu.VMEM((depth,) + block, kind),
            pltpu.VMEM((depth,) + block, kind), pltpu.VMEM((depth - 1,) + block, kind),
            pltpu.VMEM((depth - 1,) + block, kind), pltpu.VMEM(final, kind),
            pltpu.VMEM(final, kind),
        ]
    near, count = 7, len(REDUCE_ITEMS)
    scratch += [
        pltpu.VMEM((3,) + vec_part.shape, wide),
        pltpu.VMEM((2 + depth,) + vec_part.shape, wide),
        pltpu.VMEM((2, 8, LANES), wide),
        pltpu.VMEM((depth - 1 + near, 8, LANES), wide),
        pltpu.VMEM(row_args[1].shape, kind),
        pltpu.VMEM(vec_part.shape, wide),
        pltpu.SemaphoreType.DMA((count, depth + 3)),
        pltpu.SemaphoreType.DMA((count, depth + 3)),
        pltpu.SemaphoreType.DMA((2 + 2 * depth + near,)),
        pltpu.SemaphoreType.DMA((2 + 2 * depth + near,)),
        pltpu.SemaphoreType.DMA((1,)),
        pltpu.SemaphoreType.DMA((1,)),
        pltpu.SemaphoreType.DMA((count, 2)),
    ]
    shapes = [
        jax.ShapeDtypeStruct((2 * down.shape[-2], down.shape[-1] // 2), wide),
        jax.ShapeDtypeStruct(up.shape[-2:], wide),
        jax.ShapeDtypeStruct((proj.shape[-2], proj.shape[-1] // 2), wide),
        jax.ShapeDtypeStruct(qkv.shape[-2:], wide),
        jax.ShapeDtypeStruct(vec_part.shape, wide),
        jax.ShapeDtypeStruct((8, LANES), wide),
        jax.ShapeDtypeStruct(row_args[0].shape, wide),
    ]
    vmem = pl.BlockSpec(memory_space=pltpu.VMEM)
    hbm = pl.BlockSpec(memory_space=pl.ANY)
    return pl.pallas_call(
        lambda *refs: reduce_kernel(groups, *refs),
        in_specs=[hbm] * 4 + [vmem] * 6,
        out_specs=[vmem] * 7,
        out_shape=shapes,
        scratch_shapes=scratch,
        compiler_params=pltpu.CompilerParams(
            collective_id=1, has_side_effects=True, vmem_limit_bytes=56 * 1024 * 1024
        ),
        cost_estimate=pl.CostEstimate(
            flops=0, bytes_accessed=50 * down_part.size, transcendentals=0
        ),
        name="reduce_all",
    )(down, up, proj, qkv, vec_part, *row_args)


def adam_kernel(square_ref, *refs):
    count = len(refs) // 6
    norm_limit = math.sqrt(NPARAM)
    clip = norm_limit / jnp.maximum(jnp.sqrt(square_ref[0:1, 0:1]), norm_limit)
    fix_first = 1.0 - math.pow(beta_one, STEP)
    fix_second = 1.0 - math.pow(beta_two, STEP)
    ins, outs = refs[: 3 * count], refs[3 * count :]
    for index in range(count):
        weight_ref, moment_ref, grad_ref = ins[3 * index : 3 * index + 3]
        grad_out, weight_out, moment_out = outs[3 * index : 3 * index + 3]
        grad, weight = grad_ref[...], weight_ref[...]
        clipped = grad * clip
        first_new = beta_one * moment_ref[0] + (1.0 - beta_one) * clipped
        second_new = beta_two * moment_ref[1] + (1.0 - beta_two) * clipped * clipped
        direction = first_new / fix_first / (jnp.sqrt(second_new / fix_second) + adam_eps)
        grad_out[...] = grad
        weight_out[...] = weight - learn_rate * (direction + decay_rate * weight)
        moment_out[0] = first_new
        moment_out[1] = second_new


def adam_all(square, weights, moments, grads):
    steps = 4
    in_specs = [pl.BlockSpec(square.shape, lambda i: (0, 0))]
    out_specs, shapes, ins = [], [], [square]
    for weight, moment, grad in zip(weights, moments, grads):
        rows, columns = weight.shape
        if rows % (8 * steps) == 0:
            flat = pl.BlockSpec((rows // steps, columns), lambda i: (i, 0))
            both = pl.BlockSpec((2, rows // steps, columns), lambda i: (0, i, 0))
        else:
            flat = pl.BlockSpec((rows, columns), lambda i: (0, 0))
            both = pl.BlockSpec((2, rows, columns), lambda i: (0, 0, 0))
        in_specs += [flat, both, flat]
        out_specs += [flat, flat, both]
        shapes += [
            jax.ShapeDtypeStruct(grad.shape, grad.dtype),
            jax.ShapeDtypeStruct(weight.shape, weight.dtype),
            jax.ShapeDtypeStruct(moment.shape, moment.dtype),
        ]
        ins += [weight, moment, grad]
    size = sum(weight.size for weight in weights)
    results = pl.pallas_call(
        adam_kernel,
        grid=(steps,),
        in_specs=in_specs,
        out_specs=out_specs,
        out_shape=shapes,
        cost_estimate=pl.CostEstimate(
            flops=20 * size, bytes_accessed=32 * size, transcendentals=2 * size
        ),
        name="adam_all",
    )(*ins)
    return results[0::3], results[1::3], results[2::3]


def swap_shard(piece):
    return lax.ppermute(piece, "shard", [(0, 1), (1, 0)])


def pick(array, index, axis):
    return lax.dynamic_index_in_dim(array, index, axis=axis, keepdims=False)


def sum_halves(partial, member, local_rows):
    halves = partial.reshape(2, local_rows, partial.shape[-1])
    received = swap_shard(pick(halves, 1 - member, 0).astype(jnp.bfloat16))
    return pick(halves, member, 0) + received.astype(jnp.float32)


def spread(values, width, member):
    blocks = values.reshape(-1, 1, width)
    chosen = jnp.arange(2, dtype=jnp.int32)[None, :, None] == member
    return jnp.where(chosen, blocks, 0.0).reshape(-1)


def rolled(rows, cosine, down_sine, up_sine):
    width = rows.shape[1]
    lower = pltpu.roll(rows, width - ROT // 2, 1)
    upper = pltpu.roll(rows, ROT // 2, 1)
    return rows * cosine + lower * down_sine + upper * up_sine


def split_pair(rows):
    lanes = lax.broadcasted_iota(jnp.int32, rows.shape, 1)
    return (
        jnp.where(lanes < HD, rows, jnp.zeros_like(rows)),
        jnp.where(lanes < HD, jnp.zeros_like(rows), rows),
    )


def block_mask(seg_column, seg_row, start, size, extent):
    rows = start + lax.broadcasted_iota(jnp.int32, (size, extent), 0)
    keys = lax.broadcasted_iota(jnp.int32, (size, extent), 1)
    same = seg_column[start : start + size, :] == seg_row[:, :extent]
    return same & (keys <= rows)


def lane_tables(positions):
    dims = jnp.arange(2 * HD, dtype=jnp.int32) % HD
    half_dims = ROT // 2
    exponent = (dims % half_dims).astype(jnp.float32) * (2.0 / ROT)
    inverse_freq = jnp.exp(-math.log(rope_base) * exponent)
    angles = positions.astype(jnp.float32)[:, None] * inverse_freq[None, :]
    sine = jnp.sin(angles)
    return (
        jnp.where(dims[None] < ROT, jnp.cos(angles), 1.0),
        jnp.where(dims[None] < half_dims, -sine, 0.0),
        jnp.where((dims[None] >= half_dims) & (dims[None] < ROT), sine, 0.0),
    )


def shards(
    tokens,
    out_grad,
    segment_ids,
    qkv_weight,
    proj_weight,
    up_weight,
    down_weight,
    vectors,
    qkv_moments,
    proj_moments,
    up_moments,
    down_moments,
    vector_moments,
):
    groups = lax.axis_size("dp")
    members = lax.axis_size("shard")
    head_count = D // HD
    if members != 2 or groups != head_count:
        return plain_shards(
            tokens,
            out_grad,
            segment_ids,
            qkv_weight,
            proj_weight,
            up_weight,
            down_weight,
            vectors,
            qkv_moments,
            proj_moments,
            up_moments,
            down_moments,
            vector_moments,
        )
    member = lax.axis_index("shard")
    group = lax.axis_index("dp")
    half = D // 2
    local_rows = tokens.shape[0]
    vec_width = vectors.shape[1]
    pairs = half // LANES

    vec_all, qkv_all, proj_all, up_piece, down_piece, unit_all, unit, inverse = gather_first(
        groups, tokens, vectors, qkv_weight, proj_weight, up_weight, down_weight
    )
    vec_work = (
        vec_all.reshape(2 * groups, 16, LANES)[:, :VROWS, :vec_width]
        .transpose(1, 0, 2)
        .reshape(VROWS, D)
        .astype(jnp.float32)
    )
    qkv_work = qkv_all.reshape(D, 3 * half)
    proj_work = proj_all.reshape(half, D)
    unit_rows = unit_all.reshape(2 * local_rows, D).astype(jnp.float32)
    hidden_one = (unit_rows * vec_work[0] + vec_work[1]).astype(jnp.bfloat16)
    hidden_two = (unit_rows * vec_work[2] + vec_work[3]).astype(jnp.bfloat16)

    segment_row = segment_ids[0]
    positions = doc_positions(segment_row)
    tables = lane_tables(positions)

    q_bias = pick(vec_work[4].reshape(pairs, 2, LANES), member, 1).reshape(-1)
    v_bias = pick(vec_work[5].reshape(pairs, 2, LANES), member, 1).reshape(-1)
    up_bias = pick(vec_work[8:].reshape(groups, 2, LANES), member, 1).reshape(-1)

    mixed_rows = jnp.dot(hidden_one, qkv_work, preferred_element_type=jnp.float32)
    up_all, down_all, cot_all, attended_bf, grad_mixed_bf, q_bias_part, v_bias_part = (
        attention_all(
            groups, up_piece, down_piece, out_grad.astype(jnp.bfloat16), proj_work, mixed_rows,
            q_bias, v_bias, tables, segment_row,
        )
    )
    up_work = up_all.reshape(D, FF // 2)
    down_work = down_all.reshape(FF // 2, D)
    cot_bf = cot_all.reshape(2 * local_rows, D)
    proj_part = transposed_times(attended_bf, cot_bf).astype(jnp.bfloat16)
    q_bias_part, v_bias_part = q_bias_part[0], v_bias_part[0]
    qkv_part = transposed_times(hidden_one, grad_mixed_bf).astype(jnp.bfloat16)
    rows_partial = times_transposed(grad_mixed_bf, qkv_work)

    pre_act = jnp.dot(hidden_two, up_work, preferred_element_type=jnp.float32) + up_bias
    act_values, act_slope = gelu_pair(pre_act)
    act_bf = act_values.astype(jnp.bfloat16)
    grad_pre = times_transposed(cot_bf, down_work) * act_slope
    grad_pre_bf = grad_pre.astype(jnp.bfloat16)
    down_part = transposed_times(act_bf, cot_bf).astype(jnp.bfloat16)
    up_part = transposed_times(hidden_two, grad_pre_bf).astype(jnp.bfloat16)

    out_partial = jnp.dot(
        attended_bf, proj_work, preferred_element_type=jnp.float32
    ) + jnp.dot(act_bf, down_work, preferred_element_type=jnp.float32)
    block_out = (
        tokens + sum_halves(out_partial, member, local_rows) + vec_work[6] + vec_work[7]
    )
    rows_two, ln2_gain_part, ln2_bias_part = norm_back(
        sum_halves(times_transposed(grad_pre_bf, up_work), member, local_rows),
        unit,
        inverse,
        vec_work[2],
    )
    cot_sum = jnp.sum(out_grad, axis=0)
    zero_row = jnp.zeros_like(cot_sum)
    base_grad = out_grad + rows_two
    vec_part = jnp.concatenate(
        [
            jnp.stack(
                [
                    zero_row,
                    zero_row,
                    ln2_gain_part,
                    ln2_bias_part,
                    spread(q_bias_part, LANES, member),
                    spread(v_bias_part, LANES, member),
                    cot_sum,
                    cot_sum,
                ]
            ),
            spread(jnp.sum(grad_pre, axis=0), LANES, member).reshape(FF // D, D),
            jnp.zeros((16 - VROWS, D), jnp.float32),
        ],
        axis=0,
    )
    halves = rows_partial.reshape(2, local_rows, D)
    down_grad, up_grad, proj_grad, qkv_grad, vec_sum, square, rows_one = reduce_all(
        groups, down_part, up_part, proj_part, qkv_part, vec_part,
        (
            pick(halves, member, 0), pick(halves, 1 - member, 0).astype(jnp.bfloat16),
            unit, inverse, vec_work[0:1],
        ),
    )
    tokens_grad = base_grad + rows_one
    vectors_grad = lax.dynamic_slice_in_dim(
        vec_sum[:VROWS], (group * 2 + member) * vec_width, vec_width, axis=1
    )
    grads, weights_new, moments_new = adam_all(
        square,
        (qkv_weight, proj_weight, up_weight, down_weight, vectors),
        (qkv_moments, proj_moments, up_moments, down_moments, vector_moments),
        (qkv_grad, proj_grad, up_grad, down_grad, vectors_grad),
    )
    return (block_out, tokens_grad, *grads, *weights_new, *moments_new)


def solution(mesh):
    placed = (
        P(("dp", "shard"), None),
        P(("dp", "shard"), None),
        P("dp", None),
        P("dp", "shard"),
        P("dp", "shard"),
        P("dp", "shard"),
        P("dp", "shard"),
        P(None, ("dp", "shard")),
        P(None, "dp", "shard"),
        P(None, "dp", "shard"),
        P(None, "dp", "shard"),
        P(None, "dp", "shard"),
        P(None, None, ("dp", "shard")),
    )
    return jax.shard_map(
        shards,
        mesh=mesh,
        in_specs=placed,
        out_specs=(
            P(("dp", "shard"), None),
            P(("dp", "shard"), None),
            P("dp", "shard"),
            P("dp", "shard"),
            P("dp", "shard"),
            P("dp", "shard"),
            P(None, ("dp", "shard")),
            P("dp", "shard"),
            P("dp", "shard"),
            P("dp", "shard"),
            P("dp", "shard"),
            P(None, ("dp", "shard")),
            P(None, "dp", "shard"),
            P(None, "dp", "shard"),
            P(None, "dp", "shard"),
            P(None, "dp", "shard"),
            P(None, None, ("dp", "shard")),
        ),
        check_vma=False,
    )
```

```python
import math

import jax
import jax.numpy as jnp
from jax import lax
from jax.experimental import pallas as pl
from jax.experimental.pallas import tpu as pltpu
from jax.sharding import PartitionSpec as P

D = 1024
FF = 4096
HD = 64
ROT = 16
STEP = 4
VROWS = 12
NPARAM = 12595200


ln_eps = 1e-05
beta_one = 0.9
beta_two = 0.95
learn_rate = 0.005
decay_rate = 0.01
adam_eps = 1e-08
rope_base = 10000.0


def norm_rows(inputs, gain_row, bias_row):
    center = inputs - jnp.mean(inputs, axis=-1, keepdims=True)
    inverse = lax.rsqrt(jnp.mean(center * center, axis=-1, keepdims=True) + ln_eps)
    unit_rows = center * inverse
    return (unit_rows * gain_row + bias_row, unit_rows, inverse)


def norm_back(upstream, unit_rows, inverse, gain_row):
    gain_grad = jnp.sum(upstream * unit_rows, axis=0)
    bias_grad = jnp.sum(upstream, axis=0)
    scaled_up = upstream * gain_row
    mean_plain = jnp.mean(scaled_up, axis=-1, keepdims=True)
    mean_unit = jnp.mean(scaled_up * unit_rows, axis=-1, keepdims=True)
    return (inverse * (scaled_up - mean_plain - unit_rows * mean_unit), gain_grad, bias_grad)


def doc_positions(segment_row):
    length_all = segment_row.shape[0]
    indices = jnp.arange(length_all, dtype=jnp.int32)
    starting = jnp.concatenate(
        [jnp.ones((1,), dtype=jnp.bool_), segment_row[1:] != segment_row[:-1]]
    )
    begins = lax.cummax(jnp.where(starting, indices, 0), axis=0)
    return indices - begins


def rotary_tables(positions, rot_dims):
    half_dims = rot_dims // 2
    exponent = jnp.arange(half_dims, dtype=jnp.float32) * (2.0 / rot_dims)
    inverse_freq = jnp.exp(-math.log(rope_base) * exponent)
    angles = positions.astype(jnp.float32)[:, None] * inverse_freq[None, :]
    return (jnp.cos(angles)[:, None, :], jnp.sin(angles)[:, None, :])


def rotate(head_rows, cosine_table, sine_table):
    half_dims = cosine_table.shape[-1]
    lower_half = head_rows[..., :half_dims]
    upper_half = head_rows[..., half_dims : 2 * half_dims]
    return jnp.concatenate(
        [
            lower_half * cosine_table - upper_half * sine_table,
            upper_half * cosine_table + lower_half * sine_table,
            head_rows[..., 2 * half_dims :],
        ],
        axis=-1,
    )


def gelu_pair(pre_act):
    normal_cdf = 0.5 * (1.0 + lax.erf(pre_act * (1.0 / math.sqrt(2.0))))
    density = jnp.exp(-0.5 * pre_act * pre_act) * (1.0 / math.sqrt(2.0 * math.pi))
    return (pre_act * normal_cdf, normal_cdf + pre_act * density)


def times_transposed(left, right):
    return lax.dot_general(
        left, right, (((1,), (1,)), ((), ())), preferred_element_type=jnp.float32
    )


def transposed_times(left, right):
    return lax.dot_general(
        left, right, (((0,), (0,)), ((), ())), preferred_element_type=jnp.float32
    )


def adam_update(weight, moments, gradient, clip_factor):
    clipped = gradient * clip_factor
    first_new = beta_one * moments[0] + (1.0 - beta_one) * clipped
    second_new = beta_two * moments[1] + (1.0 - beta_two) * clipped * clipped
    fix_first = 1.0 - math.pow(beta_one, STEP)
    fix_second = 1.0 - math.pow(beta_two, STEP)
    direction = first_new / fix_first / (jnp.sqrt(second_new / fix_second) + adam_eps)
    return (
        weight - learn_rate * (direction + decay_rate * weight),
        jnp.stack([first_new, second_new]),
    )


def plain_shards(
    tokens,
    out_grad,
    segment_ids,
    qkv_weight,
    proj_weight,
    up_weight,
    down_weight,
    vectors,
    qkv_moments,
    proj_moments,
    up_moments,
    down_moments,
    vector_moments,
):
    columns_full = (
        lax.all_gather(qkv_weight.astype(jnp.bfloat16), "shard", axis=1, tiled=True),
        lax.all_gather(proj_weight.astype(jnp.bfloat16), "shard", axis=1, tiled=True),
        lax.all_gather(up_weight.astype(jnp.bfloat16), "shard", axis=1, tiled=True),
        lax.all_gather(down_weight.astype(jnp.bfloat16), "shard", axis=1, tiled=True),
        lax.all_gather(vectors.astype(jnp.bfloat16), "shard", axis=1, tiled=True),
    )
    qkv_work, proj_work, up_work, down_work, vec_bf = (
        lax.all_gather(columns_full[0], "dp", axis=0, tiled=True),
        lax.all_gather(columns_full[1], "dp", axis=0, tiled=True),
        lax.all_gather(columns_full[2], "dp", axis=0, tiled=True),
        lax.all_gather(columns_full[3], "dp", axis=0, tiled=True),
        lax.all_gather(columns_full[4], "dp", axis=1, tiled=True),
    )
    vec_work = vec_bf.astype(jnp.float32)
    head_count = D // HD
    score_scale = 1.0 / math.sqrt(HD)
    local_rows = tokens.shape[0]
    segment_row = segment_ids[0]
    length_all = segment_row.shape[0]
    row_start = lax.axis_index("shard") * local_rows
    query_index = row_start + jnp.arange(local_rows, dtype=jnp.int32)
    query_segment = lax.dynamic_slice_in_dim(segment_row, row_start, local_rows)
    positions = lax.dynamic_slice_in_dim(doc_positions(segment_row), row_start, local_rows)
    normed_one, unit_one, inverse_one = norm_rows(tokens, vec_work[0], vec_work[1])
    hidden_one = normed_one.astype(jnp.bfloat16)
    mixed_rows = jnp.dot(hidden_one, qkv_work, preferred_element_type=jnp.float32)
    query_raw = (mixed_rows[:, :D] + vec_work[4]).reshape(local_rows, head_count, HD)
    key_raw = mixed_rows[:, D : 2 * D].reshape(local_rows, head_count, HD)
    value_bf = (mixed_rows[:, 2 * D :] + vec_work[5]).astype(jnp.bfloat16)
    cosine_table, sine_table = rotary_tables(positions, ROT)
    query_bf = rotate(query_raw, cosine_table, sine_table).astype(jnp.bfloat16)
    key_bf = rotate(key_raw, cosine_table, sine_table).astype(jnp.bfloat16).reshape(local_rows, D)
    key_piece = lax.all_gather(key_bf, "shard", axis=0, tiled=True)
    value_piece = lax.all_gather(value_bf, "shard", axis=0, tiled=True)
    piece_rows = key_piece.shape[0]
    key_heads = key_piece.reshape(piece_rows, head_count, HD)
    value_heads = value_piece.reshape(piece_rows, head_count, HD)
    key_index = jnp.arange(piece_rows, dtype=jnp.int32)
    allowed = (segment_row[None, :] == query_segment[:, None]) & (
        key_index[None, :] <= query_index[:, None]
    )
    scores = (
        jnp.einsum("qhd,khd->hqk", query_bf, key_heads, preferred_element_type=jnp.float32)
        * score_scale
    )
    exp_scores = jnp.where(allowed[None], jnp.exp(scores), 0.0)
    numerator = jnp.einsum(
        "hqk,khd->qhd",
        exp_scores.astype(jnp.bfloat16),
        value_heads,
        preferred_element_type=jnp.float32,
    )
    numerator, totals = (numerator, jnp.sum(exp_scores, axis=-1))
    attended = numerator / jnp.transpose(totals)[:, :, None]
    log_totals = jnp.log(totals)
    attended_bf = attended.reshape(local_rows, D).astype(jnp.bfloat16)
    proj_out = jnp.dot(attended_bf, proj_work, preferred_element_type=jnp.float32) + vec_work[6]
    normed_two, unit_two, inverse_two = norm_rows(tokens, vec_work[2], vec_work[3])
    hidden_two = normed_two.astype(jnp.bfloat16)
    pre_act = jnp.dot(hidden_two, up_work, preferred_element_type=jnp.float32) + vec_work[
        8:
    ].reshape(FF)
    act_values, act_slope = gelu_pair(pre_act)
    act_bf = act_values.astype(jnp.bfloat16)
    block_out = (
        tokens
        + proj_out
        + (jnp.dot(act_bf, down_work, preferred_element_type=jnp.float32) + vec_work[7])
    )
    cot_bf = out_grad.astype(jnp.bfloat16)
    down_part = transposed_times(act_bf, cot_bf)
    proj_part = transposed_times(attended_bf, cot_bf)
    cot_sum = jnp.sum(out_grad, axis=0)
    grad_pre = times_transposed(cot_bf, down_work) * act_slope
    grad_pre_bf = grad_pre.astype(jnp.bfloat16)
    up_part = transposed_times(hidden_two, grad_pre_bf)
    rows_two, ln2_gain_part, ln2_bias_part = norm_back(
        times_transposed(grad_pre_bf, up_work), unit_two, inverse_two, vec_work[2]
    )
    grad_att_bf = (
        times_transposed(cot_bf, proj_work).astype(jnp.bfloat16).reshape(local_rows, head_count, HD)
    )
    keys_all, values_all = (
        lax.all_gather(key_bf, "shard", axis=0, tiled=True),
        lax.all_gather(value_bf, "shard", axis=0, tiled=True),
    )
    key_heads = keys_all.reshape(length_all, head_count, HD)
    value_heads = values_all.reshape(length_all, head_count, HD)
    key_index = jnp.arange(length_all, dtype=jnp.int32)
    allowed = (segment_row[None, :] == query_segment[:, None]) & (
        key_index[None, :] <= query_index[:, None]
    )
    scores = (
        jnp.einsum("qhd,khd->hqk", query_bf, key_heads, preferred_element_type=jnp.float32)
        * score_scale
    )
    probability = jnp.where(allowed[None], jnp.exp(scores - log_totals[:, :, None]), 0.0)
    grad_prob = jnp.einsum(
        "qhd,khd->hqk", grad_att_bf, value_heads, preferred_element_type=jnp.float32
    )
    row_delta = jnp.transpose(jnp.sum(grad_att_bf.astype(jnp.float32) * attended, axis=-1))
    grad_score = (probability * (grad_prob - row_delta[:, :, None]) * score_scale).astype(
        jnp.bfloat16
    )
    grad_query = jnp.einsum(
        "hqk,khd->qhd", grad_score, key_heads, preferred_element_type=jnp.float32
    )
    grad_query = rotate(grad_query, cosine_table, -sine_table).reshape(local_rows, D)
    key_terms = jnp.einsum(
        "hqk,qhd->khd", grad_score, query_bf, preferred_element_type=jnp.float32
    ).reshape(length_all, D)
    value_terms = jnp.einsum(
        "hqk,qhd->khd",
        probability.astype(jnp.bfloat16),
        grad_att_bf,
        preferred_element_type=jnp.float32,
    ).reshape(length_all, D)
    key_value_grad = lax.psum_scatter(
        jnp.concatenate([key_terms, value_terms], axis=1), "shard", scatter_dimension=0, tiled=True
    )
    grad_key = rotate(
        key_value_grad[:, :D].reshape(local_rows, head_count, HD), cosine_table, -sine_table
    ).reshape(local_rows, D)
    grad_value = key_value_grad[:, D:]
    grad_mixed_bf = jnp.concatenate([grad_query, grad_key, grad_value], axis=1).astype(jnp.bfloat16)
    qkv_part = transposed_times(hidden_one, grad_mixed_bf)
    rows_one, ln1_gain_part, ln1_bias_part = norm_back(
        times_transposed(grad_mixed_bf, qkv_work), unit_one, inverse_one, vec_work[0]
    )
    tokens_grad = out_grad + rows_one + rows_two
    vec_part = jnp.concatenate(
        [
            jnp.stack(
                [
                    ln1_gain_part,
                    ln1_bias_part,
                    ln2_gain_part,
                    ln2_bias_part,
                    jnp.sum(grad_query, axis=0),
                    jnp.sum(grad_value, axis=0),
                    cot_sum,
                    cot_sum,
                ]
            ),
            jnp.sum(grad_pre, axis=0).reshape(FF // D, D),
        ],
        axis=0,
    )
    groups = lax.axis_size("dp")
    members = lax.axis_size("shard")
    owners = groups * members
    vec_split = vec_part.reshape(VROWS, groups, members, D // owners)
    group_sums = (
        lax.psum_scatter(qkv_part, "shard", scatter_dimension=1, tiled=True),
        lax.psum_scatter(proj_part, "shard", scatter_dimension=1, tiled=True),
        lax.psum_scatter(up_part, "shard", scatter_dimension=1, tiled=True),
        lax.psum_scatter(down_part, "shard", scatter_dimension=1, tiled=True),
        lax.psum_scatter(vec_split, "shard", scatter_dimension=2, tiled=True),
    )
    owner_sums = (
        lax.psum_scatter(group_sums[0], "dp", scatter_dimension=0, tiled=True),
        lax.psum_scatter(group_sums[1], "dp", scatter_dimension=0, tiled=True),
        lax.psum_scatter(group_sums[2], "dp", scatter_dimension=0, tiled=True),
        lax.psum_scatter(group_sums[3], "dp", scatter_dimension=0, tiled=True),
        lax.psum_scatter(group_sums[4], "dp", scatter_dimension=1, tiled=True),
    )
    qkv_grad = owner_sums[0]
    proj_grad = owner_sums[1]
    up_grad = owner_sums[2]
    down_grad = owner_sums[3]
    vectors_grad = owner_sums[4].reshape(VROWS, D // owners)
    local_square = (
        jnp.sum(qkv_grad * qkv_grad)
        + jnp.sum(proj_grad * proj_grad)
        + jnp.sum(up_grad * up_grad)
        + jnp.sum(down_grad * down_grad)
        + jnp.sum(vectors_grad * vectors_grad)
    )
    square_total = lax.psum(local_square, ("dp", "shard"))
    norm_limit = math.sqrt(NPARAM)
    clip_factor = norm_limit / jnp.maximum(jnp.sqrt(square_total), norm_limit)
    qkv_new, qkv_moments_new = adam_update(qkv_weight, qkv_moments, qkv_grad, clip_factor)
    proj_new, proj_moments_new = adam_update(proj_weight, proj_moments, proj_grad, clip_factor)
    up_new, up_moments_new = adam_update(up_weight, up_moments, up_grad, clip_factor)
    down_new, down_moments_new = adam_update(down_weight, down_moments, down_grad, clip_factor)
    vectors_new, vector_moments_new = adam_update(
        vectors, vector_moments, vectors_grad, clip_factor
    )
    return (
        block_out,
        tokens_grad,
        qkv_grad,
        proj_grad,
        up_grad,
        down_grad,
        vectors_grad,
        qkv_new,
        proj_new,
        up_new,
        down_new,
        vectors_new,
        qkv_moments_new,
        proj_moments_new,
        up_moments_new,
        down_moments_new,
        vector_moments_new,
    )

MESH = pl.DeviceIdType.MESH
LANES = 128
UP_PIECES = 4
UP_EARLY = 2


def place(groups):
    group = lax.axis_index("dp")
    depth = groups // 4
    return depth, group // 4, lax.rem(group // 2, 2), lax.rem(group, 2), lax.axis_index("shard")


def device(z, y, c, x):
    return (z * 4 + y * 2 + c, x)


def greet(peers):
    barrier = pltpu.get_barrier_semaphore()
    for peer in peers:
        pl.semaphore_signal(barrier, inc=1, device_id=peer, device_id_type=MESH)
    pl.semaphore_wait(barrier, len(peers))


def half_lanes(member, width):
    return pl.ds(pl.multiple_of(member * width, LANES), width)


def gather_kernel(
    groups,
    tokens_in, vec_in, qkv_in, proj_in, up_in, down_in,
    vec_out, qkv_out, proj_out, up_out, down_out, up_early, rows_out, unit_out, inverse_out,
    vec_piece, qkv_keep, qkv_send, proj_piece, up_keep, up_send, down_keep, down_send, unit_piece,
    send_sem, recv_sem, swap_send, swap_recv, local_sem,
):
    depth, z, y, c, x = place(groups)
    kind = jnp.bfloat16
    across = device(z, y, c, 1 - x)
    beside = device(z, 1 - y, c, x)
    twin = device(z, y, 1 - c, x)
    corner = device(z, x, c, y)
    far = [lax.rem(z + k, depth) for k in range(1, depth)]
    back = [lax.rem(z + depth - k, depth) for k in range(depth)]
    greet(
        [across, beside, twin, device(z, 1 - y, c, 1 - x)] + [device(zz, y, c, x) for zz in far]
    )

    def remote(src, dst, index, peer, sems=(send_sem, recv_sem)):
        return pltpu.make_async_remote_copy(
            src_ref=src, dst_ref=dst, send_sem=sems[0].at[index], recv_sem=sems[1].at[index],
            device_id=peer, device_id_type=MESH,
        )

    def block(item, zz, yy, cc):
        if item == "vec":
            return vec_out.at[zz, yy, cc]
        if item == "proj":
            return proj_out.at[zz, cc, :, half_lanes(yy, proj_out.shape[3] // 2)]
        name, half = item
        if name == "up":
            size = up_early.shape[3] // UP_PIECES
            return up_early.at[zz, yy, cc, pl.ds(half * size, size)]
        size = qkv_out.shape[3] // 2
        return qkv_out.at[zz, yy, cc, pl.ds(half * size, size)]

    def held(item):
        if item[0] == "up":
            size = up_out.shape[0] // UP_PIECES
            return up_out.at[pl.ds(item[1] * size, size)]
        return block(item, z, y, c)

    def split(source, keep, sent):
        for b in range(keep.shape[1] // LANES):
            lanes = slice(b * LANES, (b + 1) * LANES)
            keep[:, lanes] = source[:, half_lanes(2 * b + x, LANES)].astype(kind)
            sent[:, lanes] = source[:, half_lanes(2 * b + 1 - x, LANES)].astype(kind)

    swap_sems = (swap_send, swap_recv)
    swaps, stays = [], []

    def swap(keep, sent, target):
        index = len(swaps)
        swaps.append(remote(sent, target, index, across, swap_sems))
        stays.append(pltpu.make_async_copy(keep, target, local_sem.at[index]))
        swaps[-1].start()
        stays[-1].start()

    split(qkv_in, qkv_keep, qkv_send)
    swap(qkv_keep, qkv_send, qkv_out.at[z, y, c, :, half_lanes(x, qkv_keep.shape[1])])
    vec_piece[...] = jnp.zeros_like(vec_piece)
    vec_piece[: vec_in.shape[0], : vec_in.shape[1]] = vec_in[...].astype(kind)
    swap(vec_piece, vec_piece, vec_out.at[z, y, c, x])
    proj_piece[...] = proj_in[...].astype(kind)
    proj_move = remote(
        proj_piece, proj_out.at[z, c, :, half_lanes(x, proj_out.shape[3] // 2)], 5, corner,
        swap_sems,
    )
    proj_stay = pltpu.make_async_copy(proj_piece, block("proj", z, y, c), local_sem.at[5])
    pl.when(x != y)(lambda: proj_move.start())
    pl.when(x == y)(lambda: proj_stay.start())

    @pl.loop(0, tokens_in.shape[0] // 64)
    def _(step):
        part = pl.ds(pl.multiple_of(step * 64, 64), 64)
        rows = tokens_in[part, :]
        center = rows - jnp.mean(rows, axis=-1, keepdims=True)
        inverse = lax.rsqrt(jnp.mean(center * center, axis=-1, keepdims=True) + ln_eps)
        unit = center * inverse
        unit_out[part, :] = unit
        inverse_out[part, :] = inverse
        unit_piece[part, :] = unit.astype(kind)

    items = ("vec", ("qkv", 0), ("qkv", 1), "proj") + tuple(
        ("up", early) for early in range(UP_EARLY)
    )
    along, over, pair = {}, {}, {}

    def launch(a, item):
        mine, there = held(item), block(item, z, y, c)
        for k in range(1, depth):
            along[item, k] = remote(mine, there, (a, k), device(far[k - 1], y, c, x))
            along[item, k].start()
        over[item, 0] = remote(mine, there, (a, depth), beside)
        over[item, 0].start()
        pair[item, 0, 0] = remote(mine, there, (a, 2 * depth), twin)
        pair[item, 0, 0].start()

    for index in range(2):
        stays[index].wait()
        swaps[index].wait()
    for a in range(3):
        launch(a, items[a])
    split(up_in, up_keep, up_send)
    swap(up_keep, up_send, up_out.at[:, half_lanes(x, up_keep.shape[1])])
    swap(unit_piece, unit_piece, rows_out.at[x])
    size = down_in.shape[0] // 2
    down_keep[...] = down_in[pl.ds(pl.multiple_of(x * size, 16), size), :].astype(kind)
    down_send[...] = down_in[pl.ds(pl.multiple_of((1 - x) * size, 16), size), :].astype(kind)
    swap(down_keep, down_send, down_out.at[:, half_lanes(x, down_keep.shape[1])])
    pl.when(x != y)(lambda: proj_move.wait())
    pl.when(x == y)(lambda: proj_stay.wait())
    launch(3, "proj")
    stays[2].wait()
    swaps[2].wait()
    for a in range(4, len(items)):
        launch(a, items[a])
    for a, item in enumerate(items):
        for k in range(1, depth):
            along[item, k].wait_recv()
            come = block(item, back[k], y, c)
            over[item, k] = remote(come, come, (a, depth + k), beside)
            over[item, k].start()
            pair[item, 0, k] = remote(come, come, (a, 2 * depth + k), twin)
            pair[item, 0, k].start()
    for a, item in enumerate(items):
        for k in range(depth):
            over[item, k].wait_recv()
            come = block(item, back[k], 1 - y, c)
            pair[item, 1, k] = remote(come, come, (a, 3 * depth + k), twin)
            pair[item, 1, k].start()
    for index in range(3, 5):
        stays[index].wait()
        swaps[index].wait()
    for item in items:
        for side in range(2):
            for k in range(depth):
                pair[item, side, k].wait()
        for k in range(depth):
            over[item, k].wait_send()
        for k in range(1, depth):
            along[item, k].wait_send()


def gather_first(groups, tokens, vectors, qkv, proj, up, down):
    depth = groups // 4
    kind, wide = jnp.bfloat16, jnp.float32
    local_rows, width = tokens.shape

    def halves(rows, columns):
        return [pltpu.VMEM((rows, columns), kind)] * 2

    shapes = [
        jax.ShapeDtypeStruct((depth, 2, 2, 2, 16, LANES), kind),
        jax.ShapeDtypeStruct((depth, 2, 2) + qkv.shape, kind),
        jax.ShapeDtypeStruct((depth, 2, proj.shape[0], 2 * proj.shape[1]), kind),
        jax.ShapeDtypeStruct(up.shape, kind),
        jax.ShapeDtypeStruct((down.shape[0] // 2, 2 * down.shape[1]), kind),
        jax.ShapeDtypeStruct((depth, 2, 2) + up.shape, kind),
        jax.ShapeDtypeStruct((2, local_rows, width), kind),
        jax.ShapeDtypeStruct((local_rows, width), wide),
        jax.ShapeDtypeStruct((local_rows, 1), wide),
    ]
    vmem = pl.BlockSpec(memory_space=pltpu.VMEM)
    hbm = pl.BlockSpec(memory_space=pl.ANY)
    return pl.pallas_call(
        lambda *refs: gather_kernel(groups, *refs),
        in_specs=[vmem] * 6,
        out_specs=[hbm] * 7 + [vmem] * 2,
        out_shape=shapes,
        scratch_shapes=[
            pltpu.VMEM((16, LANES), kind),
            *halves(qkv.shape[0], qkv.shape[1] // 2),
            pltpu.VMEM(proj.shape, kind),
            *halves(up.shape[0], up.shape[1] // 2),
            *halves(down.shape[0] // 2, down.shape[1]),
            pltpu.VMEM((local_rows, width), kind),
            pltpu.SemaphoreType.DMA((4 + UP_EARLY, 4 * depth)),
            pltpu.SemaphoreType.DMA((4 + UP_EARLY, 4 * depth)),
            pltpu.SemaphoreType.DMA((6,)),
            pltpu.SemaphoreType.DMA((6,)),
            pltpu.SemaphoreType.DMA((6,)),
        ],
        compiler_params=pltpu.CompilerParams(collective_id=0, has_side_effects=True),
        cost_estimate=pl.CostEstimate(
            flops=0, bytes_accessed=64 * qkv.size, transcendentals=0
        ),
        name="gather_first",
    )(tokens, vectors, qkv, proj, up, down)


def forward_pair(
    index, hidden_ref, qkv_ref, q_bias_ref, v_bias_ref, cos_ref, down_ref, up_ref, column_ref, row_ref,
    query_held, key_held, value_held, att_held, log_held, att_out,
):
    scale = 1.0 / math.sqrt(HD)
    length = hidden_ref.shape[0]
    width = qkv_ref.shape[1] // 3
    size = length // 4
    pairs = width // LANES

    def mixed(block):
        return jnp.dot(
            hidden_ref[...], qkv_ref[:, half_lanes(block, LANES)],
            preferred_element_type=jnp.float32,
        )

    lanes_of = half_lanes(index, LANES)
    cosine, down_sine, up_sine = cos_ref[...], down_ref[...], up_ref[...]
    query_held[index] = rolled(
        mixed(index) + q_bias_ref[:, lanes_of], cosine, down_sine, up_sine
    ).astype(jnp.bfloat16)
    key_held[index] = rolled(
        mixed(pairs + index), cosine, down_sine, up_sine
    ).astype(jnp.bfloat16)
    value_held[index] = (
        mixed(2 * pairs + index) + v_bias_ref[:, lanes_of]
    ).astype(jnp.bfloat16)
    for start in range(0, length, size):
        extent = start + size
        mask = block_mask(column_ref, row_ref, start, size, extent)
        keys, values = key_held[index, :extent, :], value_held[index, :extent, :]
        results = []
        for query in split_pair(query_held[index, start:extent, :].astype(jnp.float32)):
            scores = times_transposed(query.astype(jnp.bfloat16), keys) * scale
            exp_scores = jnp.where(mask, jnp.exp(scores), 0.0)
            totals = jnp.sum(exp_scores, axis=1, keepdims=True)
            numerator = jnp.dot(
                exp_scores.astype(jnp.bfloat16), values, preferred_element_type=jnp.float32
            )
            results.append((numerator / totals, jnp.log(totals)))
        lanes = lax.broadcasted_iota(jnp.int32, (size, 2 * HD), 1) < HD
        attended = jnp.where(lanes, results[0][0], results[1][0])
        att_held[index, start:extent, :] = attended
        att_out[start:extent, lanes_of] = attended.astype(jnp.bfloat16)
        log_held[index, start:extent, :] = jnp.where(lanes, results[0][1], results[1][1])


def backward_pair(
    index, cot_ref, proj_ref, cos_ref, down_ref, up_ref, column_ref, row_ref,
    query_held, key_held, value_held, att_held, log_held, grad_held,
    query_sum, key_sum, value_sum, mixed_out, q_bias_out, v_bias_out,
):
    scale = 1.0 / math.sqrt(HD)
    length = query_held.shape[1]
    size = length // 4
    pairs = query_held.shape[0]
    proj_rows = proj_ref[pl.ds(pl.multiple_of(index * LANES, LANES), LANES), :]
    local_rows = cot_ref.shape[1]
    for side in range(2):
        grad_held[side * local_rows : (side + 1) * local_rows, :] = times_transposed(
            cot_ref[side], proj_rows
        ).astype(jnp.bfloat16)
    key_sum[...] = jnp.zeros_like(key_sum)
    value_sum[...] = jnp.zeros_like(value_sum)
    for start in range(0, length, size):
        extent = start + size
        mask = block_mask(column_ref, row_ref, start, size, extent)
        keys, values = key_held[index, :extent, :], value_held[index, :extent, :]
        queries = split_pair(query_held[index, start:extent, :].astype(jnp.float32))
        grads = split_pair(grad_held[start:extent, :].astype(jnp.float32))
        attended = att_held[index, start:extent, :]
        pieces = []
        for head in range(2):
            query = queries[head].astype(jnp.bfloat16)
            grad = grads[head].astype(jnp.bfloat16)
            log_total = log_held[index, start:extent, head * HD : head * HD + 1]
            scores = times_transposed(query, keys) * scale
            probability = jnp.where(mask, jnp.exp(scores - log_total), 0.0)
            grad_prob = times_transposed(grad, values)
            delta = jnp.sum(grads[head] * attended, axis=1, keepdims=True)
            grad_score = (probability * (grad_prob - delta) * scale).astype(jnp.bfloat16)
            pieces.append(jnp.dot(grad_score, keys, preferred_element_type=jnp.float32))
            key_sum[:extent, :] += transposed_times(grad_score, query)
            value_sum[:extent, :] += transposed_times(probability.astype(jnp.bfloat16), grad)
        lanes = lax.broadcasted_iota(jnp.int32, (size, 2 * HD), 1) < HD
        query_sum[start:extent, :] = jnp.where(lanes, pieces[0], pieces[1])
    cosine, down_sine, up_sine = cos_ref[...], down_ref[...], up_ref[...]
    grad_query = rolled(query_sum[...], cosine, -down_sine, -up_sine)
    mixed_out[:, half_lanes(index, LANES)] = grad_query.astype(jnp.bfloat16)
    q_bias_out[:, half_lanes(index, LANES)] = jnp.sum(grad_query, axis=0, keepdims=True)
    mixed_out[:, half_lanes(pairs + index, LANES)] = rolled(
        key_sum[...], cosine, -down_sine, -up_sine
    ).astype(jnp.bfloat16)
    grad_value = value_sum[...]
    mixed_out[:, half_lanes(2 * pairs + index, LANES)] = grad_value.astype(jnp.bfloat16)
    v_bias_out[:, half_lanes(index, LANES)] = jnp.sum(grad_value, axis=0, keepdims=True)


def attention_kernel(
    groups,
    up_early, up_in, down_in, grad_in, proj_in, hidden_in, qkv_in, q_bias_in, v_bias_in,
    cos_in, low_in, high_in, column_in, row_in,
    up_out, down_out, cot_out, cot_sum_out, att_out, mixed_out, q_bias_out, v_bias_out,
    query_held, key_held, value_held, att_held, log_held, grad_held,
    query_sum, key_sum, value_sum, cot_in,
    send_sem, recv_sem, row_send, row_recv, local_sem,
):
    del up_early
    depth, z, y, c, x = place(groups)
    pairs = query_held.shape[0]
    firsts = (UP_EARLY, 0)
    cot_in[...] = grad_in[...].astype(jnp.bfloat16)
    across = device(z, y, c, 1 - x)
    beside = device(z, 1 - y, c, x)
    twin = device(z, y, 1 - c, x)
    far = [lax.rem(z + k, depth) for k in range(1, depth)]
    back = [lax.rem(z + depth - k, depth) for k in range(depth)]
    greet([across, beside, twin] + [device(zz, y, c, x) for zz in far])

    def remote(src, dst, index, peer, sems=(send_sem, recv_sem)):
        return pltpu.make_async_remote_copy(
            src_ref=src, dst_ref=dst, send_sem=sems[0].at[index], recv_sem=sems[1].at[index],
            device_id=peer, device_id_type=MESH,
        )

    arrays = ((up_in, up_out), (down_in, down_out))

    def rows_of(ref, i):
        size = ref.shape[-2] // pairs
        return pl.ds(pl.multiple_of(i * size, 16), size)

    def block(a, i, zz, yy, cc):
        out = arrays[a][1]
        return out.at[zz, yy, cc, rows_of(out, i)]

    def source(a, i):
        return arrays[a][0].at[rows_of(arrays[a][0], i)]

    def along(a, i, k):
        return remote(
            source(a, i), block(a, i, z, y, c), (a, i, k), device(far[k - 1], y, c, x)
        )

    def over(a, i, k):
        src = source(a, i) if k == 0 else block(a, i, back[k], y, c)
        return remote(src, block(a, i, back[k], y, c), (a, i, depth + k), beside)

    def pair(a, i, side, k):
        come = block(a, i, back[k], 1 - y if side else y, c)
        src = source(a, i) if (side, k) == (0, 0) else come
        return remote(src, come, (a, i, (2 + side) * depth + k), twin)

    cot_swap = remote(cot_in, cot_out.at[x], 0, across, (row_send, row_recv))
    cot_swap.start()
    stays = [
        pltpu.make_async_copy(arrays[a][0], arrays[a][1].at[z, y, c], local_sem.at[a])
        for a in range(2)
    ] + [pltpu.make_async_copy(cot_in, cot_out.at[x], local_sem.at[2])]
    for stay in stays:
        stay.start()

    for i in range(pairs):
        for a in range(2):
            if i < firsts[a]:
                continue
            for k in range(1, depth):
                along(a, i, k).start()
            over(a, i, 0).start()
            pair(a, i, 0, 0).start()

    def relay_along(i):
        for a in range(2):
            if i < firsts[a]:
                continue
            for k in range(1, depth):
                along(a, i, k).wait_recv()
                over(a, i, k).start()
                pair(a, i, 0, k).start()

    def relay_over(i):
        for a in range(2):
            def relay(a=a):
                for k in range(depth):
                    over(a, i, k).wait_recv()
                    pair(a, i, 1, k).start()

            pl.when(i >= firsts[a])(relay)

    @pl.loop(0, pairs)
    def _(i):
        forward_pair(
            i, hidden_in, qkv_in, q_bias_in, v_bias_in, cos_in, low_in, high_in, column_in, row_in,
            query_held, key_held, value_held, att_held, log_held, att_out,
        )

    relay_along(0)
    cot_sum_out[...] = jnp.zeros_like(cot_sum_out)

    @pl.loop(0, grad_in.shape[0] // 64)
    def _(step):
        part = pl.ds(pl.multiple_of(step * 64, 64), 64)
        cot_sum_out[...] += jnp.sum(grad_in[part, :], axis=0, keepdims=True)

    relay_along(1)
    stays[2].wait()
    cot_swap.wait()

    @pl.loop(0, pairs)
    def _(i):
        backward_pair(
            i, cot_out, proj_in, cos_in, low_in, high_in, column_in, row_in,
            query_held, key_held, value_held, att_held, log_held, grad_held,
            query_sum, key_sum, value_sum, mixed_out, q_bias_out, v_bias_out,
        )
        pl.when(i == 0)(lambda: relay_along(2))
        pl.when(i == 2)(lambda: relay_along(3))
        relay_over(i)

    for stay in stays[:2]:
        stay.wait()

    for i in range(pairs):
        for a in range(2):
            if i < firsts[a]:
                continue
            for k in range(depth):
                for side in range(2):
                    pair(a, i, side, k).wait()
                over(a, i, k).wait_send()
            for k in range(1, depth):
                along(a, i, k).wait_send()


def attention_all(
    groups, up_early, up, down, out_grad, proj_work, hidden, qkv_work, q_bias, v_bias, tables,
    segment_row,
):
    depth = groups // 4
    length = hidden.shape[0]
    width = qkv_work.shape[1] // 3
    pairs = width // LANES
    kind, wide = jnp.bfloat16, jnp.float32
    shapes = [
        jax.ShapeDtypeStruct((depth, 2, 2) + up.shape, kind),
        jax.ShapeDtypeStruct((depth, 2, 2) + down.shape, kind),
        jax.ShapeDtypeStruct((2,) + out_grad.shape, kind),
        jax.ShapeDtypeStruct((1, out_grad.shape[1]), wide),
        jax.ShapeDtypeStruct((length, width), kind),
        jax.ShapeDtypeStruct((length, 3 * width), kind),
        jax.ShapeDtypeStruct((1, width), wide),
        jax.ShapeDtypeStruct((1, width), wide),
    ]
    held = (pairs, length, LANES)
    vmem = pl.BlockSpec(memory_space=pltpu.VMEM)
    hbm = pl.BlockSpec(memory_space=pl.ANY)
    flops = 14 * length * length * width
    return pl.pallas_call(
        lambda *refs: attention_kernel(groups, *refs),
        in_specs=[hbm] + [vmem] * 13,
        out_specs=[hbm] * 2 + [vmem] * 6,
        out_shape=shapes,
        input_output_aliases={0: 0},
        scratch_shapes=[pltpu.VMEM(held, kind)] * 3
        + [pltpu.VMEM(held, wide)] * 2
        + [pltpu.VMEM((length, LANES), kind)]
        + [pltpu.VMEM((length, LANES), wide)] * 3
        + [pltpu.VMEM(out_grad.shape, kind)]
        + [
            pltpu.SemaphoreType.DMA((2, pairs, 4 * depth)),
            pltpu.SemaphoreType.DMA((2, pairs, 4 * depth)),
            pltpu.SemaphoreType.DMA((1,)),
            pltpu.SemaphoreType.DMA((1,)),
            pltpu.SemaphoreType.DMA((3,)),
        ],
        compiler_params=pltpu.CompilerParams(
            collective_id=2, has_side_effects=True, vmem_limit_bytes=56 * 1024 * 1024
        ),
        cost_estimate=pl.CostEstimate(
            flops=flops, bytes_accessed=48 * length * width, transcendentals=length * length * 8
        ),
        name="attention_all",
    )(up_early, up, down, out_grad, proj_work, hidden, qkv_work, q_bias[None], v_bias[None], *tables,
      segment_row[:, None], segment_row[None, :])


def square_sum(values):
    return jnp.sum(jnp.sum(values * values, axis=1, keepdims=True), axis=0, keepdims=True)


REDUCE_ITEMS = (
    ("proj", 0), ("up", 0), ("up", 1), ("down", 0), ("down", 1), ("qkv", 0), ("qkv", 1)
)


def reduce_kernel(groups, *refs):
    (
        down_in, up_in, proj_in, qkv_in, vec_in, rows_in, rows_sent, unit_in, inverse_in, gain_in,
        down_out, up_out, proj_out, qkv_out, vec_out, square_out, rows_out,
    ) = refs[:17]
    count = len(REDUCE_ITEMS)
    sets = [refs[17 + 9 * i : 26 + 9 * i] for i in range(count)]
    own, one, mid, two, cross, last, three, end, swap = zip(*sets)
    (
        vec_held, vec_come, tile_held, tile_come, rows_come, vec_sum,
        send_sem, recv_sem, vec_send, vec_recv, row_send, row_recv, local_sem,
    ) = refs[17 + 9 * count :]
    depth, z, y, c, x = place(groups)
    parts = dict(down=down_in, up=up_in, proj=proj_in, qkv=qkv_in)
    across = device(z, y, c, 1 - x)
    beside = device(z, 1 - y, c, x)
    twin = device(z, y, 1 - c, x)
    corner = device(z, x, c, y)
    far = [lax.rem(z + k, depth) for k in range(1, depth)]
    alongs = [device(zz, y, c, x) for zz in far]
    near = [
        device(z, yy, cc, xx)
        for xx in (x, 1 - x) for yy in (y, 1 - y) for cc in (c, 1 - c)
    ][1:]
    greet(near + alongs)

    def remote(src, dst, index, peer, sems=(send_sem, recv_sem)):
        return pltpu.make_async_remote_copy(
            src_ref=src, dst_ref=dst, send_sem=sems[0].at[index], recv_sem=sems[1].at[index],
            device_id=peer, device_id_type=MESH,
        )

    def wide(values):
        return values.astype(jnp.float32)

    vec_sems = (vec_send, vec_recv)
    vec_copies = []
    first, stays, second, third, fourth = {}, {}, {}, {}, {}
    for i, (name, piece) in enumerate(REDUCE_ITEMS):
        part = parts[name]
        first[i], stays[i] = [], []
        if name == "proj":
            moves = [(part.at[:, 1 - c], one[i], part.at[:, c], own[i])]
        else:
            size = own[i].shape[-1] // 2
            moves = []
            for side in range(2):
                start = side * part.shape[-1] // 2 + piece * size
                from_lanes, to_lanes = pl.ds(start, size), pl.ds(side * size, size)
                moves.append((
                    part.at[:, :, 1 - c, :, from_lanes], one[i].at[:, :, :, to_lanes],
                    part.at[:, :, c, :, from_lanes], own[i].at[:, :, :, to_lanes],
                ))
        for side, (theirs, there, mine, here) in enumerate(moves):
            first[i].append(remote(theirs, there, (i, side), twin))
            first[i][-1].start()
            stays[i].append(pltpu.make_async_copy(mine, here, local_sem.at[i, side]))
            stays[i][-1].start()
    rows_swap = remote(rows_sent, rows_come, 0, across, (row_send, row_recv))
    rows_swap.start()

    def rows_back():
        rows_swap.wait()
        vec_sum[...] = vec_in[...]
        gain = gain_in[...]

        @pl.loop(0, rows_in.shape[0] // 64)
        def _(step):
            part = pl.ds(pl.multiple_of(step * 64, 64), 64)
            upstream = rows_in[part, :] + wide(rows_come[part, :])
            unit = unit_in[part, :]
            scaled = upstream * gain
            mean_plain = jnp.mean(scaled, axis=-1, keepdims=True)
            mean_unit = jnp.mean(scaled * unit, axis=-1, keepdims=True)
            rows_out[part, :] = inverse_in[part, :] * (scaled - mean_plain - unit * mean_unit)
            vec_sum[0:1, :] += jnp.sum(upstream * unit, axis=0, keepdims=True)
            vec_sum[1:2, :] += jnp.sum(upstream, axis=0, keepdims=True)

        vec_copies.append(remote(vec_sum, vec_come.at[0], 0, twin, vec_sems))
        vec_copies[0].start()

    def step_one(i):
        name = REDUCE_ITEMS[i][0]
        for copy in first[i] + stays[i]:
            copy.wait()

        def body(zz, carry):
            if name == "proj":
                half = own[i].shape[2] // 2
                ours, theirs = half_lanes(y, half), half_lanes(1 - y, half)
                cross[i][zz] = (
                    wide(own[i][zz, :, theirs]) + wide(one[i][zz, :, theirs])
                ).astype(jnp.bfloat16)
                mid[i][zz] = wide(own[i][zz, :, ours]) + wide(one[i][zz, :, ours])
            else:
                cross[i][zz] = (
                    wide(own[i][zz, 1 - y]) + wide(one[i][zz, 1 - y])
                ).astype(jnp.bfloat16)
                mid[i][zz] = wide(own[i][zz, y]) + wide(one[i][zz, y])
            return carry

        lax.fori_loop(0, depth, body, 0)
        second[i] = remote(cross[i], two[i], (i, 2), beside)
        second[i].start()

    def step_two(i):
        second[i].wait()
        for k in range(1, depth):
            zz = far[k - 1]
            last[i][k - 1] = (mid[i][zz] + wide(two[i][zz])).astype(jnp.bfloat16)
            third[i, k] = remote(
                last[i].at[k - 1], three[i].at[k - 1], (i, 2 + k), alongs[k - 1]
            )
            third[i, k].start()

    def step_three(i):
        for k in range(1, depth):
            third[i, k].wait()
        total = mid[i][z] + wide(two[i][z])
        for k in range(1, depth):
            total = total + wide(three[i][k - 1])
        mid[i][0] = total
        if REDUCE_ITEMS[i][0] == "proj":
            end[i][...] = total.astype(jnp.bfloat16)
            fourth[i] = remote(end[i], swap[i], (i, depth + 2), corner)
            pl.when(x != y)(lambda: fourth[i].start())
        else:
            half = total.shape[1] // 2
            end[i][...] = mid[i][0, :, half_lanes(1 - x, half)].astype(jnp.bfloat16)
            fourth[i] = remote(end[i], swap[i], (i, depth + 2), across)
            fourth[i].start()

    def step_four(i):
        name, piece = REDUCE_ITEMS[i]
        if name == "proj":
            def swapped():
                fourth[i].wait()
                proj_out[...] = wide(swap[i][...])

            def kept():
                proj_out[...] = mid[i][0]

            pl.when(x != y)(swapped)
            pl.when(x == y)(kept)
            return square_sum(proj_out[...])
        fourth[i].wait()
        half = swap[i].shape[1]
        mine = mid[i][0, :, half_lanes(x, half)]
        theirs = wide(swap[i][...])
        if name == "down":
            size = mine.shape[0]
            lanes = slice(piece * half, (piece + 1) * half)
            down_out[pl.ds(pl.multiple_of(x * size, 8), size), lanes] = mine
            down_out[pl.ds(pl.multiple_of((1 - x) * size, 8), size), lanes] = theirs
        else:
            out = dict(up=up_out, qkv=qkv_out)[name]
            blocks = half // LANES
            for b in range(blocks):
                lanes = slice(b * LANES, (b + 1) * LANES)
                to = 2 * (piece * blocks + b)
                out[:, half_lanes(to + x, LANES)] = mine[:, lanes]
                out[:, half_lanes(to + 1 - x, LANES)] = theirs[:, lanes]
        return square_sum(mine) + square_sum(theirs)

    def vec_step(index, peers):
        for copy in vec_copies:
            copy.wait()
        vec_copies.clear()
        held = vec_sum[...] if index == 0 else vec_held[index - 1]
        vec_held[index] = held + vec_come[index]
        for k, peer in enumerate(peers):
            copy = remote(
                vec_held.at[index], vec_come.at[index + 1 + k], index + 1 + k, peer, vec_sems
            )
            copy.start()
            vec_copies.append(copy)

    step_one(0)
    step_one(1)
    squares = jnp.zeros((1, 1), jnp.float32)
    for t in range(count + 2):
        if t + 2 < count:
            step_one(t + 2)
        if t < count:
            step_two(t)
        if t == 2:
            rows_back()
        if t == 3:
            vec_step(0, [across])
        if t == 4:
            vec_step(1, [beside])
        if t == 5:
            vec_step(2, alongs)
        if 0 <= t - 1 < count:
            step_three(t - 1)
        if t == count:
            for copy in vec_copies:
                copy.wait()
            vec_total = vec_held[2]
            for k in range(depth - 1):
                vec_total = vec_total + vec_come[3 + k]
            vec_out[...] = vec_total
            vec_square = square_sum(vec_total)
        if 0 <= t - 2:
            squares = squares + step_four(t - 2)

    base = 3 + depth
    tile_held[0] = jnp.broadcast_to(squares, tile_held.shape[1:])
    copies = [
        remote(tile_held.at[0], tile_come.at[k], base + k, peer, vec_sems)
        for k, peer in enumerate(alongs)
    ]
    for copy in copies:
        copy.start()
    for copy in copies:
        copy.wait()
    tile = tile_held[0]
    for k in range(depth - 1):
        tile = tile + tile_come[k]
    tile_held[1] = tile
    copies = [
        remote(tile_held.at[1], tile_come.at[depth - 1 + k], base + depth - 1 + k, peer, vec_sems)
        for k, peer in enumerate(near)
    ]
    for copy in copies:
        copy.start()
    for copy in copies:
        copy.wait()
    for k in range(len(near)):
        tile = tile + tile_come[depth - 1 + k]
    square_out[...] = tile + vec_square


def reduce_all(groups, down_part, up_part, proj_part, qkv_part, vec_part, row_args):
    depth = groups // 4
    wide, kind = jnp.float32, jnp.bfloat16

    def grid_of(part):
        return part.reshape(depth, 2, 2, part.shape[0] // groups, part.shape[1])

    down, up, qkv = grid_of(down_part), grid_of(up_part), grid_of(qkv_part)
    proj = proj_part.reshape(depth, 2, proj_part.shape[0] // depth // 2, proj_part.shape[1])
    parts = dict(down=down, up=up, proj=proj, qkv=qkv)
    scratch = []
    for name, _ in REDUCE_ITEMS:
        rows, columns = parts[name].shape[-2:]
        block = (rows, columns // 2)
        whole = name == "proj"
        held = (depth, rows, columns) if whole else (depth, 2) + block
        final = block if whole else (rows, columns // 4)
        scratch += [
            pltpu.VMEM(held, kind), pltpu.VMEM(held, kind),
            pltpu.VMEM((depth,) + block, wide), pltpu.VMEM((depth,) + block, kind),
            pltpu.VMEM((depth,) + block, kind), pltpu.VMEM((depth - 1,) + block, kind),
            pltpu.VMEM((depth - 1,) + block, kind), pltpu.VMEM(final, kind),
            pltpu.VMEM(final, kind),
        ]
    near, count = 7, len(REDUCE_ITEMS)
    scratch += [
        pltpu.VMEM((3,) + vec_part.shape, wide),
        pltpu.VMEM((2 + depth,) + vec_part.shape, wide),
        pltpu.VMEM((2, 8, LANES), wide),
        pltpu.VMEM((depth - 1 + near, 8, LANES), wide),
        pltpu.VMEM(row_args[1].shape, kind),
        pltpu.VMEM(vec_part.shape, wide),
        pltpu.SemaphoreType.DMA((count, depth + 3)),
        pltpu.SemaphoreType.DMA((count, depth + 3)),
        pltpu.SemaphoreType.DMA((2 + 2 * depth + near,)),
        pltpu.SemaphoreType.DMA((2 + 2 * depth + near,)),
        pltpu.SemaphoreType.DMA((1,)),
        pltpu.SemaphoreType.DMA((1,)),
        pltpu.SemaphoreType.DMA((count, 2)),
    ]
    shapes = [
        jax.ShapeDtypeStruct((2 * down.shape[-2], down.shape[-1] // 2), wide),
        jax.ShapeDtypeStruct(up.shape[-2:], wide),
        jax.ShapeDtypeStruct((proj.shape[-2], proj.shape[-1] // 2), wide),
        jax.ShapeDtypeStruct(qkv.shape[-2:], wide),
        jax.ShapeDtypeStruct(vec_part.shape, wide),
        jax.ShapeDtypeStruct((8, LANES), wide),
        jax.ShapeDtypeStruct(row_args[0].shape, wide),
    ]
    vmem = pl.BlockSpec(memory_space=pltpu.VMEM)
    hbm = pl.BlockSpec(memory_space=pl.ANY)
    return pl.pallas_call(
        lambda *refs: reduce_kernel(groups, *refs),
        in_specs=[hbm] * 4 + [vmem] * 6,
        out_specs=[vmem] * 7,
        out_shape=shapes,
        scratch_shapes=scratch,
        compiler_params=pltpu.CompilerParams(
            collective_id=1, has_side_effects=True, vmem_limit_bytes=56 * 1024 * 1024
        ),
        cost_estimate=pl.CostEstimate(
            flops=0, bytes_accessed=50 * down_part.size, transcendentals=0
        ),
        name="reduce_all",
    )(down, up, proj, qkv, vec_part, *row_args)


def adam_kernel(square_ref, *refs):
    count = len(refs) // 6
    norm_limit = math.sqrt(NPARAM)
    clip = norm_limit / jnp.maximum(jnp.sqrt(square_ref[0:1, 0:1]), norm_limit)
    fix_first = 1.0 - math.pow(beta_one, STEP)
    fix_second = 1.0 - math.pow(beta_two, STEP)
    ins, outs = refs[: 3 * count], refs[3 * count :]
    for index in range(count):
        weight_ref, moment_ref, grad_ref = ins[3 * index : 3 * index + 3]
        grad_out, weight_out, moment_out = outs[3 * index : 3 * index + 3]
        grad, weight = grad_ref[...], weight_ref[...]
        clipped = grad * clip
        first_new = beta_one * moment_ref[0] + (1.0 - beta_one) * clipped
        second_new = beta_two * moment_ref[1] + (1.0 - beta_two) * clipped * clipped
        direction = first_new / fix_first / (jnp.sqrt(second_new / fix_second) + adam_eps)
        grad_out[...] = grad
        weight_out[...] = weight - learn_rate * (direction + decay_rate * weight)
        moment_out[0] = first_new
        moment_out[1] = second_new


def adam_all(square, weights, moments, grads):
    steps = 4
    in_specs = [pl.BlockSpec(square.shape, lambda i: (0, 0))]
    out_specs, shapes, ins = [], [], [square]
    for weight, moment, grad in zip(weights, moments, grads):
        rows, columns = weight.shape
        if rows % (8 * steps) == 0:
            flat = pl.BlockSpec((rows // steps, columns), lambda i: (i, 0))
            both = pl.BlockSpec((2, rows // steps, columns), lambda i: (0, i, 0))
        else:
            flat = pl.BlockSpec((rows, columns), lambda i: (0, 0))
            both = pl.BlockSpec((2, rows, columns), lambda i: (0, 0, 0))
        in_specs += [flat, both, flat]
        out_specs += [flat, flat, both]
        shapes += [
            jax.ShapeDtypeStruct(grad.shape, grad.dtype),
            jax.ShapeDtypeStruct(weight.shape, weight.dtype),
            jax.ShapeDtypeStruct(moment.shape, moment.dtype),
        ]
        ins += [weight, moment, grad]
    size = sum(weight.size for weight in weights)
    results = pl.pallas_call(
        adam_kernel,
        grid=(steps,),
        in_specs=in_specs,
        out_specs=out_specs,
        out_shape=shapes,
        cost_estimate=pl.CostEstimate(
            flops=20 * size, bytes_accessed=32 * size, transcendentals=2 * size
        ),
        name="adam_all",
    )(*ins)
    return results[0::3], results[1::3], results[2::3]


def swap_shard(piece):
    return lax.ppermute(piece, "shard", [(0, 1), (1, 0)])


def pick(array, index, axis):
    return lax.dynamic_index_in_dim(array, index, axis=axis, keepdims=False)


def sum_halves(partial, member, local_rows):
    halves = partial.reshape(2, local_rows, partial.shape[-1])
    received = swap_shard(pick(halves, 1 - member, 0).astype(jnp.bfloat16))
    return pick(halves, member, 0) + received.astype(jnp.float32)


def spread(values, width, member):
    blocks = values.reshape(-1, 1, width)
    chosen = jnp.arange(2, dtype=jnp.int32)[None, :, None] == member
    return jnp.where(chosen, blocks, 0.0).reshape(-1)


def rolled(rows, cosine, down_sine, up_sine):
    width = rows.shape[1]
    lower = pltpu.roll(rows, width - ROT // 2, 1)
    upper = pltpu.roll(rows, ROT // 2, 1)
    return rows * cosine + lower * down_sine + upper * up_sine


def split_pair(rows):
    lanes = lax.broadcasted_iota(jnp.int32, rows.shape, 1)
    return (
        jnp.where(lanes < HD, rows, jnp.zeros_like(rows)),
        jnp.where(lanes < HD, jnp.zeros_like(rows), rows),
    )


def block_mask(seg_column, seg_row, start, size, extent):
    rows = start + lax.broadcasted_iota(jnp.int32, (size, extent), 0)
    keys = lax.broadcasted_iota(jnp.int32, (size, extent), 1)
    same = seg_column[start : start + size, :] == seg_row[:, :extent]
    return same & (keys <= rows)


def lane_tables(positions):
    dims = jnp.arange(2 * HD, dtype=jnp.int32) % HD
    half_dims = ROT // 2
    exponent = (dims % half_dims).astype(jnp.float32) * (2.0 / ROT)
    inverse_freq = jnp.exp(-math.log(rope_base) * exponent)
    angles = positions.astype(jnp.float32)[:, None] * inverse_freq[None, :]
    sine = jnp.sin(angles)
    return (
        jnp.where(dims[None] < ROT, jnp.cos(angles), 1.0),
        jnp.where(dims[None] < half_dims, -sine, 0.0),
        jnp.where((dims[None] >= half_dims) & (dims[None] < ROT), sine, 0.0),
    )


def shards(
    tokens,
    out_grad,
    segment_ids,
    qkv_weight,
    proj_weight,
    up_weight,
    down_weight,
    vectors,
    qkv_moments,
    proj_moments,
    up_moments,
    down_moments,
    vector_moments,
):
    groups = lax.axis_size("dp")
    members = lax.axis_size("shard")
    head_count = D // HD
    if members != 2 or groups != head_count:
        return plain_shards(
            tokens,
            out_grad,
            segment_ids,
            qkv_weight,
            proj_weight,
            up_weight,
            down_weight,
            vectors,
            qkv_moments,
            proj_moments,
            up_moments,
            down_moments,
            vector_moments,
        )
    member = lax.axis_index("shard")
    group = lax.axis_index("dp")
    half = D // 2
    local_rows = tokens.shape[0]
    vec_width = vectors.shape[1]
    pairs = half // LANES

    vec_all, qkv_all, proj_all, up_piece, down_piece, up_early, unit_all, unit, inverse = (
        gather_first(groups, tokens, vectors, qkv_weight, proj_weight, up_weight, down_weight)
    )
    vec_work = (
        vec_all.reshape(2 * groups, 16, LANES)[:, :VROWS, :vec_width]
        .transpose(1, 0, 2)
        .reshape(VROWS, D)
        .astype(jnp.float32)
    )
    qkv_work = qkv_all.reshape(D, 3 * half)
    proj_work = proj_all.reshape(half, D)
    unit_rows = unit_all.reshape(2 * local_rows, D).astype(jnp.float32)
    hidden_one = (unit_rows * vec_work[0] + vec_work[1]).astype(jnp.bfloat16)
    hidden_two = (unit_rows * vec_work[2] + vec_work[3]).astype(jnp.bfloat16)

    segment_row = segment_ids[0]
    positions = doc_positions(segment_row)
    tables = lane_tables(positions)

    q_bias = pick(vec_work[4].reshape(pairs, 2, LANES), member, 1).reshape(-1)
    v_bias = pick(vec_work[5].reshape(pairs, 2, LANES), member, 1).reshape(-1)
    up_bias = pick(vec_work[8:].reshape(groups, 2, LANES), member, 1).reshape(-1)

    (
        up_all, down_all, cot_all, cot_sum, attended_bf, grad_mixed_bf, q_bias_part, v_bias_part
    ) = attention_all(
        groups, up_early, up_piece, down_piece, out_grad, proj_work, hidden_one, qkv_work,
        q_bias, v_bias, tables, segment_row,
    )
    cot_sum = cot_sum[0]
    up_work = up_all.reshape(D, FF // 2)
    down_work = down_all.reshape(FF // 2, D)
    cot_bf = cot_all.reshape(2 * local_rows, D)
    proj_part = transposed_times(attended_bf, cot_bf).astype(jnp.bfloat16)
    q_bias_part, v_bias_part = q_bias_part[0], v_bias_part[0]
    qkv_part = transposed_times(hidden_one, grad_mixed_bf).astype(jnp.bfloat16)
    rows_partial = times_transposed(grad_mixed_bf, qkv_work)

    pre_act = jnp.dot(hidden_two, up_work, preferred_element_type=jnp.float32) + up_bias
    act_values, act_slope = gelu_pair(pre_act)
    act_bf = act_values.astype(jnp.bfloat16)
    grad_pre = times_transposed(cot_bf, down_work) * act_slope
    grad_pre_bf = grad_pre.astype(jnp.bfloat16)
    down_part = transposed_times(act_bf, cot_bf).astype(jnp.bfloat16)
    up_part = transposed_times(hidden_two, grad_pre_bf).astype(jnp.bfloat16)

    out_partial = jnp.dot(
        attended_bf, proj_work, preferred_element_type=jnp.float32
    ) + jnp.dot(act_bf, down_work, preferred_element_type=jnp.float32)
    block_out = (
        tokens + sum_halves(out_partial, member, local_rows) + vec_work[6] + vec_work[7]
    )
    rows_two, ln2_gain_part, ln2_bias_part = norm_back(
        sum_halves(times_transposed(grad_pre_bf, up_work), member, local_rows),
        unit,
        inverse,
        vec_work[2],
    )
    zero_row = jnp.zeros_like(cot_sum)
    base_grad = out_grad + rows_two
    vec_part = jnp.concatenate(
        [
            jnp.stack(
                [
                    zero_row,
                    zero_row,
                    ln2_gain_part,
                    ln2_bias_part,
                    spread(q_bias_part, LANES, member),
                    spread(v_bias_part, LANES, member),
                    cot_sum,
                    cot_sum,
                ]
            ),
            spread(jnp.sum(grad_pre, axis=0), LANES, member).reshape(FF // D, D),
            jnp.zeros((16 - VROWS, D), jnp.float32),
        ],
        axis=0,
    )
    halves = rows_partial.reshape(2, local_rows, D)
    down_grad, up_grad, proj_grad, qkv_grad, vec_sum, square, rows_one = reduce_all(
        groups, down_part, up_part, proj_part, qkv_part, vec_part,
        (
            pick(halves, member, 0), pick(halves, 1 - member, 0).astype(jnp.bfloat16),
            unit, inverse, vec_work[0:1],
        ),
    )
    tokens_grad = base_grad + rows_one
    vectors_grad = lax.dynamic_slice_in_dim(
        vec_sum[:VROWS], (group * 2 + member) * vec_width, vec_width, axis=1
    )
    grads, weights_new, moments_new = adam_all(
        square,
        (qkv_weight, proj_weight, up_weight, down_weight, vectors),
        (qkv_moments, proj_moments, up_moments, down_moments, vector_moments),
        (qkv_grad, proj_grad, up_grad, down_grad, vectors_grad),
    )
    return (block_out, tokens_grad, *grads, *weights_new, *moments_new)


def solution(mesh):
    placed = (
        P(("dp", "shard"), None),
        P(("dp", "shard"), None),
        P("dp", None),
        P("dp", "shard"),
        P("dp", "shard"),
        P("dp", "shard"),
        P("dp", "shard"),
        P(None, ("dp", "shard")),
        P(None, "dp", "shard"),
        P(None, "dp", "shard"),
        P(None, "dp", "shard"),
        P(None, "dp", "shard"),
        P(None, None, ("dp", "shard")),
    )
    return jax.shard_map(
        shards,
        mesh=mesh,
        in_specs=placed,
        out_specs=(
            P(("dp", "shard"), None),
            P(("dp", "shard"), None),
            P("dp", "shard"),
            P("dp", "shard"),
            P("dp", "shard"),
            P("dp", "shard"),
            P(None, ("dp", "shard")),
            P("dp", "shard"),
            P("dp", "shard"),
            P("dp", "shard"),
            P("dp", "shard"),
            P(None, ("dp", "shard")),
            P(None, "dp", "shard"),
            P(None, "dp", "shard"),
            P(None, "dp", "shard"),
            P(None, "dp", "shard"),
            P(None, None, ("dp", "shard")),
        ),
        check_vma=False,
    )
```
